256 devices in a mesh: grp: 16 (over x, y), cls: 16 (over z, core).
Axes of the slice: x: 4, y: 4, z: 8, core: 2. Of those that a mesh axis runs over, the one named last changes fastest.
Arguments:
- images: bfloat16 [8192, 512], P('grp'), may hold values from -240 to 240
- labels: int32 [8192], P('grp'), may hold values from 0 to 32767
- taxon_emb: bfloat16 [32768, 512], P('cls'), may hold values from -3 to 3
- node_emb: bfloat16 [8192, 512], P('cls'), may hold values from -3 to 3
- proj: bfloat16 [512, 512], replicated, may hold values from -0.25 to 0.25
- lineage: int32 [32768, 7], P('cls'), may hold values from -1 to 8191, as said below
Outputs:
- loss: float32 [], replicated
- grad_images: bfloat16 [8192, 512], P('grp')
- grad_taxon: bfloat16 [32768, 512], P('cls')
- grad_node: float32 [8192, 512], P('cls')
- grad_proj: float32 [512, 512], replicated
The draws below stay inside these ranges and needn't reach their ends.
Inputs may be any that keep to these rules, and one draw needn't show every extreme that they name: `lineage`: nodes are numbered in depth-first order; index c of cls holds nodes c * 512 to (c + 1) * 512 - 1 and taxa c * 2048 to (c + 1) * 2048 - 1, taxa in the order of their genera. Row t lists, for each rank l, the node of rank l on the path from a root of the tree down to the taxon's genus, or -1 where that path has no node of rank l. Column 0 is never -1; column 6 is the genus, held by the same index of cls as the taxon; the last node held by each index is the genus of the last taxon it holds.
All inputs are finite; a program needn't handle non-finite values.
Results may differ from the reference program's by a relative error of at most 0.015.
Values may be sent and summed in bfloat16 or wider, within the bound.
A program may use at most 64 MiB of HBM per device.

```python
import math
import jax
import jax.numpy as jnp
import numpy as np
from jax import lax

E = 512
LEVELS = 7
TAXA_DEV = 2048
B_DEV = 512
NODE_DEV = 512
TAXA = 32768
NODES = 8192
BATCH = 8192
N_GRP = 16


def draw_images(key, part):
    values = jax.random.normal(jax.random.fold_in(key, 11), (BATCH, E), jnp.float32)
    values = jnp.clip(values, -6.0, 6.0)
    return values.astype(jnp.bfloat16)


def draw_lineage(key, part):
    deepest = LEVELS - 1
    position = jnp.arange(NODES, dtype=jnp.int32)
    jump_draw = jax.random.randint(jax.random.fold_in(key, 1), (NODES,), 0, 1024)
    down_draw = jax.random.randint(jax.random.fold_in(key, 2), (NODES,), 0, 4)
    shard_end = position % NODE_DEV == NODE_DEV - 1

    def advance(level_now, inputs):
        jump_value, down_value, at_end = inputs
        upper = jnp.where(jump_value < 440, deepest, jnp.where(jump_value < 640, deepest - 1, jnp.where(jump_value < 800, deepest - 2, jnp.where(jump_value < 900, deepest - 3, jnp.where(jump_value < 970, deepest - 4, jnp.where(jump_value < 1023, deepest - 5, 0))))))
        lower = jnp.minimum(level_now + jnp.where(down_value == 0, 2, 1), deepest)
        next_level = jnp.where(level_now == deepest, upper, lower)
        next_level = jnp.where(at_end, deepest, next_level).astype(jnp.int32)
        return (next_level, next_level)
    final_level, rest = lax.scan(advance, jnp.int32(0), (jump_draw[1:], down_draw[1:], shard_end[1:]))
    ranks = jnp.concatenate([jnp.zeros((1,), jnp.int32), rest])
    columns = []
    for column in range(LEVELS):
        candidate = jnp.where(ranks <= column, position, -1)
        latest = lax.cummax(candidate, axis=0)
        clipped = jnp.clip(latest, 0, NODES - 1)
        columns.append(jnp.where((latest >= 0) & (ranks[clipped] == column), latest, -1))
    ancestors = jnp.stack(columns, axis=1)
    shards = NODES // NODE_DEV
    genus_flag = (ranks == deepest).astype(jnp.int32).reshape(shards, NODE_DEV)
    running = jnp.cumsum(genus_flag, axis=1)
    genus_count = running[:, -1]
    taxon_iota = jnp.arange(TAXA_DEV, dtype=jnp.int32)
    wanted = taxon_iota[None, :] * genus_count[:, None] // TAXA_DEV + 1
    offset = jax.vmap(lambda cum_row, target_rank: jnp.searchsorted(cum_row, target_rank, side='left'))(running, wanted)
    genus = (offset.astype(jnp.int32) + jnp.arange(shards, dtype=jnp.int32)[:, None] * NODE_DEV).reshape(TAXA)
    return ancestors[genus].astype(jnp.int32)


def plant(result, own_key, low, top_value):
    extent = result.shape
    spot = [jax.random.randint(jax.random.fold_in(own_key, axis), (), 0, extent[axis]) for axis in range(len(extent))]
    result = result.at[tuple(spot)].set(low)
    longest = extent.index(max(extent))
    spot[longest] = (spot[longest] + 1) % extent[longest]
    return result.at[tuple(spot)].set(top_value)


def level_of(own_key, shape, pieces, smallest, largest):
    def one(dim, parts):
        steps = jax.random.uniform(jax.random.fold_in(jax.random.fold_in(own_key, 6), dim), (parts,), jnp.float32, smallest / len(pieces), largest / len(pieces))
        return jnp.repeat(jnp.exp(steps), shape[dim] // parts).reshape((-1,) + (1,) * (len(shape) - dim - 1))

    factor_of = one(*pieces[0])
    for cut in pieces[1:]:
        factor_of = factor_of * one(*cut)
    return factor_of


def rank_bounds(count, lean):
    loads = [(1 << 20) // math.isqrt(grade ** lean) + 1 for grade in range(1, count + 1)]
    deviation = 1 + sum(loads) // (1 << 30)
    return np.cumsum(np.array([max(1, weight // deviation) for weight in loads]))


def ranked_ids(key, shape, amount, lean):
    table = rank_bounds(amount, lean)
    ticket = jax.random.randint(jax.random.fold_in(key, 1), shape, 0, int(table[amount - 1]))
    rank = jnp.searchsorted(jnp.asarray(table, jnp.int32), ticket, side="right")
    return jax.random.permutation(jax.random.fold_in(key, 2), amount)[rank].astype(jnp.int32)


def scatter_about(stream_key, extent, width, reach, pieces=(), kind=jnp.bfloat16):
    values = width * jax.random.normal(stream_key, extent, jnp.float32)
    if pieces:
        values = values * level_of(stream_key, extent, pieces, -0.22, 0.18)
    return jnp.clip(values, -reach, reach).astype(kind)


def setup_inputs(seed: int = 0) -> dict:
    streams_of = jax.random.split(jax.random.key(seed), 7)
    images = draw_images(jax.random.fold_in(streams_of[6], 71), 0)
    labels = plant(ranked_ids(streams_of[1], (BATCH,), TAXA, 2), jax.random.fold_in(streams_of[1], 3), 0, TAXA - 1).astype(jnp.int32)
    taxon_emb = scatter_about(streams_of[2], (TAXA, E), 0.5, 3.0, ((0, 16),))
    node_emb = scatter_about(streams_of[3], (NODES, E), 0.5, 3.0, ((0, 16),))
    proj = scatter_about(streams_of[4], (E, E), E ** -0.5, 0.25)
    lineage = draw_lineage(jax.random.fold_in(streams_of[6], 71), 0)
    return dict(images=images, labels=labels, taxon_emb=taxon_emb, node_emb=node_emb, proj=proj, lineage=lineage)


logit_scale = 0.1


def reference(images, labels, taxon_emb, node_emb, proj, lineage):
    present = lineage >= 0
    safe_ids = jnp.clip(lineage, 0, NODES - 1).astype(jnp.int32)
    running = taxon_emb.astype(jnp.float32)
    for column in range(LEVELS):
        picked = jnp.take(node_emb, safe_ids[:, column], axis=0).astype(jnp.float32)
        running = running + jnp.where(present[:, column:column + 1], picked, jnp.float32(0.0))
    summed = running.astype(jnp.bfloat16)
    protos = jnp.dot(summed, proj, preferred_element_type=jnp.float32).astype(jnp.bfloat16)
    class_iota = jnp.arange(TAXA, dtype=jnp.int32)
    image_blocks = images.reshape(N_GRP, B_DEV, E)
    label_blocks = labels.reshape(N_GRP, B_DEV)

    def one_block(state_pair, inputs):
        loss_sum, class_sum = state_pair
        block_rows, block_labels = inputs
        scores = logit_scale * lax.dot_general(block_rows, protos, (((1,), (1,)), ((), ())), preferred_element_type=jnp.float32)
        row_top = jnp.max(scores, axis=1)
        exp_scores = jnp.exp(scores - row_top[:, None])
        row_total = jnp.sum(exp_scores, axis=1)
        label_hit = block_labels[:, None] == class_iota[None, :]
        label_score = jnp.sum(jnp.where(label_hit, scores, jnp.float32(0.0)), axis=1)
        loss_sum = loss_sum + jnp.sum(row_top + jnp.log(row_total) - label_score)
        weights = (exp_scores / row_total[:, None] - label_hit.astype(jnp.float32)).astype(jnp.bfloat16)
        row_grads = (logit_scale * jnp.dot(weights, protos, preferred_element_type=jnp.float32)).astype(jnp.bfloat16)
        class_sum = class_sum + lax.dot_general(weights, block_rows, (((0,), (0,)), ((), ())), preferred_element_type=jnp.float32)
        return (loss_sum, class_sum), row_grads

    initial = (jnp.float32(0.0), jnp.zeros((TAXA, E), jnp.float32))
    (loss_sum, class_sum), row_grads = lax.scan(one_block, initial, (image_blocks, label_blocks))
    loss = loss_sum / jnp.float32(BATCH)
    grad_images = row_grads.reshape(BATCH, E)
    class_grad = (logit_scale * class_sum).astype(jnp.bfloat16)
    grad_proj = lax.dot_general(summed, class_grad, (((0,), (0,)), ((), ())), preferred_element_type=jnp.float32)
    grad_taxon = lax.dot_general(class_grad, proj, (((1,), (1,)), ((), ())), preferred_element_type=jnp.float32).astype(jnp.bfloat16)
    taxon_wide = grad_taxon.astype(jnp.float32)
    grad_node = jnp.zeros((NODES, E), jnp.float32)
    for column in range(LEVELS):
        masked = jnp.where(present[:, column:column + 1], taxon_wide, jnp.float32(0.0))
        grad_node = grad_node + jax.ops.segment_sum(masked, safe_ids[:, column], num_segments=NODES)
    return (loss, grad_images, grad_taxon, grad_node, grad_proj)
```

```python
import jax
import jax.numpy as jnp
from jax import lax
from jax.experimental import pallas as pl
from jax.experimental.pallas import tpu as pltpu
from jax.sharding import PartitionSpec as P

MESH = pl.DeviceIdType.MESH
f32, bf16, i32 = jnp.float32, jnp.bfloat16, jnp.int32
scale = 0.1
E, LEVELS, T, B, N = 512, 7, 2048, 512, 512
NX, NY, NZ, NC = 4, 4, 8, 2
CLS = NZ * NC
GRP = NX * NY
BATCH = B * GRP
NT = (((1,), (1,)), ((), ()))
TN = (((0,), (0,)), ((), ()))


def dot(a, b):
    return jnp.dot(a, b, preferred_element_type=f32)


def dot_nt(a, b):
    return lax.dot_general(a, b, NT, preferred_element_type=f32)


def dot_tn(a, b):
    return lax.dot_general(a, b, TN, preferred_element_type=f32)


def rows(start, size):
    return pl.ds(pl.multiple_of(start, size), size)


def body(
    lin_ref, lab_ref, img_h, tax_h, node_h, proj_h,
    loss_o, gi_o, gt_o, gn_o, gp_o,
    img, tax, node, proj, lin16, cnt, base32, summed, sc32, pb, vv, acc,
    pub, pubs, ids, idss, stat, stats, labt, labs, far, fars, frow,
    us, ucr, uh, uzr, ug, ppb, ppx, ppxs, ppy, pa, lt, ltx, ltxs, lty,
    gp, rb1, tb1, g2, rb2, tb2, gt, gnb, gib, gpb, lossb,
    in_sem, out_sem,
    pub_s, pub_r, ids_s, ids_r, st_s, st_r, lab_s, lab_r, far_s, far_r,
    rs_s, rs_r, ag_s, ag_r, uc_s, uc_r, uz_s, uz_r, ug_s, ug_r,
    px_s, px_r, py_s, py_r, pz_s, pz_r, lx_s, lx_r, ly_s, ly_r,
):
    g = lax.axis_index("grp")
    c = lax.axis_index("cls")
    x, y = g // NY, lax.rem(g, NY)
    z, k = c // NC, lax.rem(c, NC)
    pos = (x, y)

    def at_x(d):
        return (lax.rem(x + d, NX) * NY + y, c)

    def at_y(d):
        return (x * NY + lax.rem(y + d, NY), c)

    def at_z(d):
        return (g, lax.rem(z + d, NZ) * NC + k)

    def at_c(d):
        return (g, lax.rem(c + d, CLS))

    mate = (g, z * NC + (1 - k))
    near = (at_x, at_y)
    started = []

    def rc(src, dst, ss, rs, dev):
        return pltpu.make_async_remote_copy(
            src_ref=src, dst_ref=dst, send_sem=ss, recv_sem=rs, device_id=dev, device_id_type=MESH
        )

    def go(src, dst, ss, rs, dev):
        cp = rc(src, dst, ss, rs, dev)
        cp.start()
        started.append(cp)
        return cp

    def got(dst, ss, rs):
        rc(dst, dst, ss, rs, mate).wait_recv()

    loads = [
        pltpu.make_async_copy(s, d, in_sem.at[i])
        for i, (s, d) in enumerate(((node_h, node), (img_h, img), (proj_h, proj), (tax_h, tax)))
    ]
    for cp in loads:
        cp.start()
    pubs[...] = jnp.zeros_like(pubs)
    fars[...] = jnp.zeros_like(fars)
    idss[...] = jnp.full_like(idss, -1)

    barrier = pltpu.get_barrier_semaphore()

    def greet(d, _):
        pl.semaphore_signal(barrier, inc=1, device_id=at_c(d), device_id_type=MESH)
        return 0

    lax.fori_loop(1, CLS, greet, 0)
    for d in range(1, NX):
        pl.semaphore_signal(barrier, inc=1, device_id=at_x(d), device_id_type=MESH)
    for d in range(1, NY):
        pl.semaphore_signal(barrier, inc=1, device_id=at_y(d), device_id_type=MESH)

    base = c * N
    tbase = c * T
    lin16[...] = jnp.full_like(lin16, -1)
    lin16[0:LEVELS, :] = lin_ref[...]
    lin = lin16[...]
    remote = (lin >= 0) & (lin < base)
    pid = jnp.max(jnp.where(remote, lin, -1), axis=1, keepdims=True)
    rem16 = jnp.where(remote, 1.0, 0.0).astype(bf16)
    cnt[N : N + 16, :] = rem16
    lane_n = lax.broadcasted_iota(i32, (16, N), 1)
    last = lin16[:, T - 128 : T][:, 127:128]
    loads[0].wait()
    sel = jnp.where(last - base == lane_n, 1.0, 0.0).astype(bf16)
    pub[...] = dot(sel, node[...])[0:8].astype(bf16)
    ids[...] = jnp.broadcast_to(pid[0:8], (8, 128))

    pl.semaphore_wait(barrier, CLS - 1 + NX - 1 + NY - 1)

    def up8(r):
        return rows(r * 8, 8)

    def send_pub(d, _):
        @pl.when(c + d < CLS)
        def _():
            rc(pub, pubs.at[up8(c), :], pub_s.at[d], pub_r.at[d], at_c(d)).start()
        return 0

    lax.fori_loop(1, CLS, send_pub, 0)

    def count_block(i, _):
        nid = lax.broadcasted_iota(i32, (32, T), 0) + (i * 32 + base)
        hit = nid == lin16[0:1, :]
        for l in range(1, LEVELS):
            hit = hit | (nid == lin16[l : l + 1, :])
        cnt[rows(i * 32, 32), :] = jnp.where(hit, 1.0, 0.0).astype(bf16)
        return 0

    lax.fori_loop(0, N // 32, count_block, 0)
    loads[1].wait()
    loads[2].wait()
    loads[3].wait()
    vv[...] = dot_nt(img[...], proj[...]).astype(bf16)

    def local_sum(i, _):
        r = rows(i * 256, 256)
        base32[r, :] = tax[r, :].astype(f32) + dot_tn(cnt[0:N, r], node[...])
        return 0

    lax.fori_loop(0, T // 256, local_sum, 0)

    def wait_pub(d, _):
        @pl.when(c >= d)
        def _():
            got(pubs.at[up8(c - d), :], pub_s.at[d], pub_r.at[d])
        return 0

    lax.fori_loop(1, CLS, wait_pub, 0)
    lane = lax.broadcasted_iota(i32, (16, 128), 1)
    want = (pid >> 9) * 8 + lax.broadcasted_iota(i32, (16, 1), 0)
    pick = jnp.where((want == lane) & (pid >= 0), 1.0, 0.0).astype(bf16)
    prefix = dot(pick, pubs[...]).astype(bf16)

    def score_block(i, top):
        r = rows(i * 256, 256)
        s = (base32[r, :] + dot_tn(cnt[N : N + 16, r], prefix)).astype(bf16)
        summed[r, :] = s
        pr = dot(s, proj[...]).astype(bf16)
        st = scale * dot_nt(pr, img[...])
        sc32[r, :] = st
        return jnp.maximum(top, jnp.max(st.reshape(32, 8, B), axis=0))

    top8 = lax.fori_loop(0, T // 256, score_block, jnp.full((8, B), -jnp.inf, f32))
    mtop = jnp.max(top8, axis=0, keepdims=True)
    label = lab_ref[...] - tbase

    def exp_block(i, carry):
        tot, ls = carry
        r = rows(i * 256, 256)
        st = sc32[r, :]
        hit = lax.broadcasted_iota(i32, (256, B), 0) + i * 256 == label
        p = jnp.exp(st - mtop)
        ls = ls + jnp.sum(jnp.where(hit, st, 0.0).reshape(32, 8, B), axis=0)
        tot = tot + jnp.sum(p.reshape(32, 8, B), axis=0)
        sc32[r, :] = p
        pb[r, 0:B] = p.astype(bf16)
        pb[r, B : 2 * B] = jnp.where(hit, 1.0, 0.0).astype(bf16)
        return tot, ls

    zero8 = jnp.zeros((8, B), f32)
    tot8, ls8 = lax.fori_loop(0, T // 256, exp_block, (zero8, zero8))
    tot = jnp.sum(tot8, axis=0, keepdims=True)
    for q in range(4):
        stat[q : q + 1, :] = mtop[:, q * 128 : q * 128 + 128]
        stat[q + 4 : q + 5, :] = tot[:, q * 128 : q * 128 + 128]
    lsum = ls8[:, 0:128] + ls8[:, 128:256] + ls8[:, 256:384] + ls8[:, 384:512]
    labt[...] = jnp.broadcast_to(jnp.sum(lsum, keepdims=True), (8, 128))

    def send_stat(d, _):
        rc(stat, stats.at[c], st_s.at[d], st_r.at[d], at_c(d)).start()
        return 0

    def send_lab(d, _):
        rc(labt, labs.at[c], lab_s.at[d], lab_r.at[d], at_c(d)).start()
        return 0

    def send_ids(d, _):
        @pl.when(c >= d)
        def _():
            rc(ids, idss.at[up8(c), :], ids_s.at[d], ids_r.at[d], at_c(CLS - d)).start()
        return 0

    lax.fori_loop(1, CLS, send_stat, 0)
    lax.fori_loop(1, CLS, send_lab, 0)
    lax.fori_loop(1, CLS, send_ids, 0)
    stats[c] = stat[...]
    labs[c] = labt[...]

    acc[...] = jnp.zeros_like(acc)

    def u_block(i, _):
        r = rows(i * 512, 512)
        acc[...] += dot_tn(summed[r, :], pb[r, :])
        return 0

    lax.fori_loop(0, T // 512, u_block, 0)

    def wait_stat(d, _):
        got(stats.at[lax.rem(c + CLS - d, CLS)], st_s.at[d], st_r.at[d])
        return 0

    lax.fori_loop(1, CLS, wait_stat, 0)
    all_m = stats[:, 0:4, :]
    gtop = jnp.max(all_m, axis=0)
    gtot = jnp.sum(stats[:, 4:8, :] * jnp.exp(all_m - gtop[None]), axis=0)
    fac = jnp.exp(stat[0:4, :] - gtop) / gtot
    for q in range(4):
        frow[:, q * 128 : q * 128 + 128] = fac[q : q + 1, :]
    fr = frow[...]
    ls_here = jnp.sum(gtop + jnp.log(gtot), keepdims=True)
    us[...] = (acc[:, 0:B] * fr - acc[:, B : 2 * B]).astype(bf16)
    other = rows((1 - k) * 256, 256)
    mine = rows(k * 256, 256)
    uc = go(us.at[other, :], ucr, uc_s.at[0], uc_r.at[0], mate)

    def grads(row):
        r = rows(row, 256)
        hit = lax.broadcasted_iota(i32, (256, B), 0) + row == label
        w = (sc32[r, :] * fr - jnp.where(hit, 1.0, 0.0)).astype(bf16)
        gp[r, :] = (scale * dot(w, vv[...])).astype(bf16)

    def q4(v):
        return lax.rem(v, 4)

    def stage(h, s):
        axis = (h + s) % 2
        p = pos[axis]
        n = 128 if s == 0 else 32
        right, left = near[axis](1), near[axis](3)
        src = gp if s == 0 else g2.at[h]
        rb = (rb1 if s == 0 else rb2).at[h]
        tb = (tb1 if s == 0 else tb2).at[h]
        off = 1024 * h if s == 0 else 0
        sem = (h * 2 + s) * 6

        def part(q, half):
            return rows(off + q * (2 * n) + half * n, n)

        def send(ref, i, dev):
            go(ref, rb.at[i], rs_s.at[sem + i], rs_r.at[sem + i], dev)

        def get(i):
            got(rb.at[i], rs_s.at[sem + i], rs_r.at[sem + i])
            return rb[i].astype(f32)

        def own(q, half):
            return src[part(q, half), :].astype(f32)

        def first():
            send(src.at[part(q4(p + 2), 0), :], 0, right)
            send(src.at[part(q4(p + 2), 1), :], 3, left)

        def second():
            send(src.at[part(q4(p + 1), 1), :], 1, right)
            send(src.at[part(q4(p + 3), 0), :], 4, left)

        def third():
            tb[0] = (own(q4(p + 1), 0) + get(0)).astype(bf16)
            send(tb.at[0], 2, right)
            tb[1] = (own(q4(p + 3), 1) + get(3)).astype(bf16)
            send(tb.at[1], 5, left)

        def last():
            a = own(p, 0) + get(4) + get(2)
            b = own(p, 1) + get(1) + get(5)
            return a.astype(bf16), b.astype(bf16)

        return first, second, third, last

    s1 = (stage(0, 0), stage(1, 0))
    s2 = (stage(0, 1), stage(1, 1))
    for h in range(2):
        grads(1024 * h + q4(pos[h] + 2) * 256)
        s1[h][0]()
    for h in range(2):
        grads(1024 * h + q4(pos[h] + 1) * 256)
        grads(1024 * h + q4(pos[h] + 3) * 256)
        s1[h][1]()
    for h in range(2):
        grads(1024 * h + pos[h] * 256)

    got(ucr, uc_s.at[0], uc_r.at[0])
    uh[...] = (us[mine, :].astype(f32) + ucr[...].astype(f32)).astype(bf16)
    for d in range(1, NZ):
        go(uh.at[rows(q8(z + d) * 32, 32), :], uzr.at[z], uz_s.at[d], uz_r.at[d], at_z(d))
    uzr[z] = uh[rows(z * 32, 32), :]

    for h in range(2):
        s1[h][2]()
    for h in range(2):
        a, b = s1[h][3]()
        g2[h, 0:128, :] = a
        g2[h, 128:256, :] = b
        s2[h][0]()
        s2[h][1]()

    for d in range(1, NZ):
        got(uzr.at[q8(z + NZ - d)], uz_s.at[d], uz_r.at[d])
    uslice = uzr[0].astype(f32)
    for d in range(1, NZ):
        uslice = uslice + uzr[d].astype(f32)
    uslice = uslice.astype(bf16)
    slot = rows((k * 8 + z) * 32, 32)
    ug[slot, :] = uslice
    for d in range(1, NZ):
        go(ug.at[slot, :], ug.at[slot, :], ug_s.at[d], ug_r.at[d], at_z(d))
    ppb[...] = (scale * dot(uslice, img[...])).astype(bf16)
    for d in range(1, 4):
        go(ppb, ppx.at[d], px_s.at[d], px_r.at[d], at_x(d))

    def wait_lab(d, _):
        got(labs.at[lax.rem(c + CLS - d, CLS)], lab_s.at[d], lab_r.at[d])
        return 0

    lax.fori_loop(1, CLS, wait_lab, 0)
    lt[...] = ls_here - jnp.sum(labs[...], axis=0)
    for d in range(1, 4):
        go(lt, ltx.at[d], lx_s.at[d], lx_r.at[d], at_x(d))

    for h in range(2):
        s2[h][2]()

    ag = []
    for h in range(2):
        a, b = s2[h][3]()
        axis1, axis2 = h, 1 - h
        start = 1024 * h + pos[axis1] * 256 + pos[axis2] * 64
        gt[rows(start, 32), :] = a
        gt[rows(start + 32, 32), :] = b

        def ag_stage(s, h=h):
            axis = (h + s) % 2
            p = pos[axis]
            n = 128 if s == 0 else 32
            right, left = near[axis](1), near[axis](3)
            off = 1024 * h + (0 if s == 0 else pos[h] * 256)
            sem = (h * 2 + s) * 6

            def part(q, half):
                return gt.at[rows(off + q * (2 * n) + half * n, n), :]

            def send(q, half, i, dev):
                ref = part(q, half)
                go(ref, ref, ag_s.at[sem + i], ag_r.at[sem + i], dev)

            def get(q, half, i):
                got(part(q, half), ag_s.at[sem + i], ag_r.at[sem + i])

            def first():
                send(p, 0, 0, right)
                send(p, 1, 3, left)
                send(p, 1, 1, right)
                send(p, 0, 4, left)

            def second():
                get(q4(p + 3), 0, 0)
                send(q4(p + 3), 0, 2, right)
                get(q4(p + 1), 1, 3)
                send(q4(p + 1), 1, 5, left)

            def last():
                get(q4(p + 3), 1, 1)
                get(q4(p + 1), 0, 4)
                get(q4(p + 2), 0, 2)
                get(q4(p + 2), 1, 5)

            return first, second, last

        ag.append((ag_stage(0), ag_stage(1)))
        ag[h][1][0]()

    for h in range(2):
        ag[h][1][1]()

    for d in range(1, 4):
        got(ppx.at[d], px_s.at[d], px_r.at[d])
        got(ltx.at[d], lx_s.at[d], lx_r.at[d])
    ppxs[...] = (
        ppb[...].astype(f32) + ppx[1].astype(f32) + ppx[2].astype(f32) + ppx[3].astype(f32)
    ).astype(bf16)
    ltxs[...] = lt[...] + ltx[1] + ltx[2] + ltx[3]
    for d in range(1, 4):
        go(ppxs, ppy.at[d], py_s.at[d], py_r.at[d], at_y(d))
        go(ltxs, lty.at[d], ly_s.at[d], ly_r.at[d], at_y(d))

    for h in range(2):
        ag[h][1][2]()
        ag[h][0][0]()

    for d in range(1, NZ):
        got(ug.at[rows((k * 8 + q8(z + NZ - d)) * 32, 32), :], ug_s.at[d], ug_r.at[d])
    go(ug.at[mine, :], ug.at[mine, :], uc_s.at[1], uc_r.at[1], mate)

    for d in range(1, 4):
        got(ppy.at[d], py_s.at[d], py_r.at[d])
        got(lty.at[d], ly_s.at[d], ly_r.at[d])
    pa[slot, :] = (
        ppxs[...].astype(f32) + ppy[1].astype(f32) + ppy[2].astype(f32) + ppy[3].astype(f32)
    ).astype(bf16)
    for d in range(1, NZ):
        go(pa.at[slot, :], pa.at[slot, :], pz_s.at[d], pz_r.at[d], at_z(d))
    total = ltxs[...] + lty[1] + lty[2] + lty[3]
    lossb[...] = total * (1.0 / BATCH)

    for h in range(2):
        ag[h][0][1]()

    got(ug.at[other, :], uc_s.at[1], uc_r.at[1])
    gib[...] = (scale * dot_tn(ug[...], proj[...])).astype(bf16)
    outs = [pltpu.make_async_copy(gib, gi_o, out_sem.at[0])]
    outs[-1].start()

    for d in range(1, NZ):
        got(pa.at[rows((k * 8 + q8(z + NZ - d)) * 32, 32), :], pz_s.at[d], pz_r.at[d])
    go(pa.at[mine, :], pa.at[mine, :], uc_s.at[2], uc_r.at[2], mate)

    for h in range(2):
        ag[h][0][2]()
    outs.append(pltpu.make_async_copy(gt, gt_o, out_sem.at[1]))
    outs[-1].start()

    far[...] = dot(cnt[N : N + 16, :], gt[...])[0:8].astype(bf16)

    def send_far(d, _):
        @pl.when(c >= d)
        def _():
            rc(far, fars.at[up8(c), :], far_s.at[d], far_r.at[d], at_c(CLS - d)).start()
        return 0

    lax.fori_loop(1, CLS, send_far, 0)

    def node_block(i, _):
        r = rows(i * 128, 128)
        gnb[r, :] = dot(cnt[r, :], gt[...])
        return 0

    lax.fori_loop(0, N // 128, node_block, 0)

    got(pa.at[other, :], uc_s.at[2], uc_r.at[2])
    gpb[...] = pa[...].astype(f32)
    outs.append(pltpu.make_async_copy(gpb, gp_o, out_sem.at[2]))
    outs[-1].start()
    outs.append(pltpu.make_async_copy(lossb, loss_o, out_sem.at[3]))
    outs[-1].start()

    def wait_far(d, _):
        @pl.when(c + d < CLS)
        def _():
            got(idss.at[up8(c + d), :], ids_s.at[d], ids_r.at[d])
            got(fars.at[up8(c + d), :], far_s.at[d], far_r.at[d])
        return 0

    lax.fori_loop(1, CLS, wait_far, 0)
    ri = lax.broadcasted_iota(i32, (128, 128), 0)
    ci = lax.broadcasted_iota(i32, (128, 128), 1)
    idrow = jnp.max(jnp.where(ri == ci, idss[...], -1), axis=0, keepdims=True)
    match = lax.broadcasted_iota(i32, (N, 128), 0) + base == idrow
    gnb[...] += dot(jnp.where(match, 1.0, 0.0).astype(bf16), fars[...])
    outs.append(pltpu.make_async_copy(gnb, gn_o, out_sem.at[4]))
    outs[-1].start()

    for cp in started:
        cp.wait_send()

    def drain(d, _):
        rc(stat, stat, st_s.at[d], st_r.at[d], mate).wait_send()
        rc(labt, labt, lab_s.at[d], lab_r.at[d], mate).wait_send()

        @pl.when(c + d < CLS)
        def _():
            rc(pub, pub, pub_s.at[d], pub_r.at[d], mate).wait_send()

        @pl.when(c >= d)
        def _():
            rc(ids, ids, ids_s.at[d], ids_r.at[d], mate).wait_send()
            rc(far, far, far_s.at[d], far_r.at[d], mate).wait_send()

        return 0

    lax.fori_loop(1, CLS, drain, 0)
    for cp in outs:
        cp.wait()


def q8(v):
    return lax.rem(v, NZ)


def per_device(images, labels, taxon_emb, node_emb, proj, lineage):
    dma = pltpu.SemaphoreType.DMA
    vm = pltpu.VMEM
    scratch = [
        vm((B, E), bf16), vm((T, E), bf16), vm((N, E), bf16), vm((E, E), bf16),
        vm((16, T), i32), vm((N + 16, T), bf16), vm((T, E), f32), vm((T, E), bf16),
        vm((T, B), f32), vm((T, 2 * B), bf16), vm((B, E), bf16), vm((E, 2 * B), f32),
        vm((8, E), bf16), vm((CLS * 8, E), bf16), vm((8, 128), i32), vm((CLS * 8, 128), i32),
        vm((8, 128), f32), vm((CLS, 8, 128), f32), vm((8, 128), f32), vm((CLS, 8, 128), f32),
        vm((8, E), bf16), vm((CLS * 8, E), bf16), vm((1, B), f32),
        vm((E, B), bf16), vm((256, B), bf16), vm((256, B), bf16), vm((NZ, 32, B), bf16),
        vm((E, B), bf16), vm((32, E), bf16), vm((4, 32, E), bf16), vm((32, E), bf16),
        vm((4, 32, E), bf16), vm((E, E), bf16), vm((8, 128), f32), vm((4, 8, 128), f32),
        vm((8, 128), f32), vm((4, 8, 128), f32),
        vm((T, E), bf16), vm((2, 6, 128, E), bf16), vm((2, 2, 128, E), bf16),
        vm((2, 256, E), bf16), vm((2, 6, 32, E), bf16), vm((2, 2, 32, E), bf16),
        vm((T, E), bf16), vm((N, E), f32), vm((B, E), bf16), vm((E, E), f32), vm((8, 128), f32),
        dma((4,)), dma((5,)),
    ]
    scratch += [dma((CLS,))] * 10
    scratch += [dma((24,))] * 4
    scratch += [dma((3,))] * 2 + [dma((NZ,))] * 4
    scratch += [dma((4,))] * 4 + [dma((NZ,))] * 2 + [dma((4,))] * 4
    hbm = pl.BlockSpec(memory_space=pl.ANY)
    vmem = pl.BlockSpec(memory_space=pltpu.VMEM)
    loss, gi, gt, gn, gp = pl.pallas_call(
        body,
        out_shape=(
            jax.ShapeDtypeStruct((8, 128), f32),
            jax.ShapeDtypeStruct((B, E), bf16),
            jax.ShapeDtypeStruct((T, E), bf16),
            jax.ShapeDtypeStruct((N, E), f32),
            jax.ShapeDtypeStruct((E, E), f32),
        ),
        in_specs=[vmem, vmem, hbm, hbm, hbm, hbm],
        out_specs=[hbm] * 5,
        scratch_shapes=scratch,
        compiler_params=pltpu.CompilerParams(
            collective_id=0, has_side_effects=True, vmem_limit_bytes=60 * 1024 * 1024
        ),
    )(lineage.T, labels.reshape(1, B), images, taxon_emb, node_emb, proj)
    return (loss[0, 0], gi, gt, gn, gp)


def solution(mesh):
    in_specs = (P("grp", None), P("grp"), P("cls", None), P("cls", None), P(), P("cls", None))
    out_specs = (P(), P("grp", None), P("cls", None), P("cls", None), P())
    return jax.shard_map(
        per_device, mesh=mesh, in_specs=in_specs, out_specs=out_specs, check_vma=False
    )
```

```python
import jax
import jax.numpy as jnp
from jax import lax
from jax.experimental import pallas as pl
from jax.experimental.pallas import tpu as pltpu
from jax.sharding import PartitionSpec as P

MESH = pl.DeviceIdType.MESH
f32, bf16, i32 = jnp.float32, jnp.bfloat16, jnp.int32
scale = 0.1
E, LEVELS, T, B, N = 512, 7, 2048, 512, 512
NX, NY, NZ, NC = 4, 4, 8, 2
CLS = NZ * NC
GRP = NX * NY
BATCH = B * GRP
NT = (((1,), (1,)), ((), ()))
TN = (((0,), (0,)), ((), ()))


def dot(a, b):
    return jnp.dot(a, b, preferred_element_type=f32)


def dot_nt(a, b):
    return lax.dot_general(a, b, NT, preferred_element_type=f32)


def dot_tn(a, b):
    return lax.dot_general(a, b, TN, preferred_element_type=f32)


def rows(start, size):
    return pl.ds(pl.multiple_of(start, size), size)


def body(
    lin_h, lab_h, img_h, tax_h, node_h, proj_h,
    lossb, ug, gt, cnt, pa, near_rows, sels, projo,
    lin_ref, lab_ref, img, tax, node, proj, lin16, base32, summed, sc32, pb, vv, acc, remt,
    pub, pubs, ids, idss, stat, stats, labt, labs, far, fars, frow,
    us, ucr, uh, uzr, ppb, ppx, ppxs, ppy, lt, ltx, ltxs, lty,
    fx, fxr, fy, fyr,
    gp, rb1, tb1, g2, rb2, tb2,
    in_sem,
    pub_s, pub_r, ids_s, ids_r, st_s, st_r, lab_s, lab_r, far_s, far_r,
    rs_s, rs_r, ag_s, ag_r, uc_s, uc_r, uz_s, uz_r, ug_s, ug_r,
    px_s, px_r, py_s, py_r, pz_s, pz_r, lx_s, lx_r, ly_s, ly_r,
    fx_s, fx_r, fy_s, fy_r,
):
    g = lax.axis_index("grp")
    c = lax.axis_index("cls")
    x, y = g // NY, lax.rem(g, NY)
    z, k = c // NC, lax.rem(c, NC)
    pos = (x, y)

    def at_x(d):
        return (lax.rem(x + d, NX) * NY + y, c)

    def at_y(d):
        return (x * NY + lax.rem(y + d, NY), c)

    def at_z(d):
        return (g, lax.rem(z + d, NZ) * NC + k)

    def at_c(d):
        return (g, lax.rem(c + d, CLS))

    mate = (g, z * NC + (1 - k))
    near = (at_x, at_y)
    started = []

    def rc(src, dst, ss, rs, dev):
        return pltpu.make_async_remote_copy(
            src_ref=src, dst_ref=dst, send_sem=ss, recv_sem=rs, device_id=dev, device_id_type=MESH
        )

    def go(src, dst, ss, rs, dev):
        cp = rc(src, dst, ss, rs, dev)
        cp.start()
        started.append(cp)
        return cp

    def got(dst, ss, rs):
        rc(dst, dst, ss, rs, mate).wait_recv()

    def far_first(i):
        return 8 + (1 - 2 * lax.rem(i, 2)) * ((i + 1) // 2)

    def peers(f):
        def step(i, _):
            f(far_first(i))
            return 0

        lax.fori_loop(0, CLS - 1, step, 0)

    loads = [
        pltpu.make_async_copy(s, d, in_sem.at[i])
        for i, (s, d) in enumerate(((lin_h, lin_ref), (node_h, node), (img_h, img), (proj_h, proj), (tax_h, tax), (lab_h, lab_ref)))
    ]
    for cp in loads:
        cp.start()
    pubs[...] = jnp.zeros_like(pubs)
    fars[...] = jnp.zeros_like(fars)
    idss[...] = jnp.full_like(idss, -1)

    barrier = pltpu.get_barrier_semaphore()

    def greet(d, _):
        pl.semaphore_signal(barrier, inc=1, device_id=at_c(d), device_id_type=MESH)
        return 0

    lax.fori_loop(1, CLS, greet, 0)
    for d in range(1, NX):
        pl.semaphore_signal(barrier, inc=1, device_id=at_x(d), device_id_type=MESH)
    for d in range(1, NY):
        pl.semaphore_signal(barrier, inc=1, device_id=at_y(d), device_id_type=MESH)

    base = c * N
    tbase = c * T
    lin16[...] = jnp.full_like(lin16, -1)
    loads[0].wait()
    lin16[0:LEVELS, :] = lin_ref[...]
    lin = lin16[...]
    remote = (lin >= 0) & (lin < base)
    pid = jnp.max(jnp.where(remote, lin, -1), axis=1, keepdims=True)
    rem16 = jnp.where(remote, 1.0, 0.0).astype(bf16)
    lane_n = lax.broadcasted_iota(i32, (16, N), 1)
    last = lin16[:, T - 128 : T][:, 127:128]
    loads[1].wait()
    sel = jnp.where(last - base == lane_n, 1.0, 0.0).astype(bf16)
    sels[...] = sel
    pub[...] = dot(sel, node[...])[0:8].astype(bf16)
    ids[...] = jnp.broadcast_to(pid[0:8], (8, 128))

    pl.semaphore_wait(barrier, CLS - 1 + NX - 1 + NY - 1)

    def up8(r):
        return rows(r * 8, 8)

    def send_pub(d):
        @pl.when(c + d < CLS)
        def _():
            rc(pub, pubs.at[up8(c), :], pub_s.at[d], pub_r.at[d], at_c(d)).start()

    peers(send_pub)

    def count_block(i, _):
        nid = lax.broadcasted_iota(i32, (32, T), 0) + (i * 32 + base)
        hit = nid == lin16[0:1, :]
        for l in range(1, LEVELS):
            hit = hit | (nid == lin16[l : l + 1, :])
        cnt[rows(i * 32, 32), :] = jnp.where(hit, 1.0, 0.0).astype(bf16)
        return 0

    lax.fori_loop(0, N // 32, count_block, 0, unroll=2)
    eye = lax.broadcasted_iota(i32, (16, 128), 0) == lax.broadcasted_iota(i32, (16, 128), 1)
    remt[...] = dot_tn(rem16, jnp.where(eye, 1.0, 0.0).astype(bf16)).astype(bf16)
    for cp in loads[2:]:
        cp.wait()
    projo[...] = proj[...]
    vv[...] = dot_nt(img[...], proj[...]).astype(bf16)

    def local_sum(i, _):
        r = rows(i * 256, 256)
        base32[r, :] = tax[r, :].astype(f32) + dot_tn(cnt[:, r], node[...])
        return 0

    lax.fori_loop(0, T // 256, local_sum, 0, unroll=2)

    def wait_pub(d, _):
        @pl.when(c >= d)
        def _():
            got(pubs.at[up8(c - d), :], pub_s.at[d], pub_r.at[d])
        return 0

    lax.fori_loop(1, CLS, wait_pub, 0)
    lane = lax.broadcasted_iota(i32, (128, 128), 1)
    pid128 = jnp.concatenate([pid, jnp.full((112, 1), -1, i32)], axis=0)
    want = (pid128 >> 9) * 8 + lax.broadcasted_iota(i32, (128, 1), 0)
    pick = jnp.where((want == lane) & (pid128 >= 0), 1.0, 0.0).astype(bf16)
    prefix = dot(pick, pubs[...]).astype(bf16)

    def score_block(i, top):
        r = rows(i * 256, 256)
        s = (base32[r, :] + dot(remt[r, :], prefix)).astype(bf16)
        summed[r, :] = s
        pr = dot(s, proj[...]).astype(bf16)
        st = scale * dot_nt(pr, img[...])
        sc32[r, :] = st
        return jnp.maximum(top, jnp.max(st.reshape(32, 8, B), axis=0))

    top8 = lax.fori_loop(0, T // 256, score_block, jnp.full((8, B), -jnp.inf, f32), unroll=2)
    mtop = jnp.max(top8, axis=0, keepdims=True)
    label = lab_ref[...] - tbase

    def exp_block(i, carry):
        tot, ls = carry
        r = rows(i * 256, 256)
        st = sc32[r, :]
        hit = lax.broadcasted_iota(i32, (256, B), 0) + i * 256 == label
        p = jnp.exp(st - mtop)
        ls = ls + jnp.sum(jnp.where(hit, st, 0.0).reshape(32, 8, B), axis=0)
        tot = tot + jnp.sum(p.reshape(32, 8, B), axis=0)
        sc32[r, :] = p
        pb[r, 0:B] = p.astype(bf16)
        pb[r, B : 2 * B] = jnp.where(hit, 1.0, 0.0).astype(bf16)
        return tot, ls

    zero8 = jnp.zeros((8, B), f32)
    tot8, ls8 = lax.fori_loop(0, T // 256, exp_block, (zero8, zero8))
    tot = jnp.sum(tot8, axis=0, keepdims=True)
    for q in range(4):
        stat[q : q + 1, :] = mtop[:, q * 128 : q * 128 + 128]
        stat[q + 4 : q + 5, :] = tot[:, q * 128 : q * 128 + 128]
    lsum = ls8[:, 0:128] + ls8[:, 128:256] + ls8[:, 256:384] + ls8[:, 384:512]
    labt[...] = jnp.broadcast_to(jnp.sum(lsum, keepdims=True), (8, 128))

    def send_stat(d):
        rc(stat, stats.at[c], st_s.at[d], st_r.at[d], at_c(d)).start()

    def send_lab(d):
        rc(labt, labs.at[c], lab_s.at[d], lab_r.at[d], at_c(d)).start()

    def send_ids(d):
        @pl.when(c >= d)
        def _():
            rc(ids, idss.at[up8(c), :], ids_s.at[d], ids_r.at[d], at_c(CLS - d)).start()

    peers(send_stat)
    stats[c] = stat[...]
    labs[c] = labt[...]

    acc[...] = jnp.zeros_like(acc)

    def u_block(i, _):
        r = rows(i * 512, 512)
        acc[...] += dot_tn(summed[r, :], pb[r, :])
        return 0

    lax.fori_loop(0, T // 512, u_block, 0)

    def wait_stat(d, _):
        got(stats.at[lax.rem(c + CLS - d, CLS)], st_s.at[d], st_r.at[d])
        return 0

    lax.fori_loop(1, CLS, wait_stat, 0)
    all_m = stats[:, 0:4, :]
    gtop = jnp.max(all_m, axis=0)
    gtot = jnp.sum(stats[:, 4:8, :] * jnp.exp(all_m - gtop[None]), axis=0)
    fac = jnp.exp(stat[0:4, :] - gtop) / gtot
    for q in range(4):
        frow[:, q * 128 : q * 128 + 128] = fac[q : q + 1, :]
    fr = frow[...]
    ls_here = jnp.sum(gtop + jnp.log(gtot), keepdims=True)
    us[...] = (acc[:, 0:B] * fr - acc[:, B : 2 * B]).astype(bf16)
    other = rows((1 - k) * 256, 256)
    mine = rows(k * 256, 256)
    uc = go(us.at[other, :], ucr, uc_s.at[0], uc_r.at[0], mate)

    peers(send_ids)
    peers(send_lab)

    def grads(row):
        r = rows(row, 256)
        hit = lax.broadcasted_iota(i32, (256, B), 0) + row == label
        w = (sc32[r, :] * fr - jnp.where(hit, 1.0, 0.0)).astype(bf16)
        gp[r, :] = (scale * dot(w, vv[...])).astype(bf16)

    def q4(v):
        return lax.rem(v, 4)

    def stage(h, s):
        axis = (h + s) % 2
        p = pos[axis]
        n = 128 if s == 0 else 32
        right, left = near[axis](1), near[axis](3)
        src = gp if s == 0 else g2.at[h]
        rb = (rb1 if s == 0 else rb2).at[h]
        tb = (tb1 if s == 0 else tb2).at[h]
        off = 1024 * h if s == 0 else 0
        sem = (h * 2 + s) * 6

        def part(q, half):
            return rows(off + q * (2 * n) + half * n, n)

        def send(ref, i, dev):
            go(ref, rb.at[i], rs_s.at[sem + i], rs_r.at[sem + i], dev)

        def get(i):
            got(rb.at[i], rs_s.at[sem + i], rs_r.at[sem + i])
            return rb[i].astype(f32)

        def own(q, half):
            return src[part(q, half), :].astype(f32)

        def first():
            send(src.at[part(q4(p + 2), 0), :], 0, right)
            send(src.at[part(q4(p + 2), 1), :], 3, left)

        def second():
            send(src.at[part(q4(p + 1), 1), :], 1, right)
            send(src.at[part(q4(p + 3), 0), :], 4, left)

        def third():
            tb[0] = (own(q4(p + 1), 0) + get(0)).astype(bf16)
            send(tb.at[0], 2, right)
            tb[1] = (own(q4(p + 3), 1) + get(3)).astype(bf16)
            send(tb.at[1], 5, left)

        def last():
            a = own(p, 0) + get(4) + get(2)
            b = own(p, 1) + get(1) + get(5)
            return a.astype(bf16), b.astype(bf16)

        return first, second, third, last

    s1 = (stage(0, 0), stage(1, 0))
    s2 = (stage(0, 1), stage(1, 1))
    for h in range(2):
        grads(1024 * h + q4(pos[h] + 2) * 256)
        s1[h][0]()
    for h in range(2):
        grads(1024 * h + q4(pos[h] + 1) * 256)
        grads(1024 * h + q4(pos[h] + 3) * 256)
        s1[h][1]()
    for h in range(2):
        grads(1024 * h + pos[h] * 256)

    got(ucr, uc_s.at[0], uc_r.at[0])
    uh[...] = (us[mine, :].astype(f32) + ucr[...].astype(f32)).astype(bf16)
    for d in range(1, NZ):
        go(uh.at[rows(q8(z + d) * 32, 32), :], uzr.at[z], uz_s.at[d], uz_r.at[d], at_z(d))
    uzr[z] = uh[rows(z * 32, 32), :]

    for h in range(2):
        s1[h][2]()
    for h in range(2):
        a, b = s1[h][3]()
        g2[h, 0:128, :] = a
        g2[h, 128:256, :] = b
        s2[h][0]()
        s2[h][1]()

    for d in range(1, NZ):
        got(uzr.at[q8(z + NZ - d)], uz_s.at[d], uz_r.at[d])
    uslice = uzr[0].astype(f32)
    for d in range(1, NZ):
        uslice = uslice + uzr[d].astype(f32)
    uslice = uslice.astype(bf16)
    slot = rows((k * 8 + z) * 32, 32)
    ug[slot, :] = uslice
    for d in range(1, NZ):
        go(ug.at[slot, :], ug.at[slot, :], ug_s.at[d], ug_r.at[d], at_z(d))
    ppb[...] = (scale * dot(uslice, img[...])).astype(bf16)
    for d in range(1, 4):
        go(ppb, ppx.at[d], px_s.at[d], px_r.at[d], at_x(d))

    def wait_lab(d, _):
        got(labs.at[lax.rem(c + CLS - d, CLS)], lab_s.at[d], lab_r.at[d])
        return 0

    lax.fori_loop(1, CLS, wait_lab, 0)
    lt[...] = ls_here - jnp.sum(labs[...], axis=0)
    for d in range(1, 4):
        go(lt, ltx.at[d], lx_s.at[d], lx_r.at[d], at_x(d))

    for h in range(2):
        s2[h][2]()

    def gather(h, s, blk):
        axis = (h + s) % 2
        p = pos[axis]
        right, left = near[axis](1), near[axis](3)
        if s == 0:
            step, off, sem = 256, 1024 * h + q4(pos[1 - h] + blk) * 64, (h * 5 + blk) * 6
        else:
            step, off, sem = 64, 1024 * h + pos[h] * 256, (h * 5 + 4) * 6

        def part(q, half):
            return gt.at[rows(off + q * step + half * 32, 32), :]

        def send(q, half, i, dev):
            ref = part(q, half)
            go(ref, ref, ag_s.at[sem + i], ag_r.at[sem + i], dev)

        def get(q, half, i):
            got(part(q, half), ag_s.at[sem + i], ag_r.at[sem + i])

        def first():
            send(p, 0, 0, right)
            send(p, 1, 3, left)
            send(p, 1, 1, right)
            send(p, 0, 4, left)

        def second():
            get(q4(p + 3), 0, 0)
            send(q4(p + 3), 0, 2, right)
            get(q4(p + 1), 1, 3)
            send(q4(p + 1), 1, 5, left)

        def third():
            get(q4(p + 3), 1, 1)
            get(q4(p + 1), 0, 4)

        def last():
            get(q4(p + 2), 0, 2)
            get(q4(p + 2), 1, 5)

        return first, second, third, last

    ag2 = [gather(h, 1, 0) for h in range(2)]
    ag1 = [[gather(h, 0, b) for b in range(4)] for h in range(2)]
    fsum = jnp.zeros((128, E), f32)
    for h in range(2):
        a, b = s2[h][3]()
        start = 1024 * h + pos[h] * 256 + pos[1 - h] * 64
        gt[rows(start, 32), :] = a
        gt[rows(start + 32, 32), :] = b
        ag2[h][0]()
        ag1[h][0][0]()
        fsum = fsum + dot_tn(remt[rows(start, 32), :], a)
        fsum = fsum + dot_tn(remt[rows(start + 32, 32), :], b)
    far[...] = fsum[0:8].astype(bf16)

    def send_far(d):
        @pl.when(c >= d)
        def _():
            rc(far, fars.at[up8(c), :], far_s.at[d], far_r.at[d], at_c(CLS - d)).start()

    peers(send_far)

    for h in range(2):
        ag2[h][1]()
    for h in range(2):
        ag1[h][0][1]()

    for d in range(1, 4):
        got(ppx.at[d], px_s.at[d], px_r.at[d])
        got(ltx.at[d], lx_s.at[d], lx_r.at[d])
    ppxs[...] = (
        ppb[...].astype(f32) + ppx[1].astype(f32) + ppx[2].astype(f32) + ppx[3].astype(f32)
    ).astype(bf16)
    ltxs[...] = lt[...] + ltx[1] + ltx[2] + ltx[3]
    for d in range(1, 4):
        go(ppxs, ppy.at[d], py_s.at[d], py_r.at[d], at_y(d))
        go(ltxs, lty.at[d], ly_s.at[d], ly_r.at[d], at_y(d))

    for h in range(2):
        ag2[h][2]()
        ag1[h][3][0]()
        ag1[h][1][0]()
    for h in range(2):
        ag2[h][3]()
        ag1[h][2][0]()

    def wait_far(d, _):
        @pl.when(c + d < CLS)
        def _():
            got(idss.at[up8(c + d), :], ids_s.at[d], ids_r.at[d])
            got(fars.at[up8(c + d), :], far_s.at[d], far_r.at[d])
        return 0

    lax.fori_loop(1, CLS, wait_far, 0)
    ri = lax.broadcasted_iota(i32, (128, 128), 0)
    ci = lax.broadcasted_iota(i32, (128, 128), 1)
    idrow = jnp.max(jnp.where(ri == ci, idss[...], -1), axis=0, keepdims=True)
    match = (last == idrow) & (last >= 0)
    fx[...] = dot(jnp.where(match, 1.0, 0.0).astype(bf16), fars[...])[0:8]
    for d in range(1, 4):
        go(fx, fxr.at[d], fx_s.at[d], fx_r.at[d], at_x(d))

    for d in range(1, NZ):
        got(ug.at[rows((k * 8 + q8(z + NZ - d)) * 32, 32), :], ug_s.at[d], ug_r.at[d])
    go(ug.at[mine, :], ug.at[mine, :], uc_s.at[1], uc_r.at[1], mate)

    for d in range(1, 4):
        got(ppy.at[d], py_s.at[d], py_r.at[d])
        got(lty.at[d], ly_s.at[d], ly_r.at[d])
    pa[slot, :] = (
        ppxs[...].astype(f32) + ppy[1].astype(f32) + ppy[2].astype(f32) + ppy[3].astype(f32)
    ).astype(bf16)
    for d in range(1, NZ):
        go(pa.at[slot, :], pa.at[slot, :], pz_s.at[d], pz_r.at[d], at_z(d))
    total = ltxs[...] + lty[1] + lty[2] + lty[3]
    lossb[...] = total * (1.0 / BATCH)

    for b in (3, 1):
        for h in range(2):
            ag1[h][b][1]()
    for d in range(1, 4):
        got(fxr.at[d], fx_s.at[d], fx_r.at[d])
    fy[...] = fx[...] + fxr[1] + fxr[2] + fxr[3]
    for d in range(1, 4):
        go(fy, fyr.at[d], fy_s.at[d], fy_r.at[d], at_y(d))
    for h in range(2):
        ag1[h][2][1]()

    got(ug.at[other, :], uc_s.at[1], uc_r.at[1])

    for d in range(1, NZ):
        got(pa.at[rows((k * 8 + q8(z + NZ - d)) * 32, 32), :], pz_s.at[d], pz_r.at[d])
    go(pa.at[mine, :], pa.at[mine, :], uc_s.at[2], uc_r.at[2], mate)

    for d in range(1, 4):
        got(fyr.at[d], fy_s.at[d], fy_r.at[d])
    near_rows[...] = fy[...] + fyr[1] + fyr[2] + fyr[3]
    for b in (0, 3, 1, 2):
        for h in range(2):
            ag1[h][b][2]()
            ag1[h][b][3]()
    got(pa.at[other, :], uc_s.at[2], uc_r.at[2])

    for cp in started:
        cp.wait_send()

    def drain(d, _):
        rc(stat, stat, st_s.at[d], st_r.at[d], mate).wait_send()
        rc(labt, labt, lab_s.at[d], lab_r.at[d], mate).wait_send()

        @pl.when(c + d < CLS)
        def _():
            rc(pub, pub, pub_s.at[d], pub_r.at[d], mate).wait_send()

        @pl.when(c >= d)
        def _():
            rc(ids, ids, ids_s.at[d], ids_r.at[d], mate).wait_send()
            rc(far, far, far_s.at[d], far_r.at[d], mate).wait_send()

        return 0

    lax.fori_loop(1, CLS, drain, 0)


def finish(lossb, ug, gt, cnt, pa, near_rows, sels, proj, loss_o, gi_o, gt_o, gn_o, gp_o, gib, gnb, gpb, sem):
    outs = [pltpu.make_async_copy(gt, gt_o, sem.at[0])]
    outs[-1].start()
    gpb[...] = pa[...].astype(f32)
    outs.append(pltpu.make_async_copy(gpb, gp_o, sem.at[1]))
    outs[-1].start()
    own = near_rows[...]
    own = jnp.concatenate([own, jnp.zeros_like(own)], axis=0)
    hi = own.astype(bf16)
    lo = (own - hi.astype(f32)).astype(bf16)
    sel = sels[...]
    for i in range(2):
        r = slice(i * 256, i * 256 + 256)
        at = sel[:, r]
        gnb[r, :] = dot(cnt[r, :], gt[...]) + dot_tn(at, hi) + dot_tn(at, lo)
        outs.append(pltpu.make_async_copy(gnb.at[r, :], gn_o.at[r, :], sem.at[2 + i]))
        outs[-1].start()
    gib[...] = (scale * dot_tn(ug[...], proj[...])).astype(bf16)
    outs.append(pltpu.make_async_copy(gib, gi_o, sem.at[4]))
    outs[-1].start()
    loss_o[...] = lossb[0:1, 0:1]
    for cp in outs:
        cp.wait()


def q8(v):
    return lax.rem(v, NZ)


def per_device(images, labels, taxon_emb, node_emb, proj, lineage):
    dma = pltpu.SemaphoreType.DMA
    vm = pltpu.VMEM
    scratch = [
        vm((LEVELS, T), i32), vm((1, B), i32),
        vm((B, E), bf16), vm((T, E), bf16), vm((N, E), bf16), vm((E, E), bf16),
        vm((16, T), i32), vm((T, E), f32), vm((T, E), bf16),
        vm((T, B), f32), vm((T, 2 * B), bf16), vm((B, E), bf16), vm((E, 2 * B), f32), vm((T, 128), bf16),
        vm((8, E), bf16), vm((CLS * 8, E), bf16), vm((8, 128), i32), vm((CLS * 8, 128), i32),
        vm((8, 128), f32), vm((CLS, 8, 128), f32), vm((8, 128), f32), vm((CLS, 8, 128), f32),
        vm((8, E), bf16), vm((CLS * 8, E), bf16), vm((1, B), f32),
        vm((E, B), bf16), vm((256, B), bf16), vm((256, B), bf16), vm((NZ, 32, B), bf16),
        vm((32, E), bf16), vm((4, 32, E), bf16), vm((32, E), bf16),
        vm((4, 32, E), bf16), vm((8, 128), f32), vm((4, 8, 128), f32),
        vm((8, 128), f32), vm((4, 8, 128), f32),
        vm((8, E), f32), vm((4, 8, E), f32), vm((8, E), f32), vm((4, 8, E), f32),
        vm((T, E), bf16), vm((2, 6, 128, E), bf16), vm((2, 2, 128, E), bf16),
        vm((2, 256, E), bf16), vm((2, 6, 32, E), bf16), vm((2, 2, 32, E), bf16),
        dma((6,)),
    ]
    scratch += [dma((CLS,))] * 10
    scratch += [dma((24,))] * 2 + [dma((60,))] * 2
    scratch += [dma((3,))] * 2 + [dma((NZ,))] * 4
    scratch += [dma((4,))] * 4 + [dma((NZ,))] * 2 + [dma((4,))] * 4
    scratch += [dma((4,))] * 4
    hbm = pl.BlockSpec(memory_space=pltpu.HBM)
    vmem = pl.BlockSpec(memory_space=pltpu.VMEM)
    args = (lineage.T, labels.reshape(1, B), images, taxon_emb, node_emb, proj)
    held = pl.pallas_call(
        body,
        out_shape=(
            vm((8, 128), f32), vm((E, B), bf16), vm((T, E), bf16), vm((N, T), bf16),
            vm((E, E), bf16), vm((8, E), f32), vm((16, N), bf16), vm((E, E), bf16),
        ),
        in_specs=[hbm] * 6,
        out_specs=[vmem] * 8,
        scratch_shapes=scratch,
        compiler_params=pltpu.CompilerParams(
            collective_id=0, has_side_effects=True, vmem_limit_bytes=46 * 1024 * 1024
        ),
    )(*[pltpu.with_memory_space_constraint(a, pltpu.HBM) for a in args])
    loss, gi, gt, gn, gp = pl.pallas_call(
        finish,
        out_shape=(
            jax.ShapeDtypeStruct((1, 1), f32),
            jax.ShapeDtypeStruct((B, E), bf16),
            jax.ShapeDtypeStruct((T, E), bf16),
            jax.ShapeDtypeStruct((N, E), f32),
            jax.ShapeDtypeStruct((E, E), f32),
        ),
        in_specs=[vmem] * 8,
        out_specs=[vmem] + [hbm] * 4,
        scratch_shapes=[vm((B, E), bf16), vm((N, E), f32), vm((E, E), f32), dma((5,))],
        compiler_params=pltpu.CompilerParams(vmem_limit_bytes=12 * 1024 * 1024),
    )(*held)
    return (loss.reshape(()), gi, gt, gn, gp)


def solution(mesh):
    in_specs = (P("grp", None), P("grp"), P("cls", None), P("cls", None), P(), P("cls", None))
    out_specs = (P(), P("grp", None), P("cls", None), P("cls", None), P())
    return jax.shard_map(
        per_device, mesh=mesh, in_specs=in_specs, out_specs=out_specs, check_vma=False
    )
```

```python
import jax
import jax.numpy as jnp
from jax import lax
from jax.experimental import pallas as pl
from jax.experimental.pallas import tpu as pltpu
from jax.sharding import PartitionSpec as P

MESH = pl.DeviceIdType.MESH
f32, bf16, i32 = jnp.float32, jnp.bfloat16, jnp.int32
scale = 0.1
E, LEVELS, T, B, N = 512, 7, 2048, 512, 512
NX, NY, NZ, NC = 4, 4, 8, 2
CLS = NZ * NC
GRP = NX * NY
BATCH = B * GRP
NT = (((1,), (1,)), ((), ()))
TN = (((0,), (0,)), ((), ()))


def dot(a, b):
    return jnp.dot(a, b, preferred_element_type=f32)


def dot_nt(a, b):
    return lax.dot_general(a, b, NT, preferred_element_type=f32)


def dot_tn(a, b):
    return lax.dot_general(a, b, TN, preferred_element_type=f32)


def rows(start, size):
    return pl.ds(pl.multiple_of(start, size), size)


def body(
    lin_h, lab_h, img_h, tax_h, node_h, proj_h,
    lossb, ug, gt, cnt, pa, near_rows, sels, projo,
    lin_ref, lab_ref, ia, tax, node, proj, lin16, base32, summed, sc32, pb, acc, remt, sall, cga, glt, gl, gst, gs,
    pub, pubs, ids, idss, stat, stats, labt, labs, far, fars, frow,
    us, ucr, uh, uzr, ppb, ppx, ppxs, ppy, lt, ltx, ltxs, lty,
    fx, fxr, fy, fyr,
    in_sem,
    pub_s, pub_r, ids_s, ids_r, st_s, st_r, lab_s, lab_r, far_s, far_r,
    ia_s, ia_r, im_s, im_r, gl_s, gl_r, gs_s, gs_r, ag_s, ag_r, uc_s, uc_r, uz_s, uz_r, ug_s, ug_r,
    px_s, px_r, py_s, py_r, pz_s, pz_r, lx_s, lx_r, ly_s, ly_r,
    fx_s, fx_r, fy_s, fy_r,
):
    g = lax.axis_index("grp")
    c = lax.axis_index("cls")
    x, y = g // NY, lax.rem(g, NY)
    z, k = c // NC, lax.rem(c, NC)
    pos = (x, y)

    def at_x(d):
        return (lax.rem(x + d, NX) * NY + y, c)

    def at_y(d):
        return (x * NY + lax.rem(y + d, NY), c)

    def at_g(d):
        return (lax.rem(g + d, GRP), c)

    def at_z(d):
        return (g, lax.rem(z + d, NZ) * NC + k)

    def at_c(d):
        return (g, lax.rem(c + d, CLS))

    mate = (g, z * NC + (1 - k))
    near = (at_x, at_y)
    started = []

    def rc(src, dst, ss, rs, dev):
        return pltpu.make_async_remote_copy(
            src_ref=src, dst_ref=dst, send_sem=ss, recv_sem=rs, device_id=dev, device_id_type=MESH
        )

    def go(src, dst, ss, rs, dev):
        cp = rc(src, dst, ss, rs, dev)
        cp.start()
        started.append(cp)
        return cp

    def got(dst, ss, rs):
        rc(dst, dst, ss, rs, mate).wait_recv()

    def far_first(i):
        return 8 + (1 - 2 * lax.rem(i, 2)) * ((i + 1) // 2)

    def peers(f):
        def step(i, _):
            f(far_first(i))
            return 0

        lax.fori_loop(0, CLS - 1, step, 0)

    img = ia.at[x, y]

    loads = [
        pltpu.make_async_copy(s, d, in_sem.at[i])
        for i, (s, d) in enumerate(((lin_h, lin_ref), (node_h, node), (img_h, img), (proj_h, proj), (tax_h, tax), (lab_h, lab_ref)))
    ]
    for cp in loads:
        cp.start()
    pubs[...] = jnp.zeros_like(pubs)
    fars[...] = jnp.zeros_like(fars)
    idss[...] = jnp.full_like(idss, -1)

    barrier = pltpu.get_barrier_semaphore()

    def greet(d, _):
        pl.semaphore_signal(barrier, inc=1, device_id=at_c(d), device_id_type=MESH)
        return 0

    lax.fori_loop(1, CLS, greet, 0)

    def greet_grp(d, _):
        pl.semaphore_signal(barrier, inc=1, device_id=at_g(d), device_id_type=MESH)
        return 0

    lax.fori_loop(1, GRP, greet_grp, 0)

    base = c * N
    tbase = c * T
    lin16[...] = jnp.full_like(lin16, -1)
    loads[0].wait()
    lin16[0:LEVELS, :] = lin_ref[...]
    lin = lin16[...]
    remote = (lin >= 0) & (lin < base)
    pid = jnp.max(jnp.where(remote, lin, -1), axis=1, keepdims=True)
    rem16 = jnp.where(remote, 1.0, 0.0).astype(bf16)
    lane_n = lax.broadcasted_iota(i32, (16, N), 1)
    last = lin16[:, T - 128 : T][:, 127:128]
    loads[1].wait()
    sel = jnp.where(last - base == lane_n, 1.0, 0.0).astype(bf16)
    sels[...] = sel
    pub[...] = dot(sel, node[...])[0:8].astype(bf16)
    ids[...] = jnp.broadcast_to(pid[0:8], (8, 128))

    pl.semaphore_wait(barrier, CLS - 1 + GRP - 1)

    def up8(r):
        return rows(r * 8, 8)

    def send_pub(d):
        @pl.when(c + d < CLS)
        def _():
            rc(pub, pubs.at[up8(c), :], pub_s.at[d], pub_r.at[d], at_c(d)).start()

    peers(send_pub)

    def q4(v):
        return lax.rem(v, 4)

    def images(h, blk):
        axis = h if blk is None else 1 - h
        p = pos[axis]
        right, left = near[axis](1), near[axis](3)
        sem = (h * 5 + (4 if blk is None else blk)) * 6

        def part(q, half):
            a, b = (q, pos[1 - h]) if blk is None else (q4(pos[h] + blk), q)
            i, j = (a, b) if h == 0 else (b, a)
            return ia.at[i, j, rows(k * 256 + h * 128 + half * 64, 64), :]

        def send(q, half, i, dev):
            ref = part(q, half)
            go(ref, ref, ia_s.at[sem + i], ia_r.at[sem + i], dev)

        def get(q, half, i):
            got(part(q, half), ia_s.at[sem + i], ia_r.at[sem + i])

        return ring(p, right, left, send, get)

    def ring(p, right, left, send, get):
        def first():
            send(p, 0, 0, right)
            send(p, 1, 3, left)
            send(p, 1, 1, right)
            send(p, 0, 4, left)

        def second():
            get(q4(p + 3), 0, 0)
            send(q4(p + 3), 0, 2, right)
            get(q4(p + 1), 1, 3)
            send(q4(p + 1), 1, 5, left)

        def third():
            get(q4(p + 3), 1, 1)
            get(q4(p + 1), 0, 4)

        def last():
            get(q4(p + 2), 0, 2)
            get(q4(p + 2), 1, 5)

        return first, second, third, last

    def whole(h, blk, core):
        r = rows(core * 256 + h * 128, 128)
        q = q4(pos[h] + blk)
        if blk:
            return [ia.at[q, :, r, :] if h == 0 else ia.at[:, q, r, :]]
        o = pos[1 - h]
        at = [q4(o + d) for d in range(1, 4)]
        return [ia.at[x, v, r, :] if h == 0 else ia.at[v, y, r, :] for v in at]

    def to_mate(h, blk):
        for n, ref in enumerate(whole(h, blk, k)):
            i = h * 6 + (n if blk == 0 else 2 + blk)
            go(ref, ref, im_s.at[i], im_r.at[i], mate)

    def from_mate(h, blk):
        for n, ref in enumerate(whole(h, blk, 1 - k)):
            i = h * 6 + (n if blk == 0 else 2 + blk)
            got(ref, im_s.at[i], im_r.at[i])

    both = range(2)
    ia_a = [images(h, None) for h in both]
    ia_b = [[images(h, b) for b in range(4)] for h in both]
    loads[2].wait()
    for h in both:
        ia_a[h][0]()
    for h in both:
        ia_b[h][0][0]()

    def count_block(i, _):
        nid = lax.broadcasted_iota(i32, (32, T), 0) + (i * 32 + base)
        hit = nid == lin16[0:1, :]
        for l in range(1, LEVELS):
            hit = hit | (nid == lin16[l : l + 1, :])
        cnt[rows(i * 32, 32), :] = jnp.where(hit, 1.0, 0.0).astype(bf16)
        return 0

    lax.fori_loop(0, N // 32, count_block, 0, unroll=2)
    eye = lax.broadcasted_iota(i32, (16, 128), 0) == lax.broadcasted_iota(i32, (16, 128), 1)
    remt[...] = dot_tn(rem16, jnp.where(eye, 1.0, 0.0).astype(bf16)).astype(bf16)
    for cp in loads[3:]:
        cp.wait()
    projo[...] = proj[...]
    for q in range(4):
        glt[q : q + 1, :] = lab_ref[:, q * 128 : q * 128 + 128]
    gl[g] = glt[...]

    def send_gl(d):
        rc(glt, gl.at[g], gl_s.at[d], gl_r.at[d], at_g(d)).start()

    def local_sum(i, _):
        r = rows(i * 256, 256)
        base32[r, :] = tax[r, :].astype(f32) + dot_tn(cnt[:, r], node[...])
        return 0

    lax.fori_loop(0, T // 256, local_sum, 0, unroll=2)

    for h in both:
        ia_a[h][1]()
    for h in both:
        ia_b[h][0][1]()
    for h in both:
        ia_a[h][2]()
        ia_b[h][3][0]()
        ia_b[h][1][0]()
    peers(send_gl)

    def wait_pub(d, _):
        @pl.when(c >= d)
        def _():
            got(pubs.at[up8(c - d), :], pub_s.at[d], pub_r.at[d])
        return 0

    lax.fori_loop(1, CLS, wait_pub, 0)
    lane = lax.broadcasted_iota(i32, (128, 128), 1)
    pid128 = jnp.concatenate([pid, jnp.full((112, 1), -1, i32)], axis=0)
    want = (pid128 >> 9) * 8 + lax.broadcasted_iota(i32, (128, 1), 0)
    pick = jnp.where((want == lane) & (pid128 >= 0), 1.0, 0.0).astype(bf16)
    prefix = dot(pick, pubs[...]).astype(bf16)

    def score_block(i, top):
        r = rows(i * 256, 256)
        s = (base32[r, :] + dot(remt[r, :], prefix)).astype(bf16)
        summed[r, :] = s
        pr = dot(s, proj[...]).astype(bf16)
        st = scale * dot_nt(pr, img[...])
        sc32[r, :] = st
        return jnp.maximum(top, jnp.max(st.reshape(32, 8, B), axis=0))

    top8 = lax.fori_loop(0, T // 256, score_block, jnp.full((8, B), -jnp.inf, f32), unroll=2)
    mtop = jnp.max(top8, axis=0, keepdims=True)
    label = lab_ref[...] - tbase

    def exp_block(i, carry):
        tot, ls = carry
        r = rows(i * 256, 256)
        st = sc32[r, :]
        hit = lax.broadcasted_iota(i32, (256, B), 0) + i * 256 == label
        p = jnp.exp(st - mtop)
        ls = ls + jnp.sum(jnp.where(hit, st, 0.0).reshape(32, 8, B), axis=0)
        tot = tot + jnp.sum(p.reshape(32, 8, B), axis=0)
        sc32[r, :] = p
        pb[r, 0:B] = p.astype(bf16)
        pb[r, B : 2 * B] = jnp.where(hit, 1.0, 0.0).astype(bf16)
        return tot, ls

    zero8 = jnp.zeros((8, B), f32)
    tot8, ls8 = lax.fori_loop(0, T // 256, exp_block, (zero8, zero8))
    tot = jnp.sum(tot8, axis=0, keepdims=True)
    for q in range(4):
        stat[q : q + 1, :] = mtop[:, q * 128 : q * 128 + 128]
        stat[q + 4 : q + 5, :] = tot[:, q * 128 : q * 128 + 128]
    lsum = ls8[:, 0:128] + ls8[:, 128:256] + ls8[:, 256:384] + ls8[:, 384:512]
    labt[...] = jnp.broadcast_to(jnp.sum(lsum, keepdims=True), (8, 128))

    def send_stat(d):
        rc(stat, stats.at[c], st_s.at[d], st_r.at[d], at_c(d)).start()

    def send_lab(d):
        rc(labt, labs.at[c], lab_s.at[d], lab_r.at[d], at_c(d)).start()

    def send_ids(d):
        @pl.when(c >= d)
        def _():
            rc(ids, idss.at[up8(c), :], ids_s.at[d], ids_r.at[d], at_c(CLS - d)).start()

    peers(send_stat)
    stats[c] = stat[...]
    labs[c] = labt[...]

    for h in both:
        ia_a[h][3]()
        ia_b[h][2][0]()
    for b in (3, 1):
        for h in both:
            ia_b[h][b][1]()
    for h in both:
        ia_b[h][0][2]()
        ia_b[h][0][3]()
        to_mate(h, 0)

    acc[...] = jnp.zeros_like(acc)

    def u_block(i, _):
        r = rows(i * 512, 512)
        acc[...] += dot_tn(summed[r, :], pb[r, :])
        return 0

    lax.fori_loop(0, T // 512, u_block, 0)

    for h in both:
        ia_b[h][2][1]()
    for b in (3, 1):
        for h in both:
            ia_b[h][b][2]()
            ia_b[h][b][3]()
            to_mate(h, b)

    def wait_stat(d, _):
        got(stats.at[lax.rem(c + CLS - d, CLS)], st_s.at[d], st_r.at[d])
        return 0

    lax.fori_loop(1, CLS, wait_stat, 0)
    all_m = stats[:, 0:4, :]
    gtop = jnp.max(all_m, axis=0)
    gtot = jnp.sum(stats[:, 4:8, :] * jnp.exp(all_m - gtop[None]), axis=0)
    fac = jnp.exp(stat[0:4, :] - gtop) / gtot
    for q in range(4):
        frow[:, q * 128 : q * 128 + 128] = fac[q : q + 1, :]
    fr = frow[...]
    ls_here = jnp.sum(gtop + jnp.log(gtot), keepdims=True)
    gst[0:4, :] = gtop
    gst[4:8, :] = 1.0 / gtot
    gs[g] = gst[...]

    def send_gs(d):
        rc(gst, gs.at[g], gs_s.at[d], gs_r.at[d], at_g(d)).start()

    peers(send_gs)
    us[...] = (acc[:, 0:B] * fr - acc[:, B : 2 * B]).astype(bf16)
    other = rows((1 - k) * 256, 256)
    mine = rows(k * 256, 256)
    uc = go(us.at[other, :], ucr, uc_s.at[0], uc_r.at[0], mate)

    peers(send_ids)
    peers(send_lab)

    for h in both:
        ia_b[h][2][2]()
        ia_b[h][2][3]()
        to_mate(h, 2)

    got(ucr, uc_s.at[0], uc_r.at[0])
    uh[...] = (us[mine, :].astype(f32) + ucr[...].astype(f32)).astype(bf16)
    for d in range(1, NZ):
        go(uh.at[rows(q8(z + d) * 32, 32), :], uzr.at[z], uz_s.at[d], uz_r.at[d], at_z(d))
    uzr[z] = uh[rows(z * 32, 32), :]

    for d in range(1, NZ):
        got(uzr.at[q8(z + NZ - d)], uz_s.at[d], uz_r.at[d])
    uslice = uzr[0].astype(f32)
    for d in range(1, NZ):
        uslice = uslice + uzr[d].astype(f32)
    uslice = uslice.astype(bf16)
    slot = rows((k * 8 + z) * 32, 32)
    ug[slot, :] = uslice
    for d in range(1, NZ):
        go(ug.at[slot, :], ug.at[slot, :], ug_s.at[d], ug_r.at[d], at_z(d))
    ppb[...] = (scale * dot(uslice, img[...])).astype(bf16)
    for d in range(1, 4):
        go(ppb, ppx.at[d], px_s.at[d], px_r.at[d], at_x(d))

    def wait_lab(d, _):
        got(labs.at[lax.rem(c + CLS - d, CLS)], lab_s.at[d], lab_r.at[d])
        return 0

    lax.fori_loop(1, CLS, wait_lab, 0)
    lt[...] = ls_here - jnp.sum(labs[...], axis=0)
    for d in range(1, 4):
        go(lt, ltx.at[d], lx_s.at[d], lx_r.at[d], at_x(d))

    starts = [1024 * h + pos[h] * 256 + pos[1 - h] * 64 for h in both]
    own = jnp.concatenate([summed[rows(starts[h], 64), :] for h in both], axis=0)
    pr_own = dot(own, proj[...]).astype(bf16)
    for b in (0, 3, 1, 2):
        for h in both:
            from_mate(h, b)

    def own_scores(j, _):
        sall[j] = scale * dot_nt(pr_own, ia[j // NY, lax.rem(j, NY)])
        return 0

    lax.fori_loop(0, GRP, own_scores, 0, unroll=2)

    def wait_gs(d, _):
        o = lax.rem(g + GRP - d, GRP)
        got(gl.at[o], gl_s.at[d], gl_r.at[d])
        got(gs.at[o], gs_s.at[d], gs_r.at[d])
        return 0

    lax.fori_loop(1, GRP, wait_gs, 0)
    ti = lax.broadcasted_iota(i32, (128, 1), 0)
    tid = ti + tbase + jnp.where(ti < 64, starts[0], starts[1] - 64)

    def flat(t, r0):
        return jnp.concatenate([t[r0 + q : r0 + q + 1, :] for q in range(4)], axis=1)

    cga[...] = jnp.zeros_like(cga)

    def own_grads(j, _):
        t = gs[j]
        hit = jnp.where(tid == flat(gl[j], 0), 1.0, 0.0)
        w = jnp.exp(sall[j] - flat(t, 0)) * flat(t, 4) - hit
        cga[...] += dot(w.astype(bf16), ia[j // NY, lax.rem(j, NY)])
        return 0

    lax.fori_loop(0, GRP, own_grads, 0, unroll=2)
    class_grad = (scale * cga[...]).astype(bf16)
    gown = dot_nt(class_grad, proj[...]).astype(bf16)

    def gather(h, s, blk):
        axis = (h + s) % 2
        p = pos[axis]
        right, left = near[axis](1), near[axis](3)
        if s == 0:
            step, off, sem = 256, 1024 * h + q4(pos[1 - h] + blk) * 64, (h * 5 + blk) * 6
        else:
            step, off, sem = 64, 1024 * h + pos[h] * 256, (h * 5 + 4) * 6

        def part(q, half):
            return gt.at[rows(off + q * step + half * 32, 32), :]

        def send(q, half, i, dev):
            ref = part(q, half)
            go(ref, ref, ag_s.at[sem + i], ag_r.at[sem + i], dev)

        def get(q, half, i):
            got(part(q, half), ag_s.at[sem + i], ag_r.at[sem + i])

        return ring(p, right, left, send, get)

    ag2 = [gather(h, 1, 0) for h in range(2)]
    ag1 = [[gather(h, 0, b) for b in range(4)] for h in range(2)]
    fsum = jnp.zeros((128, E), f32)
    for h in range(2):
        gt[rows(starts[h], 64), :] = gown[h * 64 : h * 64 + 64]
        ag2[h][0]()
        ag1[h][0][0]()
    for h in range(2):
        fsum = fsum + dot_tn(remt[rows(starts[h], 64), :], gown[h * 64 : h * 64 + 64])
    far[...] = fsum[0:8].astype(bf16)

    def send_far(d):
        @pl.when(c >= d)
        def _():
            rc(far, fars.at[up8(c), :], far_s.at[d], far_r.at[d], at_c(CLS - d)).start()

    peers(send_far)

    for h in range(2):
        ag2[h][1]()
    for h in range(2):
        ag1[h][0][1]()

    for d in range(1, 4):
        got(ppx.at[d], px_s.at[d], px_r.at[d])
        got(ltx.at[d], lx_s.at[d], lx_r.at[d])
    ppxs[...] = (
        ppb[...].astype(f32) + ppx[1].astype(f32) + ppx[2].astype(f32) + ppx[3].astype(f32)
    ).astype(bf16)
    ltxs[...] = lt[...] + ltx[1] + ltx[2] + ltx[3]
    for d in range(1, 4):
        go(ppxs, ppy.at[d], py_s.at[d], py_r.at[d], at_y(d))
        go(ltxs, lty.at[d], ly_s.at[d], ly_r.at[d], at_y(d))

    for h in range(2):
        ag2[h][2]()
        ag1[h][3][0]()
        ag1[h][1][0]()
    for h in range(2):
        ag2[h][3]()
        ag1[h][2][0]()

    def wait_far(d, _):
        @pl.when(c + d < CLS)
        def _():
            got(idss.at[up8(c + d), :], ids_s.at[d], ids_r.at[d])
            got(fars.at[up8(c + d), :], far_s.at[d], far_r.at[d])
        return 0

    lax.fori_loop(1, CLS, wait_far, 0)
    ri = lax.broadcasted_iota(i32, (128, 128), 0)
    ci = lax.broadcasted_iota(i32, (128, 128), 1)
    idrow = jnp.max(jnp.where(ri == ci, idss[...], -1), axis=0, keepdims=True)
    match = (last == idrow) & (last >= 0)
    fx[...] = dot(jnp.where(match, 1.0, 0.0).astype(bf16), fars[...])[0:8]
    for d in range(1, 4):
        go(fx, fxr.at[d], fx_s.at[d], fx_r.at[d], at_x(d))

    for d in range(1, NZ):
        got(ug.at[rows((k * 8 + q8(z + NZ - d)) * 32, 32), :], ug_s.at[d], ug_r.at[d])
    go(ug.at[mine, :], ug.at[mine, :], uc_s.at[1], uc_r.at[1], mate)

    for d in range(1, 4):
        got(ppy.at[d], py_s.at[d], py_r.at[d])
        got(lty.at[d], ly_s.at[d], ly_r.at[d])
    pa[slot, :] = (
        ppxs[...].astype(f32) + ppy[1].astype(f32) + ppy[2].astype(f32) + ppy[3].astype(f32)
    ).astype(bf16)
    for d in range(1, NZ):
        go(pa.at[slot, :], pa.at[slot, :], pz_s.at[d], pz_r.at[d], at_z(d))
    total = ltxs[...] + lty[1] + lty[2] + lty[3]
    lossb[...] = total * (1.0 / BATCH)

    for b in (3, 1):
        for h in range(2):
            ag1[h][b][1]()
    for d in range(1, 4):
        got(fxr.at[d], fx_s.at[d], fx_r.at[d])
    fy[...] = fx[...] + fxr[1] + fxr[2] + fxr[3]
    for d in range(1, 4):
        go(fy, fyr.at[d], fy_s.at[d], fy_r.at[d], at_y(d))
    for h in range(2):
        ag1[h][2][1]()

    got(ug.at[other, :], uc_s.at[1], uc_r.at[1])

    for d in range(1, NZ):
        got(pa.at[rows((k * 8 + q8(z + NZ - d)) * 32, 32), :], pz_s.at[d], pz_r.at[d])
    go(pa.at[mine, :], pa.at[mine, :], uc_s.at[2], uc_r.at[2], mate)

    for d in range(1, 4):
        got(fyr.at[d], fy_s.at[d], fy_r.at[d])
    near_rows[...] = fy[...] + fyr[1] + fyr[2] + fyr[3]
    for b in (0, 3, 1, 2):
        for h in range(2):
            ag1[h][b][2]()
            ag1[h][b][3]()
    got(pa.at[other, :], uc_s.at[2], uc_r.at[2])

    for cp in started:
        cp.wait_send()

    def drain(d, _):
        rc(stat, stat, st_s.at[d], st_r.at[d], mate).wait_send()
        rc(glt, glt, gl_s.at[d], gl_r.at[d], mate).wait_send()
        rc(gst, gst, gs_s.at[d], gs_r.at[d], mate).wait_send()
        rc(labt, labt, lab_s.at[d], lab_r.at[d], mate).wait_send()

        @pl.when(c + d < CLS)
        def _():
            rc(pub, pub, pub_s.at[d], pub_r.at[d], mate).wait_send()

        @pl.when(c >= d)
        def _():
            rc(ids, ids, ids_s.at[d], ids_r.at[d], mate).wait_send()
            rc(far, far, far_s.at[d], far_r.at[d], mate).wait_send()

        return 0

    lax.fori_loop(1, CLS, drain, 0)


def finish(lossb, ug, gt, cnt, pa, near_rows, sels, proj, loss_o, gi_o, gt_o, gn_o, gp_o, gib, gnb, gpb, sem):
    outs = [pltpu.make_async_copy(gt, gt_o, sem.at[0])]
    outs[-1].start()
    gpb[...] = pa[...].astype(f32)
    outs.append(pltpu.make_async_copy(gpb, gp_o, sem.at[1]))
    outs[-1].start()
    own = near_rows[...]
    own = jnp.concatenate([own, jnp.zeros_like(own)], axis=0)
    hi = own.astype(bf16)
    lo = (own - hi.astype(f32)).astype(bf16)
    sel = sels[...]
    for i in range(2):
        r = slice(i * 256, i * 256 + 256)
        at = sel[:, r]
        gnb[r, :] = dot(cnt[r, :], gt[...]) + dot_tn(at, hi) + dot_tn(at, lo)
        outs.append(pltpu.make_async_copy(gnb.at[r, :], gn_o.at[r, :], sem.at[2 + i]))
        outs[-1].start()
    gib[...] = (scale * dot_tn(ug[...], proj[...])).astype(bf16)
    outs.append(pltpu.make_async_copy(gib, gi_o, sem.at[4]))
    outs[-1].start()
    loss_o[...] = lossb[0:1, 0:1]
    for cp in outs:
        cp.wait()


def q8(v):
    return lax.rem(v, NZ)


def per_device(images, labels, taxon_emb, node_emb, proj, lineage):
    dma = pltpu.SemaphoreType.DMA
    vm = pltpu.VMEM
    scratch = [
        vm((LEVELS, T), i32), vm((1, B), i32),
        vm((NX, NY, B, E), bf16), vm((T, E), bf16), vm((N, E), bf16), vm((E, E), bf16),
        vm((16, T), i32), vm((T, E), f32), vm((T, E), bf16),
        vm((T, B), f32), vm((T, 2 * B), bf16), vm((E, 2 * B), f32), vm((T, 128), bf16),
        vm((GRP, 128, B), f32), vm((128, E), f32),
        vm((8, 128), i32), vm((GRP, 8, 128), i32), vm((8, 128), f32), vm((GRP, 8, 128), f32),
        vm((8, E), bf16), vm((CLS * 8, E), bf16), vm((8, 128), i32), vm((CLS * 8, 128), i32),
        vm((8, 128), f32), vm((CLS, 8, 128), f32), vm((8, 128), f32), vm((CLS, 8, 128), f32),
        vm((8, E), bf16), vm((CLS * 8, E), bf16), vm((1, B), f32),
        vm((E, B), bf16), vm((256, B), bf16), vm((256, B), bf16), vm((NZ, 32, B), bf16),
        vm((32, E), bf16), vm((4, 32, E), bf16), vm((32, E), bf16),
        vm((4, 32, E), bf16), vm((8, 128), f32), vm((4, 8, 128), f32),
        vm((8, 128), f32), vm((4, 8, 128), f32),
        vm((8, E), f32), vm((4, 8, E), f32), vm((8, E), f32), vm((4, 8, E), f32),
        dma((6,)),
    ]
    scratch += [dma((CLS,))] * 10
    scratch += [dma((60,))] * 2 + [dma((12,))] * 2 + [dma((GRP,))] * 4 + [dma((60,))] * 2
    scratch += [dma((3,))] * 2 + [dma((NZ,))] * 4
    scratch += [dma((4,))] * 4 + [dma((NZ,))] * 2 + [dma((4,))] * 4
    scratch += [dma((4,))] * 4
    hbm = pl.BlockSpec(memory_space=pltpu.HBM)
    vmem = pl.BlockSpec(memory_space=pltpu.VMEM)
    args = (lineage.T, labels.reshape(1, B), images, taxon_emb, node_emb, proj)
    held = pl.pallas_call(
        body,
        out_shape=(
            vm((8, 128), f32), vm((E, B), bf16), vm((T, E), bf16), vm((N, T), bf16),
            vm((E, E), bf16), vm((8, E), f32), vm((16, N), bf16), vm((E, E), bf16),
        ),
        in_specs=[hbm] * 6,
        out_specs=[vmem] * 8,
        scratch_shapes=scratch,
        compiler_params=pltpu.CompilerParams(
            collective_id=0, has_side_effects=True, vmem_limit_bytes=52 * 1024 * 1024
        ),
    )(*[pltpu.with_memory_space_constraint(a, pltpu.HBM) for a in args])
    loss, gi, gt, gn, gp = pl.pallas_call(
        finish,
        out_shape=(
            jax.ShapeDtypeStruct((1, 1), f32),
            jax.ShapeDtypeStruct((B, E), bf16),
            jax.ShapeDtypeStruct((T, E), bf16),
            jax.ShapeDtypeStruct((N, E), f32),
            jax.ShapeDtypeStruct((E, E), f32),
        ),
        in_specs=[vmem] * 8,
        out_specs=[vmem] + [hbm] * 4,
        scratch_shapes=[vm((B, E), bf16), vm((N, E), f32), vm((E, E), f32), dma((5,))],
        compiler_params=pltpu.CompilerParams(vmem_limit_bytes=12 * 1024 * 1024),
    )(*held)
    return (loss.reshape(()), gi, gt, gn, gp)


def solution(mesh):
    in_specs = (P("grp", None), P("grp"), P("cls", None), P("cls", None), P(), P("cls", None))
    out_specs = (P(), P("grp", None), P("cls", None), P("cls", None), P())
    return jax.shard_map(
        per_device, mesh=mesh, in_specs=in_specs, out_specs=out_specs, check_vma=False
    )
```

```python
import jax
import jax.numpy as jnp
from jax import lax
from jax.experimental import pallas as pl
from jax.experimental.pallas import tpu as pltpu
from jax.sharding import PartitionSpec as P

MESH = pl.DeviceIdType.MESH
f32, bf16, i32 = jnp.float32, jnp.bfloat16, jnp.int32
scale = 0.1
E, LEVELS, T, B, N = 512, 7, 2048, 512, 512
NX, NY, NZ, NC = 4, 4, 8, 2
CLS = NZ * NC
GRP = NX * NY
BATCH = B * GRP
NT = (((1,), (1,)), ((), ()))
TN = (((0,), (0,)), ((), ()))


def dot(a, b):
    return jnp.dot(a, b, preferred_element_type=f32)


def dot_nt(a, b):
    return lax.dot_general(a, b, NT, preferred_element_type=f32)


def dot_tn(a, b):
    return lax.dot_general(a, b, TN, preferred_element_type=f32)


def rows(start, size):
    return pl.ds(pl.multiple_of(start, size), size)


def body(
    lin_h, lab_h, img_h, tax_h, node_h, proj_h,
    lossb, ug, gt, cnt, pa, near_rows, sels, projo,
    lin_ref, lab_ref, ia, tax, node, proj, lin16, base32, summed, sc32, pb, acc, remt, sall, cga, glt, gl, gst, gs,
    pub, pubs, ids, idss, stat, stats, labt, labs, far, fars, frow,
    us, ucr, uh, uzr, ppb, ppx, ppxs, ppy, lt, ltx, ltxs, lty,
    fx, fxr, fy, fyr,
    g2, rb2, tb2,
    in_sem,
    pub_s, pub_r, ids_s, ids_r, st_s, st_r, lab_s, lab_r, far_s, far_r,
    ia_s, ia_r, gl_s, gl_r, gs_s, gs_r, rs_s, rs_r, ag_s, ag_r, uc_s, uc_r, uz_s, uz_r, ug_s, ug_r,
    px_s, px_r, py_s, py_r, pz_s, pz_r, lx_s, lx_r, ly_s, ly_r,
    fx_s, fx_r, fy_s, fy_r,
):
    g = lax.axis_index("grp")
    c = lax.axis_index("cls")
    x, y = g // NY, lax.rem(g, NY)
    z, k = c // NC, lax.rem(c, NC)
    pos = (x, y)

    def at_x(d):
        return (lax.rem(x + d, NX) * NY + y, c)

    def at_y(d):
        return (x * NY + lax.rem(y + d, NY), c)

    def at_z(d):
        return (g, lax.rem(z + d, NZ) * NC + k)

    def at_c(d):
        return (g, lax.rem(c + d, CLS))

    mate = (g, z * NC + (1 - k))
    near = (at_x, at_y)
    started = []

    def rc(src, dst, ss, rs, dev):
        return pltpu.make_async_remote_copy(
            src_ref=src, dst_ref=dst, send_sem=ss, recv_sem=rs, device_id=dev, device_id_type=MESH
        )

    def go(src, dst, ss, rs, dev):
        cp = rc(src, dst, ss, rs, dev)
        cp.start()
        started.append(cp)
        return cp

    def got(dst, ss, rs):
        rc(dst, dst, ss, rs, mate).wait_recv()

    def far_first(i):
        return 8 + (1 - 2 * lax.rem(i, 2)) * ((i + 1) // 2)

    def peers(f):
        def step(i, _):
            f(far_first(i))
            return 0

        lax.fori_loop(0, CLS - 1, step, 0)

    img = ia.at[0, x]

    loads = [
        pltpu.make_async_copy(s, d, in_sem.at[i])
        for i, (s, d) in enumerate(((lin_h, lin_ref), (node_h, node), (img_h, img), (img_h, ia.at[1, y]), (proj_h, proj), (tax_h, tax), (lab_h, lab_ref)))
    ]
    for cp in loads:
        cp.start()
    pubs[...] = jnp.zeros_like(pubs)
    fars[...] = jnp.zeros_like(fars)
    idss[...] = jnp.full_like(idss, -1)

    barrier = pltpu.get_barrier_semaphore()

    def greet(d, _):
        pl.semaphore_signal(barrier, inc=1, device_id=at_c(d), device_id_type=MESH)
        return 0

    lax.fori_loop(1, CLS, greet, 0)
    for d in range(1, NX):
        pl.semaphore_signal(barrier, inc=1, device_id=at_x(d), device_id_type=MESH)
    for d in range(1, NY):
        pl.semaphore_signal(barrier, inc=1, device_id=at_y(d), device_id_type=MESH)

    base = c * N
    tbase = c * T
    lin16[...] = jnp.full_like(lin16, -1)
    loads[0].wait()
    lin16[0:LEVELS, :] = lin_ref[...]
    lin = lin16[...]
    remote = (lin >= 0) & (lin < base)
    pid = jnp.max(jnp.where(remote, lin, -1), axis=1, keepdims=True)
    rem16 = jnp.where(remote, 1.0, 0.0).astype(bf16)
    lane_n = lax.broadcasted_iota(i32, (16, N), 1)
    last = lin16[:, T - 128 : T][:, 127:128]
    loads[1].wait()
    sel = jnp.where(last - base == lane_n, 1.0, 0.0).astype(bf16)
    sels[...] = sel
    pub[...] = dot(sel, node[...])[0:8].astype(bf16)
    ids[...] = jnp.broadcast_to(pid[0:8], (8, 128))

    pl.semaphore_wait(barrier, CLS - 1 + NX - 1 + NY - 1)

    def up8(r):
        return rows(r * 8, 8)

    def send_pub(d):
        @pl.when(c + d < CLS)
        def _():
            rc(pub, pubs.at[up8(c), :], pub_s.at[d], pub_r.at[d], at_c(d)).start()

    peers(send_pub)

    def q4(v):
        return lax.rem(v, 4)

    def ring(p, right, left, send, get):
        def first():
            send(p, 0, 0, right)
            send(p, 1, 3, left)
            send(p, 1, 1, right)
            send(p, 0, 4, left)

        def second():
            get(q4(p + 3), 0, 0)
            send(q4(p + 3), 0, 2, right)
            get(q4(p + 1), 1, 3)
            send(q4(p + 1), 1, 5, left)

        def third():
            get(q4(p + 3), 1, 1)
            get(q4(p + 1), 0, 4)

        def last():
            get(q4(p + 2), 0, 2)
            get(q4(p + 2), 1, 5)

        return first, second, third, last

    def images(h):
        def part(q, half):
            return ia.at[h, q, rows(half * 256, 256), :]

        def send(q, half, i, dev):
            ref = part(q, half)
            go(ref, ref, ia_s.at[h * 6 + i], ia_r.at[h * 6 + i], dev)

        def get(q, half, i):
            got(part(q, half), ia_s.at[h * 6 + i], ia_r.at[h * 6 + i])

        return ring(pos[h], near[h](1), near[h](3), send, get)

    both = range(2)
    lines = [images(h) for h in both]
    for h in both:
        loads[2 + h].wait()
        lines[h][0]()

    def count_block(i, _):
        nid = lax.broadcasted_iota(i32, (32, T), 0) + (i * 32 + base)
        hit = nid == lin16[0:1, :]
        for l in range(1, LEVELS):
            hit = hit | (nid == lin16[l : l + 1, :])
        cnt[rows(i * 32, 32), :] = jnp.where(hit, 1.0, 0.0).astype(bf16)
        return 0

    lax.fori_loop(0, N // 32, count_block, 0, unroll=2)
    eye = lax.broadcasted_iota(i32, (16, 128), 0) == lax.broadcasted_iota(i32, (16, 128), 1)
    remt[...] = dot_tn(rem16, jnp.where(eye, 1.0, 0.0).astype(bf16)).astype(bf16)
    for cp in loads[4:]:
        cp.wait()
    projo[...] = proj[...]
    for q in range(4):
        glt[q : q + 1, :] = lab_ref[:, q * 128 : q * 128 + 128]
    for h in both:
        gl[h, pos[h]] = glt[...]
        for d in range(1, 4):
            go(glt, gl.at[h, pos[h]], gl_s.at[h * 4 + d], gl_r.at[h * 4 + d], near[h](d))

    def local_sum(i, _):
        r = rows(i * 256, 256)
        base32[r, :] = tax[r, :].astype(f32) + dot_tn(cnt[:, r], node[...])
        return 0

    lax.fori_loop(0, T // 256, local_sum, 0, unroll=2)

    for h in both:
        lines[h][1]()

    def wait_pub(d, _):
        @pl.when(c >= d)
        def _():
            got(pubs.at[up8(c - d), :], pub_s.at[d], pub_r.at[d])
        return 0

    lax.fori_loop(1, CLS, wait_pub, 0)
    lane = lax.broadcasted_iota(i32, (128, 128), 1)
    pid128 = jnp.concatenate([pid, jnp.full((112, 1), -1, i32)], axis=0)
    want = (pid128 >> 9) * 8 + lax.broadcasted_iota(i32, (128, 1), 0)
    pick = jnp.where((want == lane) & (pid128 >= 0), 1.0, 0.0).astype(bf16)
    prefix = dot(pick, pubs[...]).astype(bf16)

    def score_block(i, top):
        r = rows(i * 256, 256)
        s = (base32[r, :] + dot(remt[r, :], prefix)).astype(bf16)
        summed[r, :] = s
        pr = dot(s, proj[...]).astype(bf16)
        st = scale * dot_nt(pr, img[...])
        sc32[r, :] = st
        return jnp.maximum(top, jnp.max(st.reshape(32, 8, B), axis=0))

    top8 = lax.fori_loop(0, T // 256, score_block, jnp.full((8, B), -jnp.inf, f32), unroll=2)
    mtop = jnp.max(top8, axis=0, keepdims=True)
    label = lab_ref[...] - tbase

    def exp_block(i, carry):
        tot, ls = carry
        r = rows(i * 256, 256)
        st = sc32[r, :]
        hit = lax.broadcasted_iota(i32, (256, B), 0) + i * 256 == label
        p = jnp.exp(st - mtop)
        ls = ls + jnp.sum(jnp.where(hit, st, 0.0).reshape(32, 8, B), axis=0)
        tot = tot + jnp.sum(p.reshape(32, 8, B), axis=0)
        sc32[r, :] = p
        pb[r, 0:B] = p.astype(bf16)
        pb[r, B : 2 * B] = jnp.where(hit, 1.0, 0.0).astype(bf16)
        return tot, ls

    zero8 = jnp.zeros((8, B), f32)
    tot8, ls8 = lax.fori_loop(0, T // 256, exp_block, (zero8, zero8))
    tot = jnp.sum(tot8, axis=0, keepdims=True)
    for q in range(4):
        stat[q : q + 1, :] = mtop[:, q * 128 : q * 128 + 128]
        stat[q + 4 : q + 5, :] = tot[:, q * 128 : q * 128 + 128]
    lsum = ls8[:, 0:128] + ls8[:, 128:256] + ls8[:, 256:384] + ls8[:, 384:512]
    labt[...] = jnp.broadcast_to(jnp.sum(lsum, keepdims=True), (8, 128))

    def send_stat(d):
        rc(stat, stats.at[c], st_s.at[d], st_r.at[d], at_c(d)).start()

    def send_lab(d):
        rc(labt, labs.at[c], lab_s.at[d], lab_r.at[d], at_c(d)).start()

    def send_ids(d):
        @pl.when(c >= d)
        def _():
            rc(ids, idss.at[up8(c), :], ids_s.at[d], ids_r.at[d], at_c(CLS - d)).start()

    peers(send_stat)
    stats[c] = stat[...]
    labs[c] = labt[...]

    acc[...] = jnp.zeros_like(acc)

    def u_block(i, _):
        r = rows(i * 512, 512)
        acc[...] += dot_tn(summed[r, :], pb[r, :])
        return 0

    lax.fori_loop(0, T // 512, u_block, 0)

    quarter = [1024 * h + pos[h] * 256 for h in both]
    for h in both:
        lines[h][2]()
        lines[h][3]()
        pr = dot(summed[rows(quarter[h], 256), :], proj[...]).astype(bf16)
        for j in range(4):
            sall[h, j] = scale * dot_nt(pr, ia[h, j])

    def wait_stat(d, _):
        got(stats.at[lax.rem(c + CLS - d, CLS)], st_s.at[d], st_r.at[d])
        return 0

    lax.fori_loop(1, CLS, wait_stat, 0)
    all_m = stats[:, 0:4, :]
    gtop = jnp.max(all_m, axis=0)
    gtot = jnp.sum(stats[:, 4:8, :] * jnp.exp(all_m - gtop[None]), axis=0)
    fac = jnp.exp(stat[0:4, :] - gtop) / gtot
    for q in range(4):
        frow[:, q * 128 : q * 128 + 128] = fac[q : q + 1, :]
    fr = frow[...]
    ls_here = jnp.sum(gtop + jnp.log(gtot), keepdims=True)
    gst[0:4, :] = gtop
    gst[4:8, :] = 1.0 / gtot
    for h in both:
        gs[h, pos[h]] = gst[...]
        for d in range(1, 4):
            go(gst, gs.at[h, pos[h]], gs_s.at[h * 4 + d], gs_r.at[h * 4 + d], near[h](d))
    us[...] = (acc[:, 0:B] * fr - acc[:, B : 2 * B]).astype(bf16)
    other = rows((1 - k) * 256, 256)
    mine = rows(k * 256, 256)
    uc = go(us.at[other, :], ucr, uc_s.at[0], uc_r.at[0], mate)

    peers(send_ids)
    peers(send_lab)

    got(ucr, uc_s.at[0], uc_r.at[0])
    uh[...] = (us[mine, :].astype(f32) + ucr[...].astype(f32)).astype(bf16)
    for d in range(1, NZ):
        go(uh.at[rows(q8(z + d) * 32, 32), :], uzr.at[z], uz_s.at[d], uz_r.at[d], at_z(d))
    uzr[z] = uh[rows(z * 32, 32), :]

    for h in both:
        for d in range(1, 4):
            got(gl.at[h, q4(pos[h] + 4 - d)], gl_s.at[h * 4 + d], gl_r.at[h * 4 + d])
            got(gs.at[h, q4(pos[h] + 4 - d)], gs_s.at[h * 4 + d], gs_r.at[h * 4 + d])

    def flat(t, r0):
        return jnp.concatenate([t[r0 + q : r0 + q + 1, :] for q in range(4)], axis=1)

    def stage(h):
        axis = 1 - h
        p = pos[axis]
        n = 32
        right, left = near[axis](1), near[axis](3)
        src = g2.at[h]
        rb = rb2.at[h]
        tb = tb2.at[h]
        sem = h * 6

        def part(q, half):
            return rows(q * (2 * n) + half * n, n)

        def send(ref, i, dev):
            go(ref, rb.at[i], rs_s.at[sem + i], rs_r.at[sem + i], dev)

        def get(i):
            got(rb.at[i], rs_s.at[sem + i], rs_r.at[sem + i])
            return rb[i].astype(f32)

        def own(q, half):
            return src[part(q, half), :].astype(f32)

        def first():
            send(src.at[part(q4(p + 2), 0), :], 0, right)
            send(src.at[part(q4(p + 2), 1), :], 3, left)

        def second():
            send(src.at[part(q4(p + 1), 1), :], 1, right)
            send(src.at[part(q4(p + 3), 0), :], 4, left)

        def third():
            tb[0] = (own(q4(p + 1), 0) + get(0)).astype(bf16)
            send(tb.at[0], 2, right)
            tb[1] = (own(q4(p + 3), 1) + get(3)).astype(bf16)
            send(tb.at[1], 5, left)

        def last():
            a = own(p, 0) + get(4) + get(2)
            b = own(p, 1) + get(1) + get(5)
            return a.astype(bf16), b.astype(bf16)

        return first, second, third, last

    s2 = (stage(0), stage(1))
    for h in both:
        tid = lax.broadcasted_iota(i32, (256, 1), 0) + (tbase + quarter[h])
        for j in range(4):
            t = gs[h, j]
            hit = jnp.where(tid == flat(gl[h, j], 0), 1.0, 0.0)
            w = jnp.exp(sall[h, j] - flat(t, 0)) * flat(t, 4) - hit
            part = dot(w.astype(bf16), ia[h, j])
            cga[...] = part if j == 0 else cga[...] + part
        g2[h] = dot_nt((scale * cga[...]).astype(bf16), proj[...]).astype(bf16)
        s2[h][0]()
        s2[h][1]()
    for h in both:
        s2[h][2]()

    def gather(h, s, blk):
        axis = (h + s) % 2
        p = pos[axis]
        right, left = near[axis](1), near[axis](3)
        if s == 0:
            step, off, sem = 256, 1024 * h + q4(pos[1 - h] + blk) * 64, (h * 5 + blk) * 6
        else:
            step, off, sem = 64, 1024 * h + pos[h] * 256, (h * 5 + 4) * 6

        def part(q, half):
            return gt.at[rows(off + q * step + half * 32, 32), :]

        def send(q, half, i, dev):
            ref = part(q, half)
            go(ref, ref, ag_s.at[sem + i], ag_r.at[sem + i], dev)

        def get(q, half, i):
            got(part(q, half), ag_s.at[sem + i], ag_r.at[sem + i])

        return ring(p, right, left, send, get)

    ag2 = [gather(h, 1, 0) for h in range(2)]
    ag1 = [[gather(h, 0, b) for b in range(4)] for h in range(2)]
    fsum = jnp.zeros((128, E), f32)
    for h in range(2):
        a, b = s2[h][3]()
        start = 1024 * h + pos[h] * 256 + pos[1 - h] * 64
        gt[rows(start, 32), :] = a
        gt[rows(start + 32, 32), :] = b
        ag2[h][0]()
        ag1[h][0][0]()
        fsum = fsum + dot_tn(remt[rows(start, 32), :], a)
        fsum = fsum + dot_tn(remt[rows(start + 32, 32), :], b)
    far[...] = fsum[0:8].astype(bf16)

    def send_far(d):
        @pl.when(c >= d)
        def _():
            rc(far, fars.at[up8(c), :], far_s.at[d], far_r.at[d], at_c(CLS - d)).start()

    peers(send_far)
    for d in range(1, NZ):
        got(uzr.at[q8(z + NZ - d)], uz_s.at[d], uz_r.at[d])
    uslice = uzr[0].astype(f32)
    for d in range(1, NZ):
        uslice = uslice + uzr[d].astype(f32)
    uslice = uslice.astype(bf16)
    slot = rows((k * 8 + z) * 32, 32)
    ug[slot, :] = uslice
    for d in range(1, NZ):
        go(ug.at[slot, :], ug.at[slot, :], ug_s.at[d], ug_r.at[d], at_z(d))
    ppb[...] = (scale * dot(uslice, img[...])).astype(bf16)
    for d in range(1, 4):
        go(ppb, ppx.at[d], px_s.at[d], px_r.at[d], at_x(d))

    def wait_lab(d, _):
        got(labs.at[lax.rem(c + CLS - d, CLS)], lab_s.at[d], lab_r.at[d])
        return 0

    lax.fori_loop(1, CLS, wait_lab, 0)
    lt[...] = ls_here - jnp.sum(labs[...], axis=0)
    for d in range(1, 4):
        go(lt, ltx.at[d], lx_s.at[d], lx_r.at[d], at_x(d))


    for h in range(2):
        ag2[h][1]()
    for h in range(2):
        ag1[h][0][1]()

    for d in range(1, 4):
        got(ppx.at[d], px_s.at[d], px_r.at[d])
        got(ltx.at[d], lx_s.at[d], lx_r.at[d])
    ppxs[...] = (
        ppb[...].astype(f32) + ppx[1].astype(f32) + ppx[2].astype(f32) + ppx[3].astype(f32)
    ).astype(bf16)
    ltxs[...] = lt[...] + ltx[1] + ltx[2] + ltx[3]
    for d in range(1, 4):
        go(ppxs, ppy.at[d], py_s.at[d], py_r.at[d], at_y(d))
        go(ltxs, lty.at[d], ly_s.at[d], ly_r.at[d], at_y(d))

    for h in range(2):
        ag2[h][2]()
        ag1[h][3][0]()
        ag1[h][1][0]()
    for h in range(2):
        ag2[h][3]()
        ag1[h][2][0]()

    def wait_far(d, _):
        @pl.when(c + d < CLS)
        def _():
            got(idss.at[up8(c + d), :], ids_s.at[d], ids_r.at[d])
            got(fars.at[up8(c + d), :], far_s.at[d], far_r.at[d])
        return 0

    lax.fori_loop(1, CLS, wait_far, 0)
    ri = lax.broadcasted_iota(i32, (128, 128), 0)
    ci = lax.broadcasted_iota(i32, (128, 128), 1)
    idrow = jnp.max(jnp.where(ri == ci, idss[...], -1), axis=0, keepdims=True)
    match = (last == idrow) & (last >= 0)
    fx[...] = dot(jnp.where(match, 1.0, 0.0).astype(bf16), fars[...])[0:8]
    for d in range(1, 4):
        go(fx, fxr.at[d], fx_s.at[d], fx_r.at[d], at_x(d))

    for d in range(1, NZ):
        got(ug.at[rows((k * 8 + q8(z + NZ - d)) * 32, 32), :], ug_s.at[d], ug_r.at[d])
    go(ug.at[mine, :], ug.at[mine, :], uc_s.at[1], uc_r.at[1], mate)

    for d in range(1, 4):
        got(ppy.at[d], py_s.at[d], py_r.at[d])
        got(lty.at[d], ly_s.at[d], ly_r.at[d])
    pa[slot, :] = (
        ppxs[...].astype(f32) + ppy[1].astype(f32) + ppy[2].astype(f32) + ppy[3].astype(f32)
    ).astype(bf16)
    for d in range(1, NZ):
        go(pa.at[slot, :], pa.at[slot, :], pz_s.at[d], pz_r.at[d], at_z(d))
    total = ltxs[...] + lty[1] + lty[2] + lty[3]
    lossb[...] = total * (1.0 / BATCH)

    for b in (3, 1):
        for h in range(2):
            ag1[h][b][1]()
    for d in range(1, 4):
        got(fxr.at[d], fx_s.at[d], fx_r.at[d])
    fy[...] = fx[...] + fxr[1] + fxr[2] + fxr[3]
    for d in range(1, 4):
        go(fy, fyr.at[d], fy_s.at[d], fy_r.at[d], at_y(d))
    for h in range(2):
        ag1[h][2][1]()

    got(ug.at[other, :], uc_s.at[1], uc_r.at[1])

    for d in range(1, NZ):
        got(pa.at[rows((k * 8 + q8(z + NZ - d)) * 32, 32), :], pz_s.at[d], pz_r.at[d])
    go(pa.at[mine, :], pa.at[mine, :], uc_s.at[2], uc_r.at[2], mate)

    for d in range(1, 4):
        got(fyr.at[d], fy_s.at[d], fy_r.at[d])
    near_rows[...] = fy[...] + fyr[1] + fyr[2] + fyr[3]
    for b in (0, 3, 1, 2):
        for h in range(2):
            ag1[h][b][2]()
            ag1[h][b][3]()
    got(pa.at[other, :], uc_s.at[2], uc_r.at[2])

    for cp in started:
        cp.wait_send()

    def drain(d, _):
        rc(stat, stat, st_s.at[d], st_r.at[d], mate).wait_send()
        rc(labt, labt, lab_s.at[d], lab_r.at[d], mate).wait_send()

        @pl.when(c + d < CLS)
        def _():
            rc(pub, pub, pub_s.at[d], pub_r.at[d], mate).wait_send()

        @pl.when(c >= d)
        def _():
            rc(ids, ids, ids_s.at[d], ids_r.at[d], mate).wait_send()
            rc(far, far, far_s.at[d], far_r.at[d], mate).wait_send()

        return 0

    lax.fori_loop(1, CLS, drain, 0)


def finish(lossb, ug, gt, cnt, pa, near_rows, sels, proj, loss_o, gi_o, gt_o, gn_o, gp_o, gib, gnb, gpb, sem):
    outs = [pltpu.make_async_copy(gt, gt_o, sem.at[0])]
    outs[-1].start()
    gpb[...] = pa[...].astype(f32)
    outs.append(pltpu.make_async_copy(gpb, gp_o, sem.at[1]))
    outs[-1].start()
    own = near_rows[...]
    own = jnp.concatenate([own, jnp.zeros_like(own)], axis=0)
    hi = own.astype(bf16)
    lo = (own - hi.astype(f32)).astype(bf16)
    sel = sels[...]
    for i in range(2):
        r = slice(i * 256, i * 256 + 256)
        at = sel[:, r]
        gnb[r, :] = dot(cnt[r, :], gt[...]) + dot_tn(at, hi) + dot_tn(at, lo)
        outs.append(pltpu.make_async_copy(gnb.at[r, :], gn_o.at[r, :], sem.at[2 + i]))
        outs[-1].start()
    gib[...] = (scale * dot_tn(ug[...], proj[...])).astype(bf16)
    outs.append(pltpu.make_async_copy(gib, gi_o, sem.at[4]))
    outs[-1].start()
    loss_o[...] = lossb[0:1, 0:1]
    for cp in outs:
        cp.wait()


def q8(v):
    return lax.rem(v, NZ)


def per_device(images, labels, taxon_emb, node_emb, proj, lineage):
    dma = pltpu.SemaphoreType.DMA
    vm = pltpu.VMEM
    scratch = [
        vm((LEVELS, T), i32), vm((1, B), i32),
        vm((2, 4, B, E), bf16), vm((T, E), bf16), vm((N, E), bf16), vm((E, E), bf16),
        vm((16, T), i32), vm((T, E), f32), vm((T, E), bf16),
        vm((T, B), f32), vm((T, 2 * B), bf16), vm((E, 2 * B), f32), vm((T, 128), bf16),
        vm((2, 4, 256, B), f32), vm((256, E), f32),
        vm((8, 128), i32), vm((2, 4, 8, 128), i32), vm((8, 128), f32), vm((2, 4, 8, 128), f32),
        vm((8, E), bf16), vm((CLS * 8, E), bf16), vm((8, 128), i32), vm((CLS * 8, 128), i32),
        vm((8, 128), f32), vm((CLS, 8, 128), f32), vm((8, 128), f32), vm((CLS, 8, 128), f32),
        vm((8, E), bf16), vm((CLS * 8, E), bf16), vm((1, B), f32),
        vm((E, B), bf16), vm((256, B), bf16), vm((256, B), bf16), vm((NZ, 32, B), bf16),
        vm((32, E), bf16), vm((4, 32, E), bf16), vm((32, E), bf16),
        vm((4, 32, E), bf16), vm((8, 128), f32), vm((4, 8, 128), f32),
        vm((8, 128), f32), vm((4, 8, 128), f32),
        vm((8, E), f32), vm((4, 8, E), f32), vm((8, E), f32), vm((4, 8, E), f32),
        vm((2, 256, E), bf16), vm((2, 6, 32, E), bf16), vm((2, 2, 32, E), bf16),
        dma((7,)),
    ]
    scratch += [dma((CLS,))] * 10
    scratch += [dma((12,))] * 2 + [dma((8,))] * 4 + [dma((12,))] * 2 + [dma((60,))] * 2
    scratch += [dma((3,))] * 2 + [dma((NZ,))] * 4
    scratch += [dma((4,))] * 4 + [dma((NZ,))] * 2 + [dma((4,))] * 4
    scratch += [dma((4,))] * 4
    hbm = pl.BlockSpec(memory_space=pltpu.HBM)
    vmem = pl.BlockSpec(memory_space=pltpu.VMEM)
    args = (lineage.T, labels.reshape(1, B), images, taxon_emb, node_emb, proj)
    held = pl.pallas_call(
        body,
        out_shape=(
            vm((8, 128), f32), vm((E, B), bf16), vm((T, E), bf16), vm((N, T), bf16),
            vm((E, E), bf16), vm((8, E), f32), vm((16, N), bf16), vm((E, E), bf16),
        ),
        in_specs=[hbm] * 6,
        out_specs=[vmem] * 8,
        scratch_shapes=scratch,
        compiler_params=pltpu.CompilerParams(
            collective_id=0, has_side_effects=True, vmem_limit_bytes=52 * 1024 * 1024
        ),
    )(*[pltpu.with_memory_space_constraint(a, pltpu.HBM) for a in args])
    loss, gi, gt, gn, gp = pl.pallas_call(
        finish,
        out_shape=(
            jax.ShapeDtypeStruct((1, 1), f32),
            jax.ShapeDtypeStruct((B, E), bf16),
            jax.ShapeDtypeStruct((T, E), bf16),
            jax.ShapeDtypeStruct((N, E), f32),
            jax.ShapeDtypeStruct((E, E), f32),
        ),
        in_specs=[vmem] * 8,
        out_specs=[vmem] + [hbm] * 4,
        scratch_shapes=[vm((B, E), bf16), vm((N, E), f32), vm((E, E), f32), dma((5,))],
        compiler_params=pltpu.CompilerParams(vmem_limit_bytes=12 * 1024 * 1024),
    )(*held)
    return (loss.reshape(()), gi, gt, gn, gp)


def solution(mesh):
    in_specs = (P("grp", None), P("grp"), P("cls", None), P("cls", None), P(), P("cls", None))
    out_specs = (P(), P("grp", None), P("cls", None), P("cls", None), P())
    return jax.shard_map(
        per_device, mesh=mesh, in_specs=in_specs, out_specs=out_specs, check_vma=False
    )
```

```python
import jax
import jax.numpy as jnp
from jax import lax
from jax.experimental import pallas as pl
from jax.experimental.pallas import tpu as pltpu
from jax.sharding import PartitionSpec as P

MESH = pl.DeviceIdType.MESH
f32, bf16, i32 = jnp.float32, jnp.bfloat16, jnp.int32
scale = 0.1
E, LEVELS, T, B, N = 512, 7, 2048, 512, 512
NX, NY, NZ, NC = 4, 4, 8, 2
CLS = NZ * NC
GRP = NX * NY
BATCH = B * GRP
NT = (((1,), (1,)), ((), ()))
TN = (((0,), (0,)), ((), ()))


def dot(a, b):
    return jnp.dot(a, b, preferred_element_type=f32)


def dot_nt(a, b):
    return lax.dot_general(a, b, NT, preferred_element_type=f32)


def dot_tn(a, b):
    return lax.dot_general(a, b, TN, preferred_element_type=f32)


def rows(start, size):
    return pl.ds(pl.multiple_of(start, size), size)


def body(
    lin_h, lab_h, img_h, tax_h, node_h, proj_h,
    lossb, gib, gt, gnb, gpb, cnt,
    lin_ref, lab_ref, ia, tax, node, proj, lin16, base32, summed, sc32, pb, acc, remt, sall, cga, glt, gl, gst, gs,
    pub, pubs, ids, idss, stat, stats, labt, labs, far, fars, frow,
    us, ucr, uh, uzr, ppb, ppx, ppxs, ppy, lt, ltx, ltxs, lty,
    fx, fxr, fy, fyr,
    g2, rb2,
    in_sem, ug, pa, sels,
    pub_s, pub_r, ids_s, ids_r, st_s, st_r, lab_s, lab_r, far_s, far_r,
    ia_s, ia_r, gl_s, gl_r, gs_s, gs_r, rs_s, rs_r, ag_s, ag_r, uc_s, uc_r, uz_s, uz_r, ug_s, ug_r,
    px_s, px_r, py_s, py_r, pz_s, pz_r, lx_s, lx_r, ly_s, ly_r,
    fx_s, fx_r, fy_s, fy_r,
):
    g = lax.axis_index("grp")
    c = lax.axis_index("cls")
    x, y = g // NY, lax.rem(g, NY)
    z, k = c // NC, lax.rem(c, NC)
    pos = (x, y)

    def at_x(d):
        return (lax.rem(x + d, NX) * NY + y, c)

    def at_y(d):
        return (x * NY + lax.rem(y + d, NY), c)

    def at_z(d):
        return (g, lax.rem(z + d, NZ) * NC + k)

    def at_c(d):
        return (g, lax.rem(c + d, CLS))

    mate = (g, z * NC + (1 - k))
    near = (at_x, at_y)
    started = []

    def rc(src, dst, ss, rs, dev):
        return pltpu.make_async_remote_copy(
            src_ref=src, dst_ref=dst, send_sem=ss, recv_sem=rs, device_id=dev, device_id_type=MESH
        )

    def go(src, dst, ss, rs, dev):
        cp = rc(src, dst, ss, rs, dev)
        cp.start()
        started.append(cp)
        return cp

    def got(dst, ss, rs):
        rc(dst, dst, ss, rs, mate).wait_recv()

    def far_first(i):
        return 8 + (1 - 2 * lax.rem(i, 2)) * ((i + 1) // 2)

    def peers(f):
        def step(i, _):
            f(far_first(i))
            return 0

        lax.fori_loop(0, CLS - 1, step, 0)

    img = ia.at[0, x]

    loads = [
        pltpu.make_async_copy(s, d, in_sem.at[i])
        for i, (s, d) in enumerate(((lin_h, lin_ref), (node_h, node), (img_h, img), (img_h, ia.at[1, y]), (proj_h, proj), (tax_h, tax), (lab_h, lab_ref)))
    ]
    for cp in loads:
        cp.start()
    pubs[...] = jnp.zeros_like(pubs)
    fars[...] = jnp.zeros_like(fars)
    idss[...] = jnp.full_like(idss, -1)

    barrier = pltpu.get_barrier_semaphore()

    def greet(d, _):
        pl.semaphore_signal(barrier, inc=1, device_id=at_c(d), device_id_type=MESH)
        return 0

    lax.fori_loop(1, CLS, greet, 0)
    for d in range(1, NX):
        pl.semaphore_signal(barrier, inc=1, device_id=at_x(d), device_id_type=MESH)
    for d in range(1, NY):
        pl.semaphore_signal(barrier, inc=1, device_id=at_y(d), device_id_type=MESH)

    base = c * N
    tbase = c * T
    lin16[...] = jnp.full_like(lin16, -1)
    loads[0].wait()
    lin16[0:LEVELS, :] = lin_ref[...]
    lin = lin16[...]
    remote = (lin >= 0) & (lin < base)
    pid = jnp.max(jnp.where(remote, lin, -1), axis=1, keepdims=True)
    rem16 = jnp.where(remote, 1.0, 0.0).astype(bf16)
    lane_n = lax.broadcasted_iota(i32, (16, N), 1)
    last = lin16[:, T - 128 : T][:, 127:128]
    loads[1].wait()
    sel = jnp.where(last - base == lane_n, 1.0, 0.0).astype(bf16)
    sels[...] = sel
    pub[...] = dot(sel, node[...])[0:8].astype(bf16)
    ids[...] = jnp.broadcast_to(pid[0:8], (8, 128))

    pl.semaphore_wait(barrier, CLS - 1 + NX - 1 + NY - 1)

    def up8(r):
        return rows(r * 8, 8)

    def send_pub(d):
        @pl.when(c + d < CLS)
        def _():
            rc(pub, pubs.at[up8(c), :], pub_s.at[d], pub_r.at[d], at_c(d)).start()

    peers(send_pub)

    def q4(v):
        return lax.rem(v, 4)

    def ring(p, right, left, send, get):
        def first():
            send(p, 0, 0, right)
            send(p, 1, 3, left)
            send(p, 1, 1, right)
            send(p, 0, 4, left)

        def second():
            get(q4(p + 3), 0, 0)
            send(q4(p + 3), 0, 2, right)
            get(q4(p + 1), 1, 3)
            send(q4(p + 1), 1, 5, left)

        def third():
            get(q4(p + 3), 1, 1)
            get(q4(p + 1), 0, 4)

        def last():
            get(q4(p + 2), 0, 2)
            get(q4(p + 2), 1, 5)

        return first, second, third, last

    def images(h):
        def part(q, half):
            return ia.at[h, q, rows(half * 256, 256), :]

        def send(q, half, i, dev):
            ref = part(q, half)
            go(ref, ref, ia_s.at[h * 6 + i], ia_r.at[h * 6 + i], dev)

        def get(q, half, i):
            got(part(q, half), ia_s.at[h * 6 + i], ia_r.at[h * 6 + i])

        return ring(pos[h], near[h](1), near[h](3), send, get)

    both = range(2)
    lines = [images(h) for h in both]
    for h in both:
        loads[2 + h].wait()
        lines[h][0]()

    def count_block(i, _):
        nid = lax.broadcasted_iota(i32, (32, T), 0) + (i * 32 + base)
        hit = nid == lin16[0:1, :]
        for l in range(1, LEVELS):
            hit = hit | (nid == lin16[l : l + 1, :])
        cnt[rows(i * 32, 32), :] = jnp.where(hit, 1.0, 0.0).astype(bf16)
        return 0

    lax.fori_loop(0, N // 32, count_block, 0, unroll=2)
    eye = lax.broadcasted_iota(i32, (16, 128), 0) == lax.broadcasted_iota(i32, (16, 128), 1)
    remt[...] = dot_tn(rem16, jnp.where(eye, 1.0, 0.0).astype(bf16)).astype(bf16)
    for cp in loads[4:]:
        cp.wait()
    for q in range(4):
        glt[q : q + 1, :] = lab_ref[:, q * 128 : q * 128 + 128]
    for h in both:
        gl[h, pos[h]] = glt[...]
        for d in range(1, 4):
            go(glt, gl.at[h, pos[h]], gl_s.at[h * 4 + d], gl_r.at[h * 4 + d], near[h](d))

    def local_sum(i, _):
        r = rows(i * 256, 256)
        base32[r, :] = tax[r, :].astype(f32) + dot_tn(cnt[:, r], node[...])
        return 0

    lax.fori_loop(0, T // 256, local_sum, 0, unroll=2)

    for h in both:
        lines[h][1]()

    def wait_pub(d, _):
        @pl.when(c >= d)
        def _():
            got(pubs.at[up8(c - d), :], pub_s.at[d], pub_r.at[d])
        return 0

    lax.fori_loop(1, CLS, wait_pub, 0)
    lane = lax.broadcasted_iota(i32, (128, 128), 1)
    pid128 = jnp.concatenate([pid, jnp.full((112, 1), -1, i32)], axis=0)
    want = (pid128 >> 9) * 8 + lax.broadcasted_iota(i32, (128, 1), 0)
    pick = jnp.where((want == lane) & (pid128 >= 0), 1.0, 0.0).astype(bf16)
    prefix = dot(pick, pubs[...]).astype(bf16)

    def score_block(i, top):
        r = rows(i * 256, 256)
        s = (base32[r, :] + dot(remt[r, :], prefix)).astype(bf16)
        summed[r, :] = s
        pr = dot(s, proj[...]).astype(bf16)
        st = scale * dot_nt(pr, img[...])
        sc32[r, :] = st
        return jnp.maximum(top, jnp.max(st.reshape(32, 8, B), axis=0))

    top8 = lax.fori_loop(0, T // 256, score_block, jnp.full((8, B), -jnp.inf, f32), unroll=2)
    mtop = jnp.max(top8, axis=0, keepdims=True)
    label = lab_ref[...] - tbase

    def exp_block(i, carry):
        tot, ls = carry
        r = rows(i * 256, 256)
        st = sc32[r, :]
        hit = lax.broadcasted_iota(i32, (256, B), 0) + i * 256 == label
        p = jnp.exp(st - mtop)
        ls = ls + jnp.sum(jnp.where(hit, st, 0.0).reshape(32, 8, B), axis=0)
        tot = tot + jnp.sum(p.reshape(32, 8, B), axis=0)
        sc32[r, :] = p
        pb[r, 0:B] = p.astype(bf16)
        pb[r, B : 2 * B] = jnp.where(hit, 1.0, 0.0).astype(bf16)
        return tot, ls

    zero8 = jnp.zeros((8, B), f32)
    tot8, ls8 = lax.fori_loop(0, T // 256, exp_block, (zero8, zero8))
    tot = jnp.sum(tot8, axis=0, keepdims=True)
    for q in range(4):
        stat[q : q + 1, :] = mtop[:, q * 128 : q * 128 + 128]
        stat[q + 4 : q + 5, :] = tot[:, q * 128 : q * 128 + 128]

    def send_stat(d):
        rc(stat, stats.at[c], st_s.at[d], st_r.at[d], at_c(d)).start()

    def send_lab(d):
        rc(labt, labs.at[c], lab_s.at[d], lab_r.at[d], at_c(d)).start()

    def send_ids(d):
        @pl.when(c >= d)
        def _():
            rc(ids, idss.at[up8(c), :], ids_s.at[d], ids_r.at[d], at_c(CLS - d)).start()

    peers(send_stat)
    lsum = ls8[:, 0:128] + ls8[:, 128:256] + ls8[:, 256:384] + ls8[:, 384:512]
    labt[...] = jnp.broadcast_to(jnp.sum(lsum, keepdims=True), (8, 128))
    stats[c] = stat[...]
    labs[c] = labt[...]

    acc[...] = jnp.zeros_like(acc)

    def u_block(i, _):
        r = rows(i * 512, 512)
        acc[...] += dot_tn(summed[r, :], pb[r, :])
        return 0

    lax.fori_loop(0, T // 512, u_block, 0)

    quarter = [1024 * h + pos[h] * 64 for h in both]

    def line_scores(h):
        lines[h][2]()
        lines[h][3]()
        own = jnp.concatenate([summed[rows(quarter[h] + i * 256, 64), :] for i in range(4)], axis=0)
        pr = dot(own, proj[...]).astype(bf16)
        for j in range(4):
            sall[h, j] = scale * dot_nt(pr, ia[h, j])

    line_scores(0)

    def wait_stat(d, _):
        got(stats.at[lax.rem(c + CLS - d, CLS)], st_s.at[d], st_r.at[d])
        return 0

    lax.fori_loop(1, CLS, wait_stat, 0)
    all_m = stats[:, 0:4, :]
    gtop = jnp.max(all_m, axis=0)
    gtot = jnp.sum(stats[:, 4:8, :] * jnp.exp(all_m - gtop[None]), axis=0)
    fac = jnp.exp(stat[0:4, :] - gtop) / gtot
    for q in range(4):
        frow[:, q * 128 : q * 128 + 128] = fac[q : q + 1, :]
    fr = frow[...]
    ls_here = jnp.sum(gtop + jnp.log(gtot), keepdims=True)
    gst[0:4, :] = gtop
    gst[4:8, :] = 1.0 / gtot
    for h in both:
        gs[h, pos[h]] = gst[...]
        for d in range(1, 4):
            go(gst, gs.at[h, pos[h]], gs_s.at[h * 4 + d], gs_r.at[h * 4 + d], near[h](d))
    us[...] = (acc[:, 0:B] * fr - acc[:, B : 2 * B]).astype(bf16)
    other = rows((1 - k) * 256, 256)
    mine = rows(k * 256, 256)
    uc = go(us.at[other, :], ucr, uc_s.at[0], uc_r.at[0], mate)

    peers(send_ids)
    peers(send_lab)

    got(ucr, uc_s.at[0], uc_r.at[0])
    uh[...] = (us[mine, :].astype(f32) + ucr[...].astype(f32)).astype(bf16)
    for d in range(1, NZ):
        go(uh.at[rows(q8(z + d) * 32, 32), :], uzr.at[z], uz_s.at[d], uz_r.at[d], at_z(d))
    uzr[z] = uh[rows(z * 32, 32), :]

    line_scores(1)
    for h in both:
        for d in range(1, 4):
            got(gl.at[h, q4(pos[h] + 4 - d)], gl_s.at[h * 4 + d], gl_r.at[h * 4 + d])
            got(gs.at[h, q4(pos[h] + 4 - d)], gs_s.at[h * 4 + d], gs_r.at[h * 4 + d])

    def flat(t, r0):
        return jnp.concatenate([t[r0 + q : r0 + q + 1, :] for q in range(4)], axis=1)

    def stage(h):
        axis = 1 - h
        p = pos[axis]

        def first():
            for d in (2, 1, 3):
                go(g2.at[h, rows(q4(p + d) * 64, 64), :], rb2.at[h, d], rs_s.at[h * 4 + d], rs_r.at[h * 4 + d], near[axis](d))

        def last():
            total = g2[h, rows(p * 64, 64), :].astype(f32)
            for d in (1, 3, 2):
                got(rb2.at[h, d], rs_s.at[h * 4 + d], rs_r.at[h * 4 + d])
                total = total + rb2[h, d].astype(f32)
            return total.astype(bf16)

        return first, last

    s2 = (stage(0), stage(1))
    for h in both:
        ri = lax.broadcasted_iota(i32, (256, 1), 0)
        tid = ri + (ri >> 6) * 192 + (tbase + quarter[h])
        for j in range(4):
            t = gs[h, j]
            hit = jnp.where(tid == flat(gl[h, j], 0), 1.0, 0.0)
            w = jnp.exp(sall[h, j] - flat(t, 0)) * flat(t, 4) - hit
            part = dot(w.astype(bf16), ia[h, j])
            cga[...] = part if j == 0 else cga[...] + part
        g2[h] = dot_nt((scale * cga[...]).astype(bf16), proj[...]).astype(bf16)
        s2[h][0]()

    def gather(h, s, blk):
        axis = (h + s) % 2
        p = pos[axis]
        right, left = near[axis](1), near[axis](3)
        if s == 0:
            step, off, sem = 64, 1024 * h + q4(pos[1 - h] + blk) * 256, (h * 5 + blk) * 6
        else:
            step, off, sem = 256, 1024 * h + pos[h] * 64, (h * 5 + 4) * 6

        def part(q, half):
            return gt.at[rows(off + q * step + half * 32, 32), :]

        def send(q, half, i, dev):
            ref = part(q, half)
            go(ref, ref, ag_s.at[sem + i], ag_r.at[sem + i], dev)

        def get(q, half, i):
            got(part(q, half), ag_s.at[sem + i], ag_r.at[sem + i])

        return ring(p, right, left, send, get)

    ag2 = [gather(h, 1, 0) for h in range(2)]
    ag1 = [[gather(h, 0, b) for b in range(4)] for h in range(2)]
    for h in range(2):
        start = 1024 * h + pos[h] * 64 + pos[1 - h] * 256
        gt[rows(start, 64), :] = s2[h][1]()
        ag2[h][0]()
        ag1[h][0][0]()
    for d in range(1, NZ):
        got(uzr.at[q8(z + NZ - d)], uz_s.at[d], uz_r.at[d])
    uslice = uzr[0].astype(f32)
    for d in range(1, NZ):
        uslice = uslice + uzr[d].astype(f32)
    uslice = uslice.astype(bf16)
    slot = rows((k * 8 + z) * 32, 32)
    ug[slot, :] = uslice
    for d in range(1, NZ):
        go(ug.at[slot, :], ug.at[slot, :], ug_s.at[d], ug_r.at[d], at_z(d))
    ppb[...] = (scale * dot(uslice, img[...])).astype(bf16)
    for d in range(1, 4):
        go(ppb, ppx.at[d], px_s.at[d], px_r.at[d], at_x(d))

    fsum = jnp.zeros((128, E), f32)
    for h in both:
        r = rows(quarter[h] + pos[1 - h] * 256, 64)
        fsum = fsum + dot_tn(remt[r, :], gt[r, :])
    far[...] = fsum[0:8].astype(bf16)

    def send_far(d):
        @pl.when(c >= d)
        def _():
            rc(far, fars.at[up8(c), :], far_s.at[d], far_r.at[d], at_c(CLS - d)).start()

    peers(send_far)

    def wait_lab(d, _):
        got(labs.at[lax.rem(c + CLS - d, CLS)], lab_s.at[d], lab_r.at[d])
        return 0

    lax.fori_loop(1, CLS, wait_lab, 0)
    lt[...] = ls_here - jnp.sum(labs[...], axis=0)
    for d in range(1, 4):
        go(lt, ltx.at[d], lx_s.at[d], lx_r.at[d], at_x(d))


    for h in range(2):
        ag2[h][1]()
    for h in range(2):
        ag1[h][0][1]()

    for d in range(1, 4):
        got(ppx.at[d], px_s.at[d], px_r.at[d])
        got(ltx.at[d], lx_s.at[d], lx_r.at[d])
    ppxs[...] = (
        ppb[...].astype(f32) + ppx[1].astype(f32) + ppx[2].astype(f32) + ppx[3].astype(f32)
    ).astype(bf16)
    ltxs[...] = lt[...] + ltx[1] + ltx[2] + ltx[3]
    for d in range(1, 4):
        go(ppxs, ppy.at[d], py_s.at[d], py_r.at[d], at_y(d))
        go(ltxs, lty.at[d], ly_s.at[d], ly_r.at[d], at_y(d))

    for h in range(2):
        ag2[h][2]()
        ag1[h][3][0]()
        ag1[h][1][0]()
    for h in range(2):
        ag2[h][3]()
        ag1[h][2][0]()

    for d in range(1, 4):
        got(ppy.at[d], py_s.at[d], py_r.at[d])
        got(lty.at[d], ly_s.at[d], ly_r.at[d])
    pa[slot, :] = (
        ppxs[...].astype(f32) + ppy[1].astype(f32) + ppy[2].astype(f32) + ppy[3].astype(f32)
    ).astype(bf16)
    for d in range(1, NZ):
        go(pa.at[slot, :], pa.at[slot, :], pz_s.at[d], pz_r.at[d], at_z(d))
    total = ltxs[...] + lty[1] + lty[2] + lty[3]
    lossb[...] = total * (1.0 / BATCH)

    for b in (3, 1):
        for h in range(2):
            ag1[h][b][1]()
    def wait_far(d, _):
        @pl.when(c + d < CLS)
        def _():
            got(idss.at[up8(c + d), :], ids_s.at[d], ids_r.at[d])
            got(fars.at[up8(c + d), :], far_s.at[d], far_r.at[d])
        return 0

    lax.fori_loop(1, CLS, wait_far, 0)
    ri = lax.broadcasted_iota(i32, (128, 128), 0)
    ci = lax.broadcasted_iota(i32, (128, 128), 1)
    idrow = jnp.max(jnp.where(ri == ci, idss[...], -1), axis=0, keepdims=True)
    match = (last == idrow) & (last >= 0)
    fx[...] = dot(jnp.where(match, 1.0, 0.0).astype(bf16), fars[...])[0:8]
    for d in range(1, 4):
        go(fx, fxr.at[d], fx_s.at[d], fx_r.at[d], at_x(d))

    for h in range(2):
        ag1[h][2][1]()

    for d in range(1, NZ):
        got(ug.at[rows((k * 8 + q8(z + NZ - d)) * 32, 32), :], ug_s.at[d], ug_r.at[d])
    go(ug.at[mine, :], ug.at[mine, :], uc_s.at[1], uc_r.at[1], mate)

    for d in range(1, 4):
        got(fxr.at[d], fx_s.at[d], fx_r.at[d])
    fy[...] = fx[...] + fxr[1] + fxr[2] + fxr[3]
    for d in range(1, 4):
        go(fy, fyr.at[d], fy_s.at[d], fy_r.at[d], at_y(d))
    def add_rows(b):
        for h in both:
            ag1[h][b][2]()
            ag1[h][b][3]()

    add_rows(0)
    got(ug.at[other, :], uc_s.at[1], uc_r.at[1])
    gib[...] = (scale * dot_tn(ug[...], proj[...])).astype(bf16)

    for d in range(1, NZ):
        got(pa.at[rows((k * 8 + q8(z + NZ - d)) * 32, 32), :], pz_s.at[d], pz_r.at[d])
    go(pa.at[mine, :], pa.at[mine, :], uc_s.at[2], uc_r.at[2], mate)

    add_rows(3)
    add_rows(1)
    for d in range(1, 4):
        got(fyr.at[d], fy_s.at[d], fy_r.at[d])
    own = fy[...] + fyr[1] + fyr[2] + fyr[3]
    own = jnp.concatenate([own, jnp.zeros_like(own)], axis=0)
    hi = own.astype(bf16)
    lo = (own - hi.astype(f32)).astype(bf16)
    gnb[...] = dot_tn(sels[...], hi) + dot_tn(sels[...], lo)
    add_rows(2)
    got(pa.at[other, :], uc_s.at[2], uc_r.at[2])
    gpb[...] = pa[...].astype(f32)

    for cp in started:
        cp.wait_send()

    def drain(d, _):
        rc(stat, stat, st_s.at[d], st_r.at[d], mate).wait_send()
        rc(labt, labt, lab_s.at[d], lab_r.at[d], mate).wait_send()

        @pl.when(c + d < CLS)
        def _():
            rc(pub, pub, pub_s.at[d], pub_r.at[d], mate).wait_send()

        @pl.when(c >= d)
        def _():
            rc(ids, ids, ids_s.at[d], ids_r.at[d], mate).wait_send()
            rc(far, far, far_s.at[d], far_r.at[d], mate).wait_send()

        return 0

    lax.fori_loop(1, CLS, drain, 0)


def finish(lossb, gi, gt, gn, gp, cnt, loss_o, gi_o, gt_o, gn_o, gp_o, gnb, sem):
    outs = [
        pltpu.make_async_copy(a, b, sem.at[i])
        for i, (a, b) in enumerate(((gt, gt_o), (gp, gp_o), (gi, gi_o)))
    ]
    for cp in outs:
        cp.start()
    loss_o[...] = lossb[0:1, 0:1]
    for i in range(2):
        r = slice(i * 256, i * 256 + 256)
        gnb[r, :] = gn[r, :] + dot(cnt[r, :], gt[...])
        outs.append(pltpu.make_async_copy(gnb.at[r, :], gn_o.at[r, :], sem.at[3 + i]))
        outs[-1].start()
    for cp in outs:
        cp.wait()


def q8(v):
    return lax.rem(v, NZ)


def per_device(images, labels, taxon_emb, node_emb, proj, lineage):
    dma = pltpu.SemaphoreType.DMA
    vm = pltpu.VMEM
    scratch = [
        vm((LEVELS, T), i32), vm((1, B), i32),
        vm((2, 4, B, E), bf16), vm((T, E), bf16), vm((N, E), bf16), vm((E, E), bf16),
        vm((16, T), i32), vm((T, E), f32), vm((T, E), bf16),
        vm((T, B), f32), vm((T, 2 * B), bf16), vm((E, 2 * B), f32), vm((T, 128), bf16),
        vm((2, 4, 256, B), f32), vm((256, E), f32),
        vm((8, 128), i32), vm((2, 4, 8, 128), i32), vm((8, 128), f32), vm((2, 4, 8, 128), f32),
        vm((8, E), bf16), vm((CLS * 8, E), bf16), vm((8, 128), i32), vm((CLS * 8, 128), i32),
        vm((8, 128), f32), vm((CLS, 8, 128), f32), vm((8, 128), f32), vm((CLS, 8, 128), f32),
        vm((8, E), bf16), vm((CLS * 8, E), bf16), vm((1, B), f32),
        vm((E, B), bf16), vm((256, B), bf16), vm((256, B), bf16), vm((NZ, 32, B), bf16),
        vm((32, E), bf16), vm((4, 32, E), bf16), vm((32, E), bf16),
        vm((4, 32, E), bf16), vm((8, 128), f32), vm((4, 8, 128), f32),
        vm((8, 128), f32), vm((4, 8, 128), f32),
        vm((8, E), f32), vm((4, 8, E), f32), vm((8, E), f32), vm((4, 8, E), f32),
        vm((2, 256, E), bf16), vm((2, 4, 64, E), bf16),
        dma((7,)), vm((E, B), bf16), vm((E, E), bf16), vm((16, N), bf16),
    ]
    scratch += [dma((CLS,))] * 10
    scratch += [dma((12,))] * 2 + [dma((8,))] * 4 + [dma((12,))] * 2 + [dma((60,))] * 2
    scratch += [dma((3,))] * 2 + [dma((NZ,))] * 4
    scratch += [dma((4,))] * 4 + [dma((NZ,))] * 2 + [dma((4,))] * 4
    scratch += [dma((4,))] * 4
    hbm = pl.BlockSpec(memory_space=pltpu.HBM)
    vmem = pl.BlockSpec(memory_space=pltpu.VMEM)
    args = (lineage.T, labels.reshape(1, B), images, taxon_emb, node_emb, proj)
    held = pl.pallas_call(
        body,
        out_shape=(
            vm((8, 128), f32), vm((B, E), bf16), vm((T, E), bf16), vm((N, E), f32), vm((E, E), f32),
            vm((N, T), bf16),
        ),
        in_specs=[hbm] * 6,
        out_specs=[vmem] * 6,
        scratch_shapes=scratch,
        compiler_params=pltpu.CompilerParams(
            collective_id=0, has_side_effects=True, vmem_limit_bytes=52 * 1024 * 1024
        ),
    )(*[pltpu.with_memory_space_constraint(a, pltpu.HBM) for a in args])
    loss, gi, gt, gn, gp = pl.pallas_call(
        finish,
        out_shape=(
            jax.ShapeDtypeStruct((1, 1), f32),
            jax.ShapeDtypeStruct((B, E), bf16),
            jax.ShapeDtypeStruct((T, E), bf16),
            jax.ShapeDtypeStruct((N, E), f32),
            jax.ShapeDtypeStruct((E, E), f32),
        ),
        in_specs=[vmem] * 6,
        out_specs=[vmem] + [hbm] * 4,
        scratch_shapes=[vm((N, E), f32), dma((5,))],
        compiler_params=pltpu.CompilerParams(vmem_limit_bytes=8 * 1024 * 1024),
    )(*held)
    return (loss.reshape(()), gi, gt, gn, gp)


def solution(mesh):
    in_specs = (P("grp", None), P("grp"), P("cls", None), P("cls", None), P(), P("cls", None))
    out_specs = (P(), P("grp", None), P("cls", None), P("cls", None), P())
    return jax.shard_map(
        per_device, mesh=mesh, in_specs=in_specs, out_specs=out_specs, check_vma=False
    )
```

```python
import jax
import jax.numpy as jnp
from jax import lax
from jax.experimental import pallas as pl
from jax.experimental.pallas import tpu as pltpu
from jax.sharding import PartitionSpec as P

MESH = pl.DeviceIdType.MESH
f32, bf16, i32 = jnp.float32, jnp.bfloat16, jnp.int32
scale = 0.1
E, LEVELS, T, B, N = 512, 7, 2048, 512, 512
NX, NY, NZ, NC = 4, 4, 8, 2
CLS = NZ * NC
GRP = NX * NY
BATCH = B * GRP
NT = (((1,), (1,)), ((), ()))
TN = (((0,), (0,)), ((), ()))


def dot(a, b):
    return jnp.dot(a, b, preferred_element_type=f32)


def dot_nt(a, b):
    return lax.dot_general(a, b, NT, preferred_element_type=f32)


def dot_tn(a, b):
    return lax.dot_general(a, b, TN, preferred_element_type=f32)


def rows(start, size):
    return pl.ds(pl.multiple_of(start, size), size)


def body(
    lin_h, lab_h, img_h, tax_h, node_h, proj_h,
    lossb, gib, gt, gnb, gpb, cnt,
    lin_ref, lab_ref, ia, tax, node, proj, lin16, base32, summed, sc32, pb, acc, remt, sall, cga, glt, gl, gst, gs,
    pub, pubs, ids, idss, stat, stats, labt, labs, far, fars, frow,
    us, ucr, uh, uzr, ppb, ppx, ppxs, ppy, lt, ltx, ltxs, lty,
    fx, fxr, fy, fyr,
    g2, rb2,
    in_sem, ug, pa, sels,
    pub_s, pub_r, ids_s, ids_r, st_s, st_r, lab_s, lab_r, far_s, far_r,
    ia_s, ia_r, gl_s, gl_r, gs_s, gs_r, rs_s, rs_r, ag_s, ag_r, uc_s, uc_r, uz_s, uz_r, ug_s, ug_r,
    px_s, px_r, py_s, py_r, pz_s, pz_r, lx_s, lx_r, ly_s, ly_r,
    fx_s, fx_r, fy_s, fy_r,
):
    g = lax.axis_index("grp")
    c = lax.axis_index("cls")
    x, y = g // NY, lax.rem(g, NY)
    z, k = c // NC, lax.rem(c, NC)
    pos = (x, y)

    def at_x(d):
        return (lax.rem(x + d, NX) * NY + y, c)

    def at_y(d):
        return (x * NY + lax.rem(y + d, NY), c)

    def at_z(d):
        return (g, lax.rem(z + d, NZ) * NC + k)

    def at_c(d):
        return (g, lax.rem(c + d, CLS))

    mate = (g, z * NC + (1 - k))
    near = (at_x, at_y)
    started = []

    def rc(src, dst, ss, rs, dev):
        return pltpu.make_async_remote_copy(
            src_ref=src, dst_ref=dst, send_sem=ss, recv_sem=rs, device_id=dev, device_id_type=MESH
        )

    def go(src, dst, ss, rs, dev):
        cp = rc(src, dst, ss, rs, dev)
        cp.start()
        started.append(cp)
        return cp

    def got(dst, ss, rs):
        rc(dst, dst, ss, rs, mate).wait_recv()

    def far_first(i):
        return 8 + (1 - 2 * lax.rem(i, 2)) * ((i + 1) // 2)

    def peers(f):
        def step(i, _):
            f(far_first(i))
            return 0

        lax.fori_loop(0, CLS - 1, step, 0)

    img = ia.at[0, x]

    loads = [
        pltpu.make_async_copy(s, d, in_sem.at[i])
        for i, (s, d) in enumerate(((lin_h, lin_ref), (node_h, node), (img_h, img), (img_h, ia.at[1, y]), (proj_h, proj), (tax_h, tax), (lab_h, lab_ref)))
    ]
    for cp in loads:
        cp.start()
    pubs[...] = jnp.zeros_like(pubs)
    fars[...] = jnp.zeros_like(fars)
    idss[...] = jnp.full_like(idss, -1)

    barrier = pltpu.get_barrier_semaphore()

    def greet(d, _):
        pl.semaphore_signal(barrier, inc=1, device_id=at_c(d), device_id_type=MESH)
        return 0

    lax.fori_loop(1, CLS, greet, 0)
    for d in range(1, NX):
        pl.semaphore_signal(barrier, inc=1, device_id=at_x(d), device_id_type=MESH)
    for d in range(1, NY):
        pl.semaphore_signal(barrier, inc=1, device_id=at_y(d), device_id_type=MESH)

    base = c * N
    tbase = c * T
    lin16[...] = jnp.full_like(lin16, -1)
    loads[0].wait()
    lin16[0:LEVELS, :] = lin_ref[...]
    lin = lin16[...]
    remote = (lin >= 0) & (lin < base)
    pid = jnp.max(jnp.where(remote, lin, -1), axis=1, keepdims=True)
    rem16 = jnp.where(remote, 1.0, 0.0).astype(bf16)
    lane_n = lax.broadcasted_iota(i32, (16, N), 1)
    last = lin16[:, T - 128 : T][:, 127:128]
    loads[1].wait()
    sel = jnp.where(last - base == lane_n, 1.0, 0.0).astype(bf16)
    sels[...] = sel
    pub[...] = dot(sel, node[...])[0:8].astype(bf16)
    ids[...] = jnp.broadcast_to(pid[0:8], (8, 128))

    pl.semaphore_wait(barrier, CLS - 1 + NX - 1 + NY - 1)

    def up8(r):
        return rows(r * 8, 8)

    def send_pub(d):
        @pl.when(c + d < CLS)
        def _():
            rc(pub, pubs.at[up8(c), :], pub_s.at[d], pub_r.at[d], at_c(d)).start()

    peers(send_pub)

    def q4(v):
        return lax.rem(v, 4)

    def ring(p, right, left, send, get):
        def first():
            send(p, 0, 0, right)
            send(p, 1, 3, left)
            send(p, 1, 1, right)
            send(p, 0, 4, left)

        def second():
            get(q4(p + 3), 0, 0)
            send(q4(p + 3), 0, 2, right)
            get(q4(p + 1), 1, 3)
            send(q4(p + 1), 1, 5, left)

        def third():
            get(q4(p + 3), 1, 1)
            get(q4(p + 1), 0, 4)

        def last():
            get(q4(p + 2), 0, 2)
            get(q4(p + 2), 1, 5)

        return first, second, third, last

    def images(h):
        def part(q, half):
            return ia.at[h, q, rows(half * 256, 256), :]

        def send(q, half, i, dev):
            ref = part(q, half)
            go(ref, ref, ia_s.at[h * 6 + i], ia_r.at[h * 6 + i], dev)

        def get(q, half, i):
            got(part(q, half), ia_s.at[h * 6 + i], ia_r.at[h * 6 + i])

        return ring(pos[h], near[h](1), near[h](3), send, get)

    both = range(2)
    lines = [images(h) for h in both]
    for h in both:
        loads[2 + h].wait()
        lines[h][0]()

    def count_block(i, _):
        nid = lax.broadcasted_iota(i32, (32, T), 0) + (i * 32 + base)
        hit = nid == lin16[0:1, :]
        for l in range(1, LEVELS):
            hit = hit | (nid == lin16[l : l + 1, :])
        cnt[rows(i * 32, 32), :] = jnp.where(hit, 1.0, 0.0).astype(bf16)
        return 0

    lax.fori_loop(0, N // 32, count_block, 0, unroll=2)
    eye = lax.broadcasted_iota(i32, (16, 128), 0) == lax.broadcasted_iota(i32, (16, 128), 1)
    remt[...] = dot_tn(rem16, jnp.where(eye, 1.0, 0.0).astype(bf16)).astype(bf16)
    for cp in loads[4:]:
        cp.wait()
    for q in range(4):
        glt[q : q + 1, :] = lab_ref[:, q * 128 : q * 128 + 128]
    for h in both:
        gl[h, pos[h]] = glt[...]
        for d in range(1, 4):
            go(glt, gl.at[h, pos[h]], gl_s.at[h * 4 + d], gl_r.at[h * 4 + d], near[h](d))

    def local_sum(i, _):
        r = rows(i * 256, 256)
        base32[r, :] = tax[r, :].astype(f32) + dot_tn(cnt[:, r], node[...])
        return 0

    lax.fori_loop(0, T // 256, local_sum, 0, unroll=2)

    for h in both:
        lines[h][1]()

    def wait_pub(d, _):
        @pl.when(c >= d)
        def _():
            got(pubs.at[up8(c - d), :], pub_s.at[d], pub_r.at[d])
        return 0

    lax.fori_loop(1, CLS, wait_pub, 0)
    lane = lax.broadcasted_iota(i32, (128, 128), 1)
    pid128 = jnp.concatenate([pid, jnp.full((112, 1), -1, i32)], axis=0)
    want = (pid128 >> 9) * 8 + lax.broadcasted_iota(i32, (128, 1), 0)
    pick = jnp.where((want == lane) & (pid128 >= 0), 1.0, 0.0).astype(bf16)
    prefix = dot(pick, pubs[...]).astype(bf16)

    def score_block(i, top):
        r = rows(i * 256, 256)
        s = (base32[r, :] + dot(remt[r, :], prefix)).astype(bf16)
        summed[r, :] = s
        pr = dot(s, proj[...]).astype(bf16)
        st = scale * dot_nt(pr, img[...])
        sc32[r, :] = st
        return jnp.maximum(top, jnp.max(st.reshape(32, 8, B), axis=0))

    top8 = lax.fori_loop(0, T // 256, score_block, jnp.full((8, B), -jnp.inf, f32), unroll=2)
    mtop = jnp.max(top8, axis=0, keepdims=True)
    label = lab_ref[...] - tbase

    def exp_block(i, carry):
        tot, ls = carry
        r = rows(i * 256, 256)
        st = sc32[r, :]
        hit = lax.broadcasted_iota(i32, (256, B), 0) + i * 256 == label
        p = jnp.exp(st - mtop)
        ls = ls + jnp.sum(jnp.where(hit, st, 0.0).reshape(32, 8, B), axis=0)
        tot = tot + jnp.sum(p.reshape(32, 8, B), axis=0)
        sc32[r, :] = p
        pb[r, 0:B] = p.astype(bf16)
        pb[r, B : 2 * B] = jnp.where(hit, 1.0, 0.0).astype(bf16)
        return tot, ls

    zero8 = jnp.zeros((8, B), f32)
    tot8, ls8 = lax.fori_loop(0, T // 256, exp_block, (zero8, zero8))
    tot = jnp.sum(tot8, axis=0, keepdims=True)
    for q in range(4):
        stat[q : q + 1, :] = mtop[:, q * 128 : q * 128 + 128]
        stat[q + 4 : q + 5, :] = tot[:, q * 128 : q * 128 + 128]

    def send_stat(d):
        rc(stat, stats.at[c], st_s.at[d], st_r.at[d], at_c(d)).start()

    def send_lab(d):
        rc(labt, labs.at[c], lab_s.at[d], lab_r.at[d], at_c(d)).start()

    def send_ids(d):
        @pl.when(c >= d)
        def _():
            rc(ids, idss.at[up8(c), :], ids_s.at[d], ids_r.at[d], at_c(CLS - d)).start()

    peers(send_stat)
    lsum = ls8[:, 0:128] + ls8[:, 128:256] + ls8[:, 256:384] + ls8[:, 384:512]
    labt[...] = jnp.broadcast_to(jnp.sum(lsum, keepdims=True), (8, 128))
    stats[c] = stat[...]
    labs[c] = labt[...]

    acc[...] = jnp.zeros_like(acc)

    def u_block(i, _):
        r = rows(i * 512, 512)
        acc[...] += dot_tn(summed[r, :], pb[r, :])
        return 0

    lax.fori_loop(0, T // 512, u_block, 0)

    quarter = [1024 * h + pos[h] * 64 for h in both]

    def line_scores(h):
        lines[h][2]()
        lines[h][3]()
        own = jnp.concatenate([summed[rows(quarter[h] + i * 256, 64), :] for i in range(4)], axis=0)
        pr = dot(own, proj[...]).astype(bf16)
        for j in range(4):
            sall[h, j] = scale * dot_nt(pr, ia[h, j])

    line_scores(0)

    def wait_stat(d, _):
        got(stats.at[lax.rem(c + CLS - d, CLS)], st_s.at[d], st_r.at[d])
        return 0

    lax.fori_loop(1, CLS, wait_stat, 0)
    all_m = stats[:, 0:4, :]
    gtop = jnp.max(all_m, axis=0)
    gtot = jnp.sum(stats[:, 4:8, :] * jnp.exp(all_m - gtop[None]), axis=0)
    fac = jnp.exp(stat[0:4, :] - gtop) / gtot
    for q in range(4):
        frow[:, q * 128 : q * 128 + 128] = fac[q : q + 1, :]
    fr = frow[...]
    ls_here = jnp.sum(gtop + jnp.log(gtot), keepdims=True)
    gst[0:4, :] = gtop
    gst[4:8, :] = 1.0 / gtot
    for h in both:
        gs[h, pos[h]] = gst[...]
        for d in range(1, 4):
            go(gst, gs.at[h, pos[h]], gs_s.at[h * 4 + d], gs_r.at[h * 4 + d], near[h](d))
    us[...] = (acc[:, 0:B] * fr - acc[:, B : 2 * B]).astype(bf16)
    other = rows((1 - k) * 256, 256)
    mine = rows(k * 256, 256)
    uc = go(us.at[other, :], ucr, uc_s.at[0], uc_r.at[0], mate)

    peers(send_ids)
    peers(send_lab)

    got(ucr, uc_s.at[0], uc_r.at[0])
    uh[...] = (us[mine, :].astype(f32) + ucr[...].astype(f32)).astype(bf16)
    for d in range(1, NZ):
        go(uh.at[rows(q8(z + d) * 32, 32), :], uzr.at[z], uz_s.at[d], uz_r.at[d], at_z(d))
    uzr[z] = uh[rows(z * 32, 32), :]

    line_scores(1)
    for h in both:
        for d in range(1, 4):
            got(gl.at[h, q4(pos[h] + 4 - d)], gl_s.at[h * 4 + d], gl_r.at[h * 4 + d])
            got(gs.at[h, q4(pos[h] + 4 - d)], gs_s.at[h * 4 + d], gs_r.at[h * 4 + d])

    def flat(t, r0):
        return jnp.concatenate([t[r0 + q : r0 + q + 1, :] for q in range(4)], axis=1)

    def stage(h):
        axis = 1 - h
        p = pos[axis]

        def first():
            for d in (2, 1, 3):
                go(g2.at[h, rows(q4(p + d) * 64, 64), :], rb2.at[h, d], rs_s.at[h * 4 + d], rs_r.at[h * 4 + d], near[axis](d))

        def last():
            total = g2[h, rows(p * 64, 64), :].astype(f32)
            for d in (1, 3, 2):
                got(rb2.at[h, d], rs_s.at[h * 4 + d], rs_r.at[h * 4 + d])
                total = total + rb2[h, d].astype(f32)
            return total.astype(bf16)

        return first, last

    s2 = (stage(0), stage(1))
    for h in both:
        ri = lax.broadcasted_iota(i32, (256, 1), 0)
        tid = ri + (ri >> 6) * 192 + (tbase + quarter[h])
        for j in range(4):
            t = gs[h, j]
            hit = jnp.where(tid == flat(gl[h, j], 0), 1.0, 0.0)
            w = jnp.exp(sall[h, j] - flat(t, 0)) * flat(t, 4) - hit
            part = dot(w.astype(bf16), ia[h, j])
            cga[...] = part if j == 0 else cga[...] + part
        g2[h] = dot_nt((scale * cga[...]).astype(bf16), proj[...]).astype(bf16)
        s2[h][0]()
    fsum = jnp.zeros((128, E), f32)
    for h in both:
        for i in range(4):
            fsum = fsum + dot_tn(remt[rows(quarter[h] + i * 256, 64), :], g2[h, i * 64 : i * 64 + 64, :])
    far[...] = fsum[0:8].astype(bf16)

    def send_far(d):
        @pl.when(c >= d)
        def _():
            rc(far, fars.at[up8(c), :], far_s.at[d], far_r.at[d], at_c(CLS - d)).start()

    peers(send_far)

    def gather(h, s, blk):
        axis = (h + s) % 2
        p = pos[axis]
        right, left = near[axis](1), near[axis](3)
        if s == 0:
            step, off, sem = 64, 1024 * h + q4(pos[1 - h] + blk) * 256, (h * 5 + blk) * 6
        else:
            step, off, sem = 256, 1024 * h + pos[h] * 64, (h * 5 + 4) * 6

        def part(q, half):
            return gt.at[rows(off + q * step + half * 32, 32), :]

        def send(q, half, i, dev):
            ref = part(q, half)
            go(ref, ref, ag_s.at[sem + i], ag_r.at[sem + i], dev)

        def get(q, half, i):
            got(part(q, half), ag_s.at[sem + i], ag_r.at[sem + i])

        return ring(p, right, left, send, get)

    ag2 = [gather(h, 1, 0) for h in range(2)]
    ag1 = [[gather(h, 0, b) for b in range(4)] for h in range(2)]
    for h in range(2):
        start = 1024 * h + pos[h] * 64 + pos[1 - h] * 256
        gt[rows(start, 64), :] = s2[h][1]()
        ag2[h][0]()
        ag1[h][0][0]()
    for d in range(1, NZ):
        got(uzr.at[q8(z + NZ - d)], uz_s.at[d], uz_r.at[d])
    uslice = uzr[0].astype(f32)
    for d in range(1, NZ):
        uslice = uslice + uzr[d].astype(f32)
    uslice = uslice.astype(bf16)
    slot = rows((k * 8 + z) * 32, 32)
    ug[slot, :] = uslice
    for d in range(1, NZ):
        go(ug.at[slot, :], ug.at[slot, :], ug_s.at[d], ug_r.at[d], at_z(d))
    ppb[...] = (scale * dot(uslice, img[...])).astype(bf16)
    for d in range(1, 4):
        go(ppb, ppx.at[d], px_s.at[d], px_r.at[d], at_x(d))

    def wait_lab(d, _):
        got(labs.at[lax.rem(c + CLS - d, CLS)], lab_s.at[d], lab_r.at[d])
        return 0

    lax.fori_loop(1, CLS, wait_lab, 0)
    lt[...] = ls_here - jnp.sum(labs[...], axis=0)
    for d in range(1, 4):
        go(lt, ltx.at[d], lx_s.at[d], lx_r.at[d], at_x(d))


    def wait_far(d, _):
        @pl.when(c + d < CLS)
        def _():
            got(idss.at[up8(c + d), :], ids_s.at[d], ids_r.at[d])
            got(fars.at[up8(c + d), :], far_s.at[d], far_r.at[d])
        return 0

    lax.fori_loop(1, CLS, wait_far, 0)
    ri = lax.broadcasted_iota(i32, (128, 128), 0)
    ci = lax.broadcasted_iota(i32, (128, 128), 1)
    idrow = jnp.max(jnp.where(ri == ci, idss[...], -1), axis=0, keepdims=True)
    match = (last == idrow) & (last >= 0)
    fx[...] = dot(jnp.where(match, 1.0, 0.0).astype(bf16), fars[...])[0:8]
    for d in range(1, 4):
        go(fx, fxr.at[d], fx_s.at[d], fx_r.at[d], at_x(d))

    for h in range(2):
        ag2[h][1]()
    for h in range(2):
        ag1[h][0][1]()

    for d in range(1, 4):
        got(ppx.at[d], px_s.at[d], px_r.at[d])
        got(ltx.at[d], lx_s.at[d], lx_r.at[d])
    ppxs[...] = (
        ppb[...].astype(f32) + ppx[1].astype(f32) + ppx[2].astype(f32) + ppx[3].astype(f32)
    ).astype(bf16)
    ltxs[...] = lt[...] + ltx[1] + ltx[2] + ltx[3]
    for d in range(1, 4):
        go(ppxs, ppy.at[d], py_s.at[d], py_r.at[d], at_y(d))
        go(ltxs, lty.at[d], ly_s.at[d], ly_r.at[d], at_y(d))
    for d in range(1, 4):
        got(fxr.at[d], fx_s.at[d], fx_r.at[d])
    fy[...] = fx[...] + fxr[1] + fxr[2] + fxr[3]
    for d in range(1, 4):
        go(fy, fyr.at[d], fy_s.at[d], fy_r.at[d], at_y(d))

    for h in range(2):
        ag2[h][2]()
        ag1[h][3][0]()
        ag1[h][1][0]()
    for h in range(2):
        ag2[h][3]()
        ag1[h][2][0]()

    for d in range(1, 4):
        got(ppy.at[d], py_s.at[d], py_r.at[d])
        got(lty.at[d], ly_s.at[d], ly_r.at[d])
    pa[slot, :] = (
        ppxs[...].astype(f32) + ppy[1].astype(f32) + ppy[2].astype(f32) + ppy[3].astype(f32)
    ).astype(bf16)
    for d in range(1, NZ):
        go(pa.at[slot, :], pa.at[slot, :], pz_s.at[d], pz_r.at[d], at_z(d))
    total = ltxs[...] + lty[1] + lty[2] + lty[3]
    lossb[...] = total * (1.0 / BATCH)

    for b in (3, 1):
        for h in range(2):
            ag1[h][b][1]()
    for h in range(2):
        ag1[h][2][1]()

    for d in range(1, NZ):
        got(ug.at[rows((k * 8 + q8(z + NZ - d)) * 32, 32), :], ug_s.at[d], ug_r.at[d])
    go(ug.at[mine, :], ug.at[mine, :], uc_s.at[1], uc_r.at[1], mate)

    def add_rows(b):
        for h in both:
            ag1[h][b][2]()
            ag1[h][b][3]()

    add_rows(0)
    got(ug.at[other, :], uc_s.at[1], uc_r.at[1])
    gib[...] = (scale * dot_tn(ug[...], proj[...])).astype(bf16)

    for d in range(1, NZ):
        got(pa.at[rows((k * 8 + q8(z + NZ - d)) * 32, 32), :], pz_s.at[d], pz_r.at[d])
    go(pa.at[mine, :], pa.at[mine, :], uc_s.at[2], uc_r.at[2], mate)

    add_rows(3)
    add_rows(1)
    for d in range(1, 4):
        got(fyr.at[d], fy_s.at[d], fy_r.at[d])
    own = fy[...] + fyr[1] + fyr[2] + fyr[3]
    own = jnp.concatenate([own, jnp.zeros_like(own)], axis=0)
    hi = own.astype(bf16)
    lo = (own - hi.astype(f32)).astype(bf16)
    gnb[...] = dot_tn(sels[...], hi) + dot_tn(sels[...], lo)
    add_rows(2)
    got(pa.at[other, :], uc_s.at[2], uc_r.at[2])
    gpb[...] = pa[...].astype(f32)

    for cp in started:
        cp.wait_send()

    def drain(d, _):
        rc(stat, stat, st_s.at[d], st_r.at[d], mate).wait_send()
        rc(labt, labt, lab_s.at[d], lab_r.at[d], mate).wait_send()

        @pl.when(c + d < CLS)
        def _():
            rc(pub, pub, pub_s.at[d], pub_r.at[d], mate).wait_send()

        @pl.when(c >= d)
        def _():
            rc(ids, ids, ids_s.at[d], ids_r.at[d], mate).wait_send()
            rc(far, far, far_s.at[d], far_r.at[d], mate).wait_send()

        return 0

    lax.fori_loop(1, CLS, drain, 0)


def finish(lossb, gi, gt, gn, gp, cnt, loss_o, gi_o, gt_o, gn_o, gp_o, gnb, sem):
    outs = [
        pltpu.make_async_copy(a, b, sem.at[i])
        for i, (a, b) in enumerate(((gt, gt_o), (gp, gp_o), (gi, gi_o)))
    ]
    for cp in outs:
        cp.start()
    loss_o[...] = lossb[0:1, 0:1]
    for i in range(2):
        r = slice(i * 256, i * 256 + 256)
        gnb[r, :] = gn[r, :] + dot(cnt[r, :], gt[...])
        outs.append(pltpu.make_async_copy(gnb.at[r, :], gn_o.at[r, :], sem.at[3 + i]))
        outs[-1].start()
    for cp in outs:
        cp.wait()


def q8(v):
    return lax.rem(v, NZ)


def per_device(images, labels, taxon_emb, node_emb, proj, lineage):
    dma = pltpu.SemaphoreType.DMA
    vm = pltpu.VMEM
    scratch = [
        vm((LEVELS, T), i32), vm((1, B), i32),
        vm((2, 4, B, E), bf16), vm((T, E), bf16), vm((N, E), bf16), vm((E, E), bf16),
        vm((16, T), i32), vm((T, E), f32), vm((T, E), bf16),
        vm((T, B), f32), vm((T, 2 * B), bf16), vm((E, 2 * B), f32), vm((T, 128), bf16),
        vm((2, 4, 256, B), f32), vm((256, E), f32),
        vm((8, 128), i32), vm((2, 4, 8, 128), i32), vm((8, 128), f32), vm((2, 4, 8, 128), f32),
        vm((8, E), bf16), vm((CLS * 8, E), bf16), vm((8, 128), i32), vm((CLS * 8, 128), i32),
        vm((8, 128), f32), vm((CLS, 8, 128), f32), vm((8, 128), f32), vm((CLS, 8, 128), f32),
        vm((8, E), bf16), vm((CLS * 8, E), bf16), vm((1, B), f32),
        vm((E, B), bf16), vm((256, B), bf16), vm((256, B), bf16), vm((NZ, 32, B), bf16),
        vm((32, E), bf16), vm((4, 32, E), bf16), vm((32, E), bf16),
        vm((4, 32, E), bf16), vm((8, 128), f32), vm((4, 8, 128), f32),
        vm((8, 128), f32), vm((4, 8, 128), f32),
        vm((8, E), f32), vm((4, 8, E), f32), vm((8, E), f32), vm((4, 8, E), f32),
        vm((2, 256, E), bf16), vm((2, 4, 64, E), bf16),
        dma((7,)), vm((E, B), bf16), vm((E, E), bf16), vm((16, N), bf16),
    ]
    scratch += [dma((CLS,))] * 10
    scratch += [dma((12,))] * 2 + [dma((8,))] * 4 + [dma((12,))] * 2 + [dma((60,))] * 2
    scratch += [dma((3,))] * 2 + [dma((NZ,))] * 4
    scratch += [dma((4,))] * 4 + [dma((NZ,))] * 2 + [dma((4,))] * 4
    scratch += [dma((4,))] * 4
    hbm = pl.BlockSpec(memory_space=pltpu.HBM)
    vmem = pl.BlockSpec(memory_space=pltpu.VMEM)
    args = (lineage.T, labels.reshape(1, B), images, taxon_emb, node_emb, proj)
    held = pl.pallas_call(
        body,
        out_shape=(
            vm((8, 128), f32), vm((B, E), bf16), vm((T, E), bf16), vm((N, E), f32), vm((E, E), f32),
            vm((N, T), bf16),
        ),
        in_specs=[hbm] * 6,
        out_specs=[vmem] * 6,
        scratch_shapes=scratch,
        compiler_params=pltpu.CompilerParams(
            collective_id=0, has_side_effects=True, vmem_limit_bytes=52 * 1024 * 1024
        ),
    )(*[pltpu.with_memory_space_constraint(a, pltpu.HBM) for a in args])
    loss, gi, gt, gn, gp = pl.pallas_call(
        finish,
        out_shape=(
            jax.ShapeDtypeStruct((1, 1), f32),
            jax.ShapeDtypeStruct((B, E), bf16),
            jax.ShapeDtypeStruct((T, E), bf16),
            jax.ShapeDtypeStruct((N, E), f32),
            jax.ShapeDtypeStruct((E, E), f32),
        ),
        in_specs=[vmem] * 6,
        out_specs=[vmem] + [hbm] * 4,
        scratch_shapes=[vm((N, E), f32), dma((5,))],
        compiler_params=pltpu.CompilerParams(vmem_limit_bytes=8 * 1024 * 1024),
    )(*held)
    return (loss.reshape(()), gi, gt, gn, gp)


def solution(mesh):
    in_specs = (P("grp", None), P("grp"), P("cls", None), P("cls", None), P(), P("cls", None))
    out_specs = (P(), P("grp", None), P("cls", None), P("cls", None), P())
    return jax.shard_map(
        per_device, mesh=mesh, in_specs=in_specs, out_specs=out_specs, check_vma=False
    )
```

```python
import jax
import jax.numpy as jnp
from jax import lax
from jax.experimental import pallas as pl
from jax.experimental.pallas import tpu as pltpu
from jax.sharding import PartitionSpec as P

MESH = pl.DeviceIdType.MESH
f32, bf16, i32 = jnp.float32, jnp.bfloat16, jnp.int32
scale = 0.1
E, LEVELS, T, B, N = 512, 7, 2048, 512, 512
NX, NY, NZ, NC = 4, 4, 8, 2
CLS = NZ * NC
GRP = NX * NY
BATCH = B * GRP
NT = (((1,), (1,)), ((), ()))
TN = (((0,), (0,)), ((), ()))


def dot(a, b):
    return jnp.dot(a, b, preferred_element_type=f32)


def dot_nt(a, b):
    return lax.dot_general(a, b, NT, preferred_element_type=f32)


def dot_tn(a, b):
    return lax.dot_general(a, b, TN, preferred_element_type=f32)


def rows(start, size):
    return pl.ds(pl.multiple_of(start, size), size)


def body(
    lin_h, lab_h, img_h, tax_h, node_h, proj_h,
    lossb, gib, gt, gnb, gpb, cnt,
    lin_ref, lab_ref, ia, tax, node, proj, lin16, base32, summed, sc32, pb, acc, remt, sall, cga, glt, gl, gst, gs,
    pub, pubs, ids, idss, stat, stats, labt, labs, far, fars, frow,
    us, ucr, uh, uzr, ppb, ppx, ppxs, ppy, lt, ltx, ltxs, lty,
    fx, fxr, fy, fyr,
    g2, rb2,
    in_sem, ug, pa, sels,
    pub_s, pub_r, ids_s, ids_r, st_s, st_r, lab_s, lab_r, far_s, far_r,
    ia_s, ia_r, gl_s, gl_r, gs_s, gs_r, rs_s, rs_r, ag_s, ag_r, uc_s, uc_r, uz_s, uz_r, ug_s, ug_r,
    px_s, px_r, py_s, py_r, pz_s, pz_r, lx_s, lx_r, ly_s, ly_r,
    fx_s, fx_r, fy_s, fy_r,
):
    g = lax.axis_index("grp")
    c = lax.axis_index("cls")
    x, y = g // NY, lax.rem(g, NY)
    z, k = c // NC, lax.rem(c, NC)
    pos = (x, y)

    def at_x(d):
        return (lax.rem(x + d, NX) * NY + y, c)

    def at_y(d):
        return (x * NY + lax.rem(y + d, NY), c)

    def at_z(d):
        return (g, lax.rem(z + d, NZ) * NC + k)

    def at_c(d):
        return (g, lax.rem(c + d, CLS))

    mate = (g, z * NC + (1 - k))
    near = (at_x, at_y)
    started = []

    def rc(src, dst, ss, rs, dev):
        return pltpu.make_async_remote_copy(
            src_ref=src, dst_ref=dst, send_sem=ss, recv_sem=rs, device_id=dev, device_id_type=MESH
        )

    def go(src, dst, ss, rs, dev):
        cp = rc(src, dst, ss, rs, dev)
        cp.start()
        started.append(cp)
        return cp

    def got(dst, ss, rs):
        rc(dst, dst, ss, rs, mate).wait_recv()

    def far_first(i):
        return 8 + (1 - 2 * lax.rem(i, 2)) * ((i + 1) // 2)

    def peers(f):
        def step(i, _):
            f(far_first(i))
            return 0

        lax.fori_loop(0, CLS - 1, step, 0)

    img = ia.at[0, x]

    loads = [
        pltpu.make_async_copy(s, d, in_sem.at[i])
        for i, (s, d) in enumerate(((lin_h, lin_ref), (node_h, node), (img_h, img), (img_h, ia.at[1, y]), (proj_h, proj), (tax_h, tax), (lab_h, lab_ref)))
    ]
    for cp in loads:
        cp.start()
    pubs[...] = jnp.zeros_like(pubs)
    fars[...] = jnp.zeros_like(fars)
    idss[...] = jnp.full_like(idss, -1)

    barrier = pltpu.get_barrier_semaphore()

    def greet(d, _):
        pl.semaphore_signal(barrier, inc=1, device_id=at_c(d), device_id_type=MESH)
        return 0

    lax.fori_loop(1, CLS, greet, 0)
    for d in range(1, NX):
        pl.semaphore_signal(barrier, inc=1, device_id=at_x(d), device_id_type=MESH)
    for d in range(1, NY):
        pl.semaphore_signal(barrier, inc=1, device_id=at_y(d), device_id_type=MESH)

    base = c * N
    tbase = c * T
    lin16[...] = jnp.full_like(lin16, -1)
    loads[0].wait()
    lin16[0:LEVELS, :] = lin_ref[...]
    lin = lin16[...]
    remote = (lin >= 0) & (lin < base)
    pid = jnp.max(jnp.where(remote, lin, -1), axis=1, keepdims=True)
    rem16 = jnp.where(remote, 1.0, 0.0).astype(bf16)
    lane_n = lax.broadcasted_iota(i32, (16, N), 1)
    last = lin16[:, T - 128 : T][:, 127:128]
    loads[1].wait()
    sel = jnp.where(last - base == lane_n, 1.0, 0.0).astype(bf16)
    sels[...] = sel
    pub[...] = dot(sel, node[...])[0:8].astype(bf16)
    ids[...] = jnp.broadcast_to(pid[0:8], (8, 128))

    pl.semaphore_wait(barrier, CLS - 1 + NX - 1 + NY - 1)

    def up8(r):
        return rows(r * 8, 8)

    def send_pub(d):
        @pl.when(c + d < CLS)
        def _():
            rc(pub, pubs.at[up8(c), :], pub_s.at[d], pub_r.at[d], at_c(d)).start()

    peers(send_pub)

    def q4(v):
        return lax.rem(v, 4)

    def ring(p, right, left, send, get):
        def first():
            send(p, 0, 0, right)
            send(p, 1, 3, left)
            send(p, 1, 1, right)
            send(p, 0, 4, left)

        def second():
            get(q4(p + 3), 0, 0)
            send(q4(p + 3), 0, 2, right)
            get(q4(p + 1), 1, 3)
            send(q4(p + 1), 1, 5, left)

        def third():
            get(q4(p + 3), 1, 1)
            get(q4(p + 1), 0, 4)

        def last():
            get(q4(p + 2), 0, 2)
            get(q4(p + 2), 1, 5)

        return first, second, third, last

    def images(h):
        def part(q, half):
            return ia.at[h, q, rows(half * 256, 256), :]

        def send(q, half, i, dev):
            ref = part(q, half)
            go(ref, ref, ia_s.at[h * 6 + i], ia_r.at[h * 6 + i], dev)

        def get(q, half, i):
            got(part(q, half), ia_s.at[h * 6 + i], ia_r.at[h * 6 + i])

        return ring(pos[h], near[h](1), near[h](3), send, get)

    both = range(2)
    lines = [images(h) for h in both]
    for h in both:
        loads[2 + h].wait()
        lines[h][0]()

    def count_block(i, _):
        nid = lax.broadcasted_iota(i32, (32, T), 0) + (i * 32 + base)
        hit = nid == lin16[0:1, :]
        for l in range(1, LEVELS):
            hit = hit | (nid == lin16[l : l + 1, :])
        cnt[rows(i * 32, 32), :] = jnp.where(hit, 1.0, 0.0).astype(bf16)
        return 0

    lax.fori_loop(0, N // 32, count_block, 0, unroll=2)
    eye = lax.broadcasted_iota(i32, (16, 128), 0) == lax.broadcasted_iota(i32, (16, 128), 1)
    remt[...] = dot_tn(rem16, jnp.where(eye, 1.0, 0.0).astype(bf16)).astype(bf16)
    for cp in loads[4:]:
        cp.wait()
    for q in range(4):
        glt[q : q + 1, :] = lab_ref[:, q * 128 : q * 128 + 128]
    for h in both:
        gl[h, pos[h]] = glt[...]
        for d in range(1, 4):
            go(glt, gl.at[h, pos[h]], gl_s.at[h * 4 + d], gl_r.at[h * 4 + d], near[h](d))

    def local_sum(i, _):
        r = rows(i * 256, 256)
        base32[r, :] = tax[r, :].astype(f32) + dot_tn(cnt[:, r], node[...])
        return 0

    lax.fori_loop(0, T // 256, local_sum, 0, unroll=2)

    for h in both:
        lines[h][1]()

    def send_ids(d):
        @pl.when(c >= d)
        def _():
            rc(ids, idss.at[up8(c), :], ids_s.at[d], ids_r.at[d], at_c(CLS - d)).start()

    peers(send_ids)

    def wait_pub(d, _):
        @pl.when(c >= d)
        def _():
            got(pubs.at[up8(c - d), :], pub_s.at[d], pub_r.at[d])
        return 0

    lax.fori_loop(1, CLS, wait_pub, 0)
    lane = lax.broadcasted_iota(i32, (128, 128), 1)
    pid128 = jnp.concatenate([pid, jnp.full((112, 1), -1, i32)], axis=0)
    want = (pid128 >> 9) * 8 + lax.broadcasted_iota(i32, (128, 1), 0)
    pick = jnp.where((want == lane) & (pid128 >= 0), 1.0, 0.0).astype(bf16)
    prefix = dot(pick, pubs[...]).astype(bf16)

    def score_block(i, top):
        r = rows(i * 256, 256)
        s = (base32[r, :] + dot(remt[r, :], prefix)).astype(bf16)
        summed[r, :] = s
        pr = dot(s, proj[...]).astype(bf16)
        st = scale * dot_nt(pr, img[...])
        sc32[r, :] = st
        return jnp.maximum(top, jnp.max(st.reshape(32, 8, B), axis=0))

    top8 = lax.fori_loop(0, T // 256, score_block, jnp.full((8, B), -jnp.inf, f32), unroll=2)
    mtop = jnp.max(top8, axis=0, keepdims=True)
    label = lab_ref[...] - tbase

    def exp_block(i, carry):
        tot, ls = carry
        r = rows(i * 256, 256)
        st = sc32[r, :]
        hit = lax.broadcasted_iota(i32, (256, B), 0) + i * 256 == label
        p = jnp.exp(st - mtop)
        ls = ls + jnp.sum(jnp.where(hit, st, 0.0).reshape(32, 8, B), axis=0)
        tot = tot + jnp.sum(p.reshape(32, 8, B), axis=0)
        sc32[r, :] = p
        pb[r, 0:B] = p.astype(bf16)
        pb[r, B : 2 * B] = jnp.where(hit, 1.0, 0.0).astype(bf16)
        return tot, ls

    zero8 = jnp.zeros((8, B), f32)
    tot8, ls8 = lax.fori_loop(0, T // 256, exp_block, (zero8, zero8))
    tot = jnp.sum(tot8, axis=0, keepdims=True)
    for q in range(4):
        stat[q : q + 1, :] = mtop[:, q * 128 : q * 128 + 128]
        stat[q + 4 : q + 5, :] = tot[:, q * 128 : q * 128 + 128]

    def send_stat(d):
        rc(stat, stats.at[c], st_s.at[d], st_r.at[d], at_c(d)).start()

    def send_lab(d):
        rc(labt, labs.at[c], lab_s.at[d], lab_r.at[d], at_c(d)).start()

    peers(send_stat)
    lsum = ls8[:, 0:128] + ls8[:, 128:256] + ls8[:, 256:384] + ls8[:, 384:512]
    labt[...] = jnp.broadcast_to(jnp.sum(lsum, keepdims=True), (8, 128))
    stats[c] = stat[...]
    labs[c] = labt[...]

    acc[...] = jnp.zeros_like(acc)

    def u_block(i, _):
        r = rows(i * 512, 512)
        acc[...] += dot_tn(summed[r, :], pb[r, :])
        return 0

    lax.fori_loop(0, T // 512, u_block, 0)
    peers(send_lab)

    quarter = [1024 * h + pos[h] * 64 for h in both]

    def line_scores(h):
        lines[h][2]()
        lines[h][3]()
        own = jnp.concatenate([summed[rows(quarter[h] + i * 256, 64), :] for i in range(4)], axis=0)
        pr = dot(own, proj[...]).astype(bf16)
        for j in range(4):
            sall[h, j] = scale * dot_nt(pr, ia[h, j])

    line_scores(0)

    def wait_stat(d, _):
        got(stats.at[lax.rem(c + CLS - d, CLS)], st_s.at[d], st_r.at[d])
        return 0

    lax.fori_loop(1, CLS, wait_stat, 0)
    all_m = stats[:, 0:4, :]
    gtop = jnp.max(all_m, axis=0)
    gtot = jnp.sum(stats[:, 4:8, :] * jnp.exp(all_m - gtop[None]), axis=0)
    fac = jnp.exp(stat[0:4, :] - gtop) / gtot
    for q in range(4):
        frow[:, q * 128 : q * 128 + 128] = fac[q : q + 1, :]
    fr = frow[...]
    ls_here = jnp.sum(gtop + jnp.log(gtot), keepdims=True)
    gst[0:4, :] = gtop
    gst[4:8, :] = 1.0 / gtot
    for h in both:
        gs[h, pos[h]] = gst[...]
        for d in range(1, 4):
            go(gst, gs.at[h, pos[h]], gs_s.at[h * 4 + d], gs_r.at[h * 4 + d], near[h](d))
    us[...] = (acc[:, 0:B] * fr - acc[:, B : 2 * B]).astype(bf16)
    other = rows((1 - k) * 256, 256)
    mine = rows(k * 256, 256)
    uc = go(us.at[other, :], ucr, uc_s.at[0], uc_r.at[0], mate)


    got(ucr, uc_s.at[0], uc_r.at[0])
    uh[...] = (us[mine, :].astype(f32) + ucr[...].astype(f32)).astype(bf16)
    for d in range(1, NZ):
        go(uh.at[rows(q8(z + d) * 32, 32), :], uzr.at[z], uz_s.at[d], uz_r.at[d], at_z(d))
    uzr[z] = uh[rows(z * 32, 32), :]

    line_scores(1)
    for h in both:
        for d in range(1, 4):
            got(gl.at[h, q4(pos[h] + 4 - d)], gl_s.at[h * 4 + d], gl_r.at[h * 4 + d])
            got(gs.at[h, q4(pos[h] + 4 - d)], gs_s.at[h * 4 + d], gs_r.at[h * 4 + d])

    def flat(t, r0):
        return jnp.concatenate([t[r0 + q : r0 + q + 1, :] for q in range(4)], axis=1)

    def stage(h):
        axis = 1 - h
        p = pos[axis]

        def first():
            for d in (2, 1, 3):
                go(g2.at[h, rows(q4(p + d) * 64, 64), :], rb2.at[h, d], rs_s.at[h * 4 + d], rs_r.at[h * 4 + d], near[axis](d))

        def last():
            total = g2[h, rows(p * 64, 64), :].astype(f32)
            for d in (1, 3, 2):
                got(rb2.at[h, d], rs_s.at[h * 4 + d], rs_r.at[h * 4 + d])
                total = total + rb2[h, d].astype(f32)
            return total.astype(bf16)

        return first, last

    s2 = (stage(0), stage(1))
    for h in both:
        ri = lax.broadcasted_iota(i32, (256, 1), 0)
        tid = ri + (ri >> 6) * 192 + (tbase + quarter[h])
        for j in range(4):
            t = gs[h, j]
            hit = jnp.where(tid == flat(gl[h, j], 0), 1.0, 0.0)
            w = jnp.exp(sall[h, j] - flat(t, 0)) * flat(t, 4) - hit
            part = dot(w.astype(bf16), ia[h, j])
            cga[...] = part if j == 0 else cga[...] + part
        g2[h] = dot_nt((scale * cga[...]).astype(bf16), proj[...]).astype(bf16)
        s2[h][0]()
    fsum = jnp.zeros((128, E), f32)
    for h in both:
        for i in range(4):
            fsum = fsum + dot_tn(remt[rows(quarter[h] + i * 256, 64), :], g2[h, i * 64 : i * 64 + 64, :])
    far[...] = fsum[0:8].astype(bf16)

    def send_far(d):
        @pl.when(c >= d)
        def _():
            rc(far, fars.at[up8(c), :], far_s.at[d], far_r.at[d], at_c(CLS - d)).start()

    peers(send_far)

    def gather(h, s, blk):
        axis = (h + s) % 2
        p = pos[axis]
        right, left = near[axis](1), near[axis](3)
        if s == 0:
            step, off, sem = 64, 1024 * h + q4(pos[1 - h] + blk) * 256, (h * 5 + blk) * 6
        else:
            step, off, sem = 256, 1024 * h + pos[h] * 64, (h * 5 + 4) * 6

        def part(q, half):
            return gt.at[rows(off + q * step + half * 32, 32), :]

        def send(q, half, i, dev):
            ref = part(q, half)
            go(ref, ref, ag_s.at[sem + i], ag_r.at[sem + i], dev)

        def get(q, half, i):
            got(part(q, half), ag_s.at[sem + i], ag_r.at[sem + i])

        return ring(p, right, left, send, get)

    ag2 = [gather(h, 1, 0) for h in range(2)]
    ag1 = [[gather(h, 0, b) for b in range(4)] for h in range(2)]
    for h in range(2):
        start = 1024 * h + pos[h] * 64 + pos[1 - h] * 256
        gt[rows(start, 64), :] = s2[h][1]()
        ag2[h][0]()
        ag1[h][0][0]()
    for d in range(1, NZ):
        got(uzr.at[q8(z + NZ - d)], uz_s.at[d], uz_r.at[d])
    uslice = uzr[0].astype(f32)
    for d in range(1, NZ):
        uslice = uslice + uzr[d].astype(f32)
    uslice = uslice.astype(bf16)
    slot = rows((k * 8 + z) * 32, 32)
    ug[slot, :] = uslice
    for d in range(1, NZ):
        go(ug.at[slot, :], ug.at[slot, :], ug_s.at[d], ug_r.at[d], at_z(d))
    ppb[...] = (scale * dot(uslice, img[...])).astype(bf16)
    for d in range(1, 4):
        go(ppb, ppx.at[d], px_s.at[d], px_r.at[d], at_x(d))

    def wait_lab(d, _):
        got(labs.at[lax.rem(c + CLS - d, CLS)], lab_s.at[d], lab_r.at[d])
        return 0

    lax.fori_loop(1, CLS, wait_lab, 0)
    lt[...] = ls_here - jnp.sum(labs[...], axis=0)
    for d in range(1, 4):
        go(lt, ltx.at[d], lx_s.at[d], lx_r.at[d], at_x(d))


    def wait_far(d, _):
        @pl.when(c + d < CLS)
        def _():
            got(idss.at[up8(c + d), :], ids_s.at[d], ids_r.at[d])
            got(fars.at[up8(c + d), :], far_s.at[d], far_r.at[d])
        return 0

    lax.fori_loop(1, CLS, wait_far, 0)
    ri = lax.broadcasted_iota(i32, (128, 128), 0)
    ci = lax.broadcasted_iota(i32, (128, 128), 1)
    idrow = jnp.max(jnp.where(ri == ci, idss[...], -1), axis=0, keepdims=True)
    match = (last == idrow) & (last >= 0)
    fx[...] = dot(jnp.where(match, 1.0, 0.0).astype(bf16), fars[...])[0:8]
    for d in range(1, 4):
        go(fx, fxr.at[d], fx_s.at[d], fx_r.at[d], at_x(d))

    for h in range(2):
        ag2[h][1]()
    for h in range(2):
        ag1[h][0][1]()

    for d in range(1, 4):
        got(ppx.at[d], px_s.at[d], px_r.at[d])
        got(ltx.at[d], lx_s.at[d], lx_r.at[d])
    ppxs[...] = (
        ppb[...].astype(f32) + ppx[1].astype(f32) + ppx[2].astype(f32) + ppx[3].astype(f32)
    ).astype(bf16)
    ltxs[...] = lt[...] + ltx[1] + ltx[2] + ltx[3]
    for d in range(1, 4):
        go(ppxs, ppy.at[d], py_s.at[d], py_r.at[d], at_y(d))
        go(ltxs, lty.at[d], ly_s.at[d], ly_r.at[d], at_y(d))
    for d in range(1, 4):
        got(fxr.at[d], fx_s.at[d], fx_r.at[d])
    fy[...] = fx[...] + fxr[1] + fxr[2] + fxr[3]
    for d in range(1, 4):
        go(fy, fyr.at[d], fy_s.at[d], fy_r.at[d], at_y(d))

    for h in range(2):
        ag2[h][2]()
        ag1[h][3][0]()
        ag1[h][1][0]()
    for h in range(2):
        ag2[h][3]()
        ag1[h][2][0]()

    for d in range(1, 4):
        got(ppy.at[d], py_s.at[d], py_r.at[d])
        got(lty.at[d], ly_s.at[d], ly_r.at[d])
    pa[slot, :] = (
        ppxs[...].astype(f32) + ppy[1].astype(f32) + ppy[2].astype(f32) + ppy[3].astype(f32)
    ).astype(bf16)
    for d in range(1, NZ):
        go(pa.at[slot, :], pa.at[slot, :], pz_s.at[d], pz_r.at[d], at_z(d))
    total = ltxs[...] + lty[1] + lty[2] + lty[3]
    lossb[...] = total * (1.0 / BATCH)

    for b in (3, 1):
        for h in range(2):
            ag1[h][b][1]()
    for h in range(2):
        ag1[h][2][1]()

    for d in range(1, NZ):
        got(ug.at[rows((k * 8 + q8(z + NZ - d)) * 32, 32), :], ug_s.at[d], ug_r.at[d])
    go(ug.at[mine, :], ug.at[mine, :], uc_s.at[1], uc_r.at[1], mate)

    def add_rows(b):
        for h in both:
            ag1[h][b][2]()
            ag1[h][b][3]()

    add_rows(0)
    got(ug.at[other, :], uc_s.at[1], uc_r.at[1])
    gib[...] = (scale * dot_tn(ug[...], proj[...])).astype(bf16)

    for d in range(1, NZ):
        got(pa.at[rows((k * 8 + q8(z + NZ - d)) * 32, 32), :], pz_s.at[d], pz_r.at[d])
    go(pa.at[mine, :], pa.at[mine, :], uc_s.at[2], uc_r.at[2], mate)

    add_rows(3)
    add_rows(1)
    for d in range(1, 4):
        got(fyr.at[d], fy_s.at[d], fy_r.at[d])
    own = fy[...] + fyr[1] + fyr[2] + fyr[3]
    own = jnp.concatenate([own, jnp.zeros_like(own)], axis=0)
    hi = own.astype(bf16)
    lo = (own - hi.astype(f32)).astype(bf16)
    gnb[...] = dot_tn(sels[...], hi) + dot_tn(sels[...], lo)
    add_rows(2)
    got(pa.at[other, :], uc_s.at[2], uc_r.at[2])
    gpb[...] = pa[...].astype(f32)

    for cp in started:
        cp.wait_send()

    def drain(d, _):
        rc(stat, stat, st_s.at[d], st_r.at[d], mate).wait_send()
        rc(labt, labt, lab_s.at[d], lab_r.at[d], mate).wait_send()

        @pl.when(c + d < CLS)
        def _():
            rc(pub, pub, pub_s.at[d], pub_r.at[d], mate).wait_send()

        @pl.when(c >= d)
        def _():
            rc(ids, ids, ids_s.at[d], ids_r.at[d], mate).wait_send()
            rc(far, far, far_s.at[d], far_r.at[d], mate).wait_send()

        return 0

    lax.fori_loop(1, CLS, drain, 0)


def finish(lossb, gi, gt, gn, gp, cnt, loss_o, gi_o, gt_o, gn_o, gp_o, gnb, sem):
    outs = [
        pltpu.make_async_copy(a, b, sem.at[i])
        for i, (a, b) in enumerate(((gt, gt_o), (gp, gp_o), (gi, gi_o)))
    ]
    for cp in outs:
        cp.start()
    loss_o[...] = lossb[0:1, 0:1]
    for i in range(2):
        r = slice(i * 256, i * 256 + 256)
        gnb[r, :] = gn[r, :] + dot(cnt[r, :], gt[...])
        outs.append(pltpu.make_async_copy(gnb.at[r, :], gn_o.at[r, :], sem.at[3 + i]))
        outs[-1].start()
    for cp in outs:
        cp.wait()


def q8(v):
    return lax.rem(v, NZ)


def per_device(images, labels, taxon_emb, node_emb, proj, lineage):
    dma = pltpu.SemaphoreType.DMA
    vm = pltpu.VMEM
    scratch = [
        vm((LEVELS, T), i32), vm((1, B), i32),
        vm((2, 4, B, E), bf16), vm((T, E), bf16), vm((N, E), bf16), vm((E, E), bf16),
        vm((16, T), i32), vm((T, E), f32), vm((T, E), bf16),
        vm((T, B), f32), vm((T, 2 * B), bf16), vm((E, 2 * B), f32), vm((T, 128), bf16),
        vm((2, 4, 256, B), f32), vm((256, E), f32),
        vm((8, 128), i32), vm((2, 4, 8, 128), i32), vm((8, 128), f32), vm((2, 4, 8, 128), f32),
        vm((8, E), bf16), vm((CLS * 8, E), bf16), vm((8, 128), i32), vm((CLS * 8, 128), i32),
        vm((8, 128), f32), vm((CLS, 8, 128), f32), vm((8, 128), f32), vm((CLS, 8, 128), f32),
        vm((8, E), bf16), vm((CLS * 8, E), bf16), vm((1, B), f32),
        vm((E, B), bf16), vm((256, B), bf16), vm((256, B), bf16), vm((NZ, 32, B), bf16),
        vm((32, E), bf16), vm((4, 32, E), bf16), vm((32, E), bf16),
        vm((4, 32, E), bf16), vm((8, 128), f32), vm((4, 8, 128), f32),
        vm((8, 128), f32), vm((4, 8, 128), f32),
        vm((8, E), f32), vm((4, 8, E), f32), vm((8, E), f32), vm((4, 8, E), f32),
        vm((2, 256, E), bf16), vm((2, 4, 64, E), bf16),
        dma((7,)), vm((E, B), bf16), vm((E, E), bf16), vm((16, N), bf16),
    ]
    scratch += [dma((CLS,))] * 10
    scratch += [dma((12,))] * 2 + [dma((8,))] * 4 + [dma((12,))] * 2 + [dma((60,))] * 2
    scratch += [dma((3,))] * 2 + [dma((NZ,))] * 4
    scratch += [dma((4,))] * 4 + [dma((NZ,))] * 2 + [dma((4,))] * 4
    scratch += [dma((4,))] * 4
    hbm = pl.BlockSpec(memory_space=pltpu.HBM)
    vmem = pl.BlockSpec(memory_space=pltpu.VMEM)
    args = (lineage.T, labels.reshape(1, B), images, taxon_emb, node_emb, proj)
    held = pl.pallas_call(
        body,
        out_shape=(
            vm((8, 128), f32), vm((B, E), bf16), vm((T, E), bf16), vm((N, E), f32), vm((E, E), f32),
            vm((N, T), bf16),
        ),
        in_specs=[hbm] * 6,
        out_specs=[vmem] * 6,
        scratch_shapes=scratch,
        compiler_params=pltpu.CompilerParams(
            collective_id=0, has_side_effects=True, vmem_limit_bytes=52 * 1024 * 1024
        ),
    )(*[pltpu.with_memory_space_constraint(a, pltpu.HBM) for a in args])
    loss, gi, gt, gn, gp = pl.pallas_call(
        finish,
        out_shape=(
            jax.ShapeDtypeStruct((1, 1), f32),
            jax.ShapeDtypeStruct((B, E), bf16),
            jax.ShapeDtypeStruct((T, E), bf16),
            jax.ShapeDtypeStruct((N, E), f32),
            jax.ShapeDtypeStruct((E, E), f32),
        ),
        in_specs=[vmem] * 6,
        out_specs=[vmem] + [hbm] * 4,
        scratch_shapes=[vm((N, E), f32), dma((5,))],
        compiler_params=pltpu.CompilerParams(vmem_limit_bytes=8 * 1024 * 1024),
    )(*held)
    return (loss.reshape(()), gi, gt, gn, gp)


def solution(mesh):
    in_specs = (P("grp", None), P("grp"), P("cls", None), P("cls", None), P(), P("cls", None))
    out_specs = (P(), P("grp", None), P("cls", None), P("cls", None), P())
    return jax.shard_map(
        per_device, mesh=mesh, in_specs=in_specs, out_specs=out_specs, check_vma=False
    )
```
